128 devices in a mesh: tgt: 16 (over y, x), src: 8 (over z, core).
Axes of the slice: x: 4, y: 4, z: 4, core: 2. Of those that a mesh axis runs over, the one named last changes fastest.
Arguments:
- charges: bfloat16 [8, 131072], P(None, 'src'), may hold values from -6 to 6
- weights: float32 [131072], P('tgt'), may hold values from 0.4 to 7.5
- cell_order: int32 [128, 1024], P(('tgt', 'src')), may hold values from 0 to 1023, as said below
- leaf_coords: int32 [3, 128], replicated, may hold values from 0 to 7, as said below
- near_src: int32 [128, 27], P('tgt'), may hold values from -1 to 127, as said below
Outputs:
- potential: bfloat16 [8, 131072], P(None, ('tgt', 'src'))
- root_factor: float32 [64, 64], replicated
The draws below stay inside these ranges and needn't reach their ends.
Inputs may be any that keep to these rules, and one draw needn't show every extreme that they name: `cell_order`: each row is a permutation of 0 to 1023. `leaf_coords`: distinct positions on a grid of 8 x 4 x 4 leaf boxes. `near_src`: row l lists in increasing order every leaf whose coordinates differ from leaf l's by at most one in each dimension, l itself included, then -1.
All inputs are finite; a program needn't handle non-finite values.
Results may differ from the reference program's by a relative error of at most 0.0013.
The reference program's roundings to bfloat16 on the way count: a program that leaves them out, or rounds other values in their place, can miss the bound.
Values may be sent and summed in bfloat16 or wider, within the bound.
A program may use at most 64 MiB of HBM per device.

```python
import math
import jax
import jax.numpy as jnp
from jax import lax

EDGE = 8
LEAF = 1024
NB = 27
SCEN = 8
LV = 128
CELLS = 131072


def leaf_layout(key):
    shuffle = jax.random.permutation(jax.random.fold_in(key, 7), LV).astype(jnp.int32)
    coords = jnp.stack([shuffle // 16, shuffle // 4 % 4, shuffle % 4]).astype(jnp.int32)
    between = jnp.abs(coords[:, :, None] - coords[:, None, :])
    adjacent = jnp.all(between <= 1, axis=0)
    leaf_ids = jnp.arange(LV, dtype=jnp.int32)
    scores = jnp.where(adjacent, 2 * LV - leaf_ids[None, :], LV - leaf_ids[None, :])
    values, picks = lax.top_k(scores, NB)
    near = jnp.where(values > LV, picks, -1).astype(jnp.int32)
    return (coords, near)


def order_rows(key):
    row_keys = jax.random.split(jax.random.fold_in(key, 3), LV)
    rows = jax.vmap(lambda row_key: jax.random.permutation(row_key, LEAF))(row_keys)
    return rows.astype(jnp.int32)


def draw_leaf_coords(key, part):
    coords, near = leaf_layout(key)
    return coords


def draw_near_src(key, part):
    coords, near = leaf_layout(key)
    return near


def draw_cell_order(key, part):
    return order_rows(key)


def draw_charges(key, part):
    coords, near = leaf_layout(key)
    rows = order_rows(key)
    plane = 2 * EDGE * EDGE
    global_x = coords[0][:, None] * EDGE + rows // plane
    global_y = coords[1][:, None] * EDGE + rows // (2 * EDGE) % EDGE
    global_z = coords[2][:, None] * (2 * EDGE) + rows % (2 * EDGE)
    parity = (global_x + global_y + global_z) % 2
    checker = (1 - 2 * parity).astype(jnp.float32).reshape(CELLS)
    magnitude = jax.random.uniform(jax.random.fold_in(key, 19), (SCEN, CELLS), jnp.float32, 0.5, 1.5)
    return (magnitude * checker[None, :]).astype(jnp.bfloat16)


def draw_weights(key, part):
    cell_leaf = (jnp.arange(CELLS, dtype=jnp.int32) // LEAF).astype(jnp.float32)
    trend = jnp.exp(math.log(3.0) * cell_leaf / LV)
    base = jnp.exp(jax.random.uniform(jax.random.fold_in(key, 11), (CELLS,), jnp.float32, math.log(0.5), math.log(2.0)))
    return (base * trend).astype(jnp.float32)


def setup_inputs(seed: int = 0) -> dict:
    seeds = jax.random.split(jax.random.key(seed), 6)
    charges = draw_charges(jax.random.fold_in(seeds[5], 71), 0)
    weights = draw_weights(jax.random.fold_in(seeds[5], 71), 0)
    cell_order = draw_cell_order(jax.random.fold_in(seeds[5], 71), 0)
    leaf_coords = draw_leaf_coords(jax.random.fold_in(seeds[5], 71), 0)
    near_src = draw_near_src(jax.random.fold_in(seeds[5], 71), 0)
    return {"charges": charges, "weights": weights, "cell_order": cell_order, "leaf_coords": leaf_coords, "near_src": near_src}


def chebyshev_nodes(extent):
    number = jnp.arange(4, dtype=jnp.float32)
    return extent * 0.5 + extent * 0.5 * jnp.cos((2.0 * number + 1.0) * (math.pi / 8.0))

def lagrange(points, node_list):
    columns = []
    for node_a in range(4):
        factor = jnp.ones_like(points)
        for node_b in range(4):
            if node_b != node_a:
                factor = factor * (points - node_list[node_b]) / (node_list[node_a] - node_list[node_b])
        columns.append(factor)
    return jnp.stack(columns, axis=1)

def in_leaf(order_row, edge_cells):
    plane = 2 * edge_cells * edge_cells
    along_x = order_row // plane
    along_y = order_row // (2 * edge_cells) % edge_cells
    along_z = order_row % (2 * edge_cells)
    return jnp.stack([along_x, along_y, along_z]).astype(jnp.float32) + 0.5

def leaf_basis(edge_cells):
    cell_ids = jnp.arange(2 * edge_cells ** 3, dtype=jnp.int32)
    placed = in_leaf(cell_ids, edge_cells)
    along_x = lagrange(placed[0], chebyshev_nodes(1.0 * edge_cells))
    along_y = lagrange(placed[1], chebyshev_nodes(1.0 * edge_cells))
    along_z = lagrange(placed[2], chebyshev_nodes(2.0 * edge_cells))
    joined = along_x[:, :, None, None] * along_y[:, None, :, None] * along_z[:, None, None, :]
    return joined.reshape(cell_ids.shape[0], 64)

def node_offsets(edge_cells):
    node_x = chebyshev_nodes(1.0 * edge_cells)
    node_z = chebyshev_nodes(2.0 * edge_cells)
    first = jnp.broadcast_to(node_x[:, None, None], (4, 4, 4)).reshape(64)
    second = jnp.broadcast_to(node_x[None, :, None], (4, 4, 4)).reshape(64)
    third = jnp.broadcast_to(node_z[None, None, :], (4, 4, 4)).reshape(64)
    return jnp.stack([first, second, third], axis=1)

def cell_positions(order_row, leaf_coord, spacing, edge_cells):
    return leaf_coord[:, None] * spacing[:, None] + in_leaf(order_row, edge_cells)

def kernel(tgt_points, src_points):
    between = tgt_points[:, :, None] - src_points[:, None, :]
    distance = lax.optimization_barrier(jnp.sum(between * between, axis=0))
    return 0.05 / jnp.sqrt(distance + 1.0)

def reference(charges, weights, cell_order, leaf_coords, near_src):
    leaves = cell_order.shape[0]
    leaf_size = cell_order.shape[1]
    highest = lax.Precision.HIGHEST
    spacing = jnp.array([EDGE, EDGE, 2 * EDGE], dtype=jnp.float32)
    coords_f = leaf_coords.astype(jnp.float32)

    def near_one(target):
        near_row = near_src[target]
        live_count = jnp.sum((near_row >= 0).astype(jnp.int32))
        tgt_points = cell_positions(cell_order[target], coords_f[:, target], spacing, EDGE)

        def near_step(number, summed):
            source = near_row[number]
            src_points = cell_positions(cell_order[source], coords_f[:, source], spacing, EDGE)
            kernel_block = kernel(tgt_points, src_points).astype(jnp.bfloat16)
            source_charges = lax.dynamic_slice_in_dim(charges, (source * leaf_size).astype(jnp.int32), leaf_size, 1)
            return summed + lax.dot_general(source_charges.astype(jnp.float32), kernel_block.astype(jnp.float32), (((1,), (1,)), ((), ())), preferred_element_type=jnp.float32)
        return lax.fori_loop(0, live_count, near_step, jnp.zeros((SCEN, leaf_size), jnp.float32))
    leaf_ids = jnp.arange(leaves, dtype=jnp.int32)
    near_part = lax.map(near_one, leaf_ids)
    lagrange_basis = leaf_basis(EDGE)
    bases = lagrange_basis[cell_order]
    charges_f = charges.astype(jnp.float32).reshape(SCEN, leaves, leaf_size)
    moments = jnp.einsum('lje,slj->les', bases, charges_f, precision=highest)
    leaf_nodes = coords_f.T[:, None, :] * spacing[None, None, :] + node_offsets(EDGE)[None]

    def far_one(target):
        near_mask = jnp.any(near_src[target][:, None] == leaf_ids[None, :], axis=0)
        between = leaf_nodes[target][:, None, None, :] - leaf_nodes[None, :, :, :]
        distance = lax.optimization_barrier(jnp.sum(between * between, axis=3))
        keep = 1.0 - near_mask.astype(jnp.float32)
        coupling = 0.05 / jnp.sqrt(distance + 1.0) * keep[None, :, None]
        return jnp.einsum('ebf,bfs->es', coupling, moments, precision=highest)
    local_sums = lax.map(far_one, leaf_ids)
    far_part = jnp.einsum('lje,les->slj', bases, local_sums, precision=highest)
    total = jnp.transpose(near_part, (1, 0, 2)) + far_part
    leaf_weights = weights.reshape(leaves, leaf_size)
    potential = (leaf_weights[None] * total).reshape(SCEN, leaves * leaf_size).astype(jnp.bfloat16)
    weighted = leaf_weights[:, :, None] * bases
    gram_matrix = jnp.einsum('lje,ljf->ef', weighted, weighted, precision=highest)
    root_factor = jnp.linalg.cholesky(gram_matrix).T / jnp.sqrt(jnp.float32(leaves * leaf_size))
    return (potential, root_factor)
```

```python
import math

import jax
import jax.numpy as jnp
import ml_dtypes
import numpy as np
from jax import lax
from jax.experimental import pallas as pl
from jax.experimental.pallas import tpu as pltpu
from jax.sharding import PartitionSpec as P

EDGE = 8
LEAF = 1024
SCEN = 8
LV = 128
NT = 16
NS = 8
TL = LV // NT
SL = LV // NS
NODES = 64
CELLS = LV * LEAF
MESH = pl.DeviceIdType.MESH
F32 = jnp.float32
BF16 = jnp.bfloat16
NT_DIMS = (((1,), (1,)), ((), ()))


def chebyshev_nodes(extent):
    number = np.arange(4, dtype=np.float64)
    return extent * 0.5 + extent * 0.5 * np.cos((2.0 * number + 1.0) * (math.pi / 8.0))


def lagrange(points, nodes):
    columns = []
    for a in range(4):
        factor = np.ones_like(points)
        for b in range(4):
            if b != a:
                factor = factor * (points - nodes[b]) / (nodes[a] - nodes[b])
        columns.append(factor)
    return np.stack(columns, axis=1)


def basis_table():
    p = np.arange(LEAF)
    along_x = lagrange(p // 128 + 0.5, chebyshev_nodes(8.0))
    along_y = lagrange(p // 16 % 8 + 0.5, chebyshev_nodes(8.0))
    along_z = lagrange(p % 16 + 0.5, chebyshev_nodes(16.0))
    joined = along_x[:, :, None, None] * along_y[:, None, :, None] * along_z[:, None, None, :]
    return joined.reshape(LEAF, NODES).astype(np.float32)


def split_two(table):
    high = table.astype(ml_dtypes.bfloat16)
    low = (table - high.astype(np.float32)).astype(ml_dtypes.bfloat16)
    return high, low


def node_offsets():
    node_x = chebyshev_nodes(8.0)
    node_z = chebyshev_nodes(16.0)
    grid = np.meshgrid(node_x, node_x, node_z, indexing="ij")
    return np.stack([g.reshape(NODES) for g in grid]).astype(np.float32)


def near_table():
    cell = np.arange(128)
    y, z = cell // 16, cell % 16
    delta = np.arange(16)
    blocks = []
    for oy in (-1, 0, 1):
        for oz in (-1, 0, 1):
            dy = y[None, :] - (y[:, None] + 8 * oy)
            dz = z[None, :] - (z[:, None] + 16 * oz)
            square = (dy * dy + dz * dz)[:, None, :] + (delta * delta)[None, :, None]
            value = np.float32(0.05) / np.sqrt(square.astype(np.float32) + np.float32(1.0))
            blocks.append(value.reshape(128, 2048))
    return np.stack(blocks).astype(ml_dtypes.bfloat16)


def exchange_kernel(
    order_ref, w_ref, inv_ref, sq_ref, mine, buf, send_a, recv_a, send_b, recv_b
):
    a = lax.axis_index("tgt")
    b = lax.axis_index("src")
    barrier = pltpu.get_barrier_semaphore()
    home = lax.rem(a, 2) * NS + b
    column = lax.div(a, 2)
    loops_back = b == column

    def signal_sender(k, carry):
        pl.semaphore_signal(
            barrier, 1, device_id=(2 * b + lax.div(k, NS), lax.rem(k, NS)), device_id_type=MESH
        )
        return carry

    def signal_peer(k, carry):
        pl.semaphore_signal(barrier, 1, device_id=(lax.rem(a + k, NT), b), device_id_type=MESH)
        return carry

    own_sender = lax.rem(a, 2) * NS + b
    sends_to_me = lax.div(a, 2) == b

    def signal_other(k, carry):
        at = lax.rem(own_sender + k, NT)
        return signal_sender(at, carry)

    @pl.when(jnp.logical_not(sends_to_me))
    def _():
        signal_other(0, 0)

    lax.fori_loop(1, NT, signal_other, 0)
    lax.fori_loop(1, NT, signal_peer, 0)

    rows = lax.broadcasted_iota(jnp.int32, (8, 128), 0)
    lanes = lax.broadcasted_iota(jnp.int32, (8, 128), 1)
    low_rows = lax.broadcasted_iota(jnp.int32, (128, 128), 0)
    weights = w_ref[pl.ds(pl.multiple_of(b * 8, 8), 8), :]
    square = weights * weights
    placed = jnp.zeros((40, 128), F32)
    for c in range(8):
        order = order_ref[0:1, c * 128 : (c + 1) * 128]
        hit = lax.shift_right_logical(jnp.broadcast_to(order, (8, 128)), 7) == rows
        value = jnp.broadcast_to(square[c : c + 1, :], (8, 128))
        first = value.astype(BF16).astype(F32)
        rest = value - first
        second = rest.astype(BF16).astype(F32)
        third = rest - second
        parts = [jnp.full((8, 128), float(c), F32), lanes.astype(F32), first, second, third]
        left = jnp.concatenate([jnp.where(hit, part, 0.0) for part in parts], axis=0)
        low = jnp.broadcast_to(jnp.bitwise_and(order, 127), (128, 128)) == low_rows
        right = jnp.where(low, 1.0, 0.0).astype(BF16)
        placed = placed + lax.dot_general(
            left.astype(BF16), right, NT_DIMS, preferred_element_type=F32
        )
    inverse = (placed[0:8] * 128.0 + placed[8:16]).astype(jnp.int32)
    mine[...] = inverse
    buf[a] = placed[16:24] + placed[24:32] + placed[32:40]

    pl.semaphore_wait(
        barrier, jnp.where(loops_back, 2 * NT - 2, 2 * NT - 1).astype(jnp.int32)
    )

    def order_copy(k):
        at = lax.rem(a + k, NT)
        return pltpu.make_async_remote_copy(
            src_ref=mine,
            dst_ref=inv_ref.at[home],
            send_sem=send_a.at[k],
            recv_sem=recv_a.at[home],
            device_id=(at, column),
            device_id_type=MESH,
        )

    def square_copy(k):
        return pltpu.make_async_remote_copy(
            src_ref=buf.at[a],
            dst_ref=buf.at[a],
            send_sem=send_b.at[k],
            recv_sem=recv_b.at[a],
            device_id=(lax.rem(a + k, NT), b),
            device_id_type=MESH,
        )

    @pl.when(jnp.logical_not(loops_back))
    def _():
        order_copy(0).start()

    @pl.when(loops_back)
    def _():
        inv_ref[home] = inverse

    def start_both(k, carry):
        order_copy(k).start()
        square_copy(k).start()
        return carry

    lax.fori_loop(1, NT, start_both, 0)

    def order_arrival(slot):
        pltpu.make_async_remote_copy(
            src_ref=mine,
            dst_ref=inv_ref.at[slot],
            send_sem=send_a.at[0],
            recv_sem=recv_a.at[slot],
            device_id=(a, b),
            device_id_type=MESH,
        ).wait_recv()

    def square_arrival(slot):
        pltpu.make_async_remote_copy(
            src_ref=mine,
            dst_ref=buf.at[slot],
            send_sem=send_b.at[0],
            recv_sem=recv_b.at[slot],
            device_id=(a, b),
            device_id_type=MESH,
        ).wait_recv()

    @pl.when(jnp.logical_not(loops_back))
    def _():
        order_arrival(home)
        order_copy(0).wait_send()

    def wait_both(k, carry):
        order_arrival(lax.rem(home + k, NT))
        square_arrival(lax.rem(a + k, NT))
        order_copy(k).wait_send()
        square_copy(k).wait_send()
        return carry

    lax.fori_loop(1, NT, wait_both, 0)
    total = buf[0]
    for k in range(1, NT):
        total = total + buf[k]
    sq_ref[...] = total


def exchange(order, weights):
    return pl.pallas_call(
        exchange_kernel,
        out_shape=(
            jax.ShapeDtypeStruct((SL, 8, 128), jnp.int32),
            jax.ShapeDtypeStruct((8, 128), F32),
        ),
        in_specs=[pl.BlockSpec(memory_space=pltpu.VMEM)] * 2,
        out_specs=(pl.BlockSpec(memory_space=pltpu.VMEM),) * 2,
        scratch_shapes=[
            pltpu.VMEM((8, 128), jnp.int32),
            pltpu.VMEM((NT, 8, 128), F32),
            pltpu.SemaphoreType.DMA((NT,)),
            pltpu.SemaphoreType.DMA((NT,)),
            pltpu.SemaphoreType.DMA((NT,)),
            pltpu.SemaphoreType.DMA((NT,)),
        ],
        compiler_params=pltpu.CompilerParams(collective_id=0, has_side_effects=True),
        name="exchange",
    )(order, weights)


def lane_gather(block, lane):
    return jnp.take_along_axis(block, lane, axis=1, mode="promise_in_bounds")


def permute_row(blocks, index):
    block = lax.shift_right_logical(index, 7)
    lane = jnp.bitwise_and(index, 127)
    out = lane_gather(blocks[0], lane)
    for k in range(1, 8):
        out = jnp.where(block == k, lane_gather(blocks[k], lane), out)
    return out


def local_kernel(
    coords, charges, inv, basis_m, basis_h, basis_l, node_sub, node_lane, table_hbm, out, table, qf, qb, pairs, sem
):
    i = lax.axis_index("tgt")
    j = lax.axis_index("src")
    fetch = pltpu.make_async_copy(table_hbm, table, sem)
    fetch.start()

    def canonical(leaf, carry):
        base = pl.multiple_of(leaf * LEAF, LEAF)
        raw = charges[:, pl.ds(base, LEAF)].astype(F32)
        blocks = [raw[:, k * 128 : (k + 1) * 128] for k in range(8)]
        order = inv[leaf]
        pieces = [
            permute_row(blocks, jnp.broadcast_to(order[x : x + 1, :], (8, 128))) for x in range(8)
        ]
        rows = jnp.concatenate(pieces, axis=0)
        qf[leaf] = rows
        qb[leaf] = rows.astype(BF16)
        return carry

    lax.fori_loop(0, SL, canonical, 0)

    both = jnp.zeros((SL * SCEN, 128), F32)
    for x in range(8):
        rows = qf[:, x * 8 : (x + 1) * 8, :].reshape(SL * SCEN, 128).astype(BF16)
        both = both + jnp.dot(
            rows, basis_m[x * 128 : (x + 1) * 128, :], preferred_element_type=F32
        )
    moments = both[:, :NODES] + both[:, NODES:]

    slot = lax.shift_right_logical(lax.broadcasted_iota(jnp.int32, (1, TL * NODES), 1), 6)
    tgt_box = []
    for d in range(3):
        row = jnp.zeros((1, TL * NODES), jnp.int32)
        for t in range(TL):
            row = jnp.where(slot == t, coords[d, i * TL + t], row)
        tgt_box.append(row)
    spacing = (8.0, 8.0, 16.0)
    tgt_node = [
        tgt_box[d].astype(F32) * spacing[d] + node_lane[d : d + 1, :] for d in range(3)
    ]
    coeff = jnp.zeros((SCEN, TL * NODES), F32)
    for s in range(SL):
        distance = jnp.full((NODES, TL * NODES), 1.0, F32)
        close = jnp.full((1, TL * NODES), True)
        for d in range(3):
            box = coords[d, j * SL + s]
            close = close & (jnp.abs(tgt_box[d] - box) <= 1)
            shifted = tgt_node[d] - box.astype(F32) * spacing[d]
            source = jnp.tile(node_sub[d], (1, TL * NODES // 128))
            between = shifted - source
            distance = distance + between * between
        keep = jnp.where(close, 0.0, 0.05)
        phi = keep / jnp.sqrt(distance)
        high = phi.astype(BF16)
        low = (phi - high.astype(F32)).astype(BF16)
        part = moments[s * 8 : (s + 1) * 8, :]
        part_high = part.astype(BF16)
        part_low = (part - part_high.astype(F32)).astype(BF16)
        twice = jnp.concatenate([part_high.astype(F32), part_low.astype(F32)], axis=0).astype(BF16)
        product = jnp.dot(twice, high, preferred_element_type=F32)
        coeff = coeff + product[:8] + product[8:]
        coeff = coeff + jnp.dot(part_high, low, preferred_element_type=F32)

    stacked = jnp.concatenate(
        [coeff[:, t * NODES : (t + 1) * NODES] for t in range(TL)], axis=0
    )
    stacked_high = stacked.astype(BF16)
    stacked_low = (stacked - stacked_high.astype(F32)).astype(BF16)
    far = jnp.dot(stacked_high, basis_h[...], preferred_element_type=F32)
    far = far + jnp.dot(stacked_low, basis_h[...], preferred_element_type=F32)
    far = far + jnp.dot(stacked_high, basis_l[...], preferred_element_type=F32)
    for t in range(TL):
        out[t] = far[t * 8 : (t + 1) * 8, :]

    def list_target(t, count):
        box = [coords[d, i * TL + t] for d in range(3)]
        for s in range(SL):
            step = [coords[d, j * SL + s] - box[d] for d in range(3)]
            close = jnp.maximum(jnp.maximum(jnp.abs(step[0]), jnp.abs(step[1])), jnp.abs(step[2])) <= 1
            pairs[count] = t + 8 * s + 128 * (step[0] + 1) + 512 * ((step[1] + 1) * 3 + step[2] + 1)
            count = count + close.astype(jnp.int32)
        return count

    count = lax.fori_loop(0, TL, list_target, 0)
    fetch.wait()

    def near_pair(n, carry):
        code = pairs[n]
        t = jnp.bitwise_and(code, 7)
        s = jnp.bitwise_and(lax.shift_right_logical(code, 3), 15)
        step = jnp.bitwise_and(lax.shift_right_logical(code, 7), 3)
        which = lax.shift_right_logical(code, 9)
        for value in (0, 1, 2):

            @pl.when(step == value)
            def _():
                left = qb[s]
                total = [out[t, :, x * 128 : (x + 1) * 128] for x in range(8)]
                for chunk in range(4 if value == 1 else 8):
                    product = jnp.dot(
                        left,
                        table[which, :, chunk * 256 : (chunk + 1) * 256],
                        preferred_element_type=F32,
                    )
                    for half in range(2):
                        delta = 2 * chunk + half
                        for sx in range(8):
                            if value == 1:
                                hits = {sx - delta, sx + delta}
                            elif value == 2:
                                hits = {8 + sx - delta}
                            else:
                                hits = {delta - 8 + sx}
                            for x in sorted(hits):
                                if 0 <= x < 8:
                                    total[x] = total[x] + product[
                                        sx * 8 : (sx + 1) * 8, half * 128 : (half + 1) * 128
                                    ]
                for x in range(8):
                    out[t, :, x * 128 : (x + 1) * 128] = total[x]

        return carry

    lax.fori_loop(0, count, near_pair, 0)


def local_part(leaf_coords, charges, inverse):
    table = basis_table()
    high, low = split_two(table)
    basis_m = np.concatenate([high, low], axis=1)
    offsets = node_offsets()
    node_sub = np.broadcast_to(offsets[:, :, None], (3, NODES, 128)).astype(np.float32)
    node_lane = np.tile(offsets, (1, TL))
    vmem = pl.BlockSpec(memory_space=pltpu.VMEM)
    return pl.pallas_call(
        local_kernel,
        out_shape=jax.ShapeDtypeStruct((TL, SCEN, LEAF), F32),
        in_specs=[pl.BlockSpec(memory_space=pltpu.SMEM)]
        + [vmem] * 7
        + [pl.BlockSpec(memory_space=pl.ANY)],
        out_specs=vmem,
        scratch_shapes=[
            pltpu.VMEM((9, 128, 2048), BF16),
            pltpu.VMEM((SL, 64, 128), F32),
            pltpu.VMEM((SL, 64, 128), BF16),
            pltpu.SMEM((136,), jnp.int32),
            pltpu.SemaphoreType.DMA,
        ],
        compiler_params=pltpu.CompilerParams(vmem_limit_bytes=40 << 20),
        name="local_part",
    )(
        leaf_coords,
        charges,
        inverse,
        jnp.asarray(basis_m),
        jnp.asarray(np.ascontiguousarray(high.T)),
        jnp.asarray(np.ascontiguousarray(low.T)),
        jnp.asarray(node_sub),
        jnp.asarray(node_lane),
        jnp.asarray(near_table()),
    )


def reduce_kernel(
    part_ref, sq_ref, order_ref, w_ref, basis_ref, pot_ref, root_ref, recv, buf, send_a, recv_a, send_b, recv_b
):
    a = lax.axis_index("tgt")
    b = lax.axis_index("src")
    barrier = pltpu.get_barrier_semaphore()

    def greet(k, carry):
        pl.semaphore_signal(barrier, 1, device_id=(a, lax.rem(b + k, NS)), device_id_type=MESH)
        return carry

    lax.fori_loop(1, NS, greet, 0)
    buf[b] = sq_ref[...]
    pl.semaphore_wait(barrier, NS - 1)

    def square_copy(k):
        return pltpu.make_async_remote_copy(
            src_ref=buf.at[b],
            dst_ref=buf.at[b],
            send_sem=send_b.at[k],
            recv_sem=recv_b.at[b],
            device_id=(a, lax.rem(b + k, NS)),
            device_id_type=MESH,
        )

    def part_copy(k):
        at = lax.rem(b + k, NS)
        return pltpu.make_async_remote_copy(
            src_ref=part_ref.at[at],
            dst_ref=recv.at[b],
            send_sem=send_a.at[k],
            recv_sem=recv_a.at[b],
            device_id=(a, at),
            device_id_type=MESH,
        )

    def start(copy):
        def step(k, carry):
            copy(k).start()
            return carry

        lax.fori_loop(1, NS, step, 0)

    start(square_copy)
    start(part_copy)
    recv[b] = part_ref[b]

    def square_wait(k, carry):
        slot = lax.rem(b + k, NS)
        pltpu.make_async_remote_copy(
            src_ref=buf.at[b],
            dst_ref=buf.at[slot],
            send_sem=send_b.at[0],
            recv_sem=recv_b.at[slot],
            device_id=(a, b),
            device_id_type=MESH,
        ).wait_recv()
        square_copy(k).wait_send()
        return carry

    lax.fori_loop(1, NS, square_wait, 0)
    square = buf[0]
    for k in range(1, NS):
        square = square + buf[k]
    basis = basis_ref[...]
    scaled = jnp.concatenate(
        [basis[:, k * 128 : (k + 1) * 128] * square[k : k + 1, :] for k in range(8)], axis=1
    )
    gram = lax.dot_general(
        scaled, basis, NT_DIMS, precision=lax.Precision.HIGHEST, preferred_element_type=F32
    )
    lane = lax.broadcasted_iota(jnp.int32, (1, NODES), 1)
    left = [gram[8 * k : 8 * k + 8, :] for k in range(8)]
    scale = np.float32(1.0 / math.sqrt(CELLS))
    for k in range(NODES):
        block, row_at = k // 8, k % 8
        row = left[block][row_at : row_at + 1, :]
        pivot = row[:, k : k + 1]
        root = 1.0 / jnp.sqrt(pivot)
        unit = row * root
        root_ref[k : k + 1, :] = jnp.where(lane >= k, unit * scale, 0.0)
        for m in range(block, 8):
            left[m] = left[m] - (left[m][:, k : k + 1] * root) * unit

    def part_wait(k, carry):
        slot = lax.rem(b + k, NS)
        pltpu.make_async_remote_copy(
            src_ref=part_ref.at[0],
            dst_ref=recv.at[slot],
            send_sem=send_a.at[0],
            recv_sem=recv_a.at[slot],
            device_id=(a, b),
            device_id_type=MESH,
        ).wait_recv()
        part_copy(k).wait_send()
        return carry

    lax.fori_loop(1, NS, part_wait, 0)
    total = recv[0]
    for k in range(1, NS):
        total = total + recv[k]
    blocks = [total[:, k * 128 : (k + 1) * 128] for k in range(8)]
    weights = w_ref[pl.ds(pl.multiple_of(b * 8, 8), 8), :]
    for c in range(8):
        index = jnp.broadcast_to(order_ref[0:1, c * 128 : (c + 1) * 128], (8, 128))
        value = permute_row(blocks, index) * weights[c : c + 1, :]
        pot_ref[:, c * 128 : (c + 1) * 128] = value.astype(BF16)


def reduce_part(part, square, order, weights):
    vmem = pl.BlockSpec(memory_space=pltpu.VMEM)
    basis = jnp.asarray(np.ascontiguousarray(basis_table().T))
    return pl.pallas_call(
        reduce_kernel,
        out_shape=(
            jax.ShapeDtypeStruct((SCEN, LEAF), BF16),
            jax.ShapeDtypeStruct((NODES, NODES), F32),
        ),
        in_specs=[vmem] * 5,
        out_specs=(vmem, vmem),
        scratch_shapes=[
            pltpu.VMEM((NS, SCEN, LEAF), F32),
            pltpu.VMEM((NS, 8, 128), F32),
            pltpu.SemaphoreType.DMA((NS,)),
            pltpu.SemaphoreType.DMA((NS,)),
            pltpu.SemaphoreType.DMA((NS,)),
            pltpu.SemaphoreType.DMA((NS,)),
        ],
        compiler_params=pltpu.CompilerParams(collective_id=1, has_side_effects=True),
        name="reduce_part",
    )(part, square, order, weights, basis)


def shards(charges, weights, cell_order, leaf_coords, near_src):
    weights = weights.reshape(TL * 8, 128)
    inverse, square = exchange(cell_order, weights)
    part = local_part(leaf_coords, charges, inverse)
    return tuple(reduce_part(part, square, cell_order, weights))


def solution(mesh):
    placed = (P(None, "src"), P("tgt"), P(("tgt", "src"), None), P(), P("tgt", None))
    return jax.shard_map(
        shards,
        mesh=mesh,
        in_specs=placed,
        out_specs=(P(None, ("tgt", "src")), P()),
        check_vma=False,
    )
```

```python
import math

import jax
import jax.numpy as jnp
import numpy as np
from jax import lax
from jax.experimental import pallas as pl
from jax.experimental.pallas import tpu as pltpu
from jax.sharding import PartitionSpec as P

EDGE = 8
LEAF = 1024
SCEN = 8
LV = 128
NT = 16
NS = 8
TL = LV // NT
SL = LV // NS
NODES = 64
CELLS = LV * LEAF
VMEM = 60 << 20
MESH = pl.DeviceIdType.MESH
F32 = jnp.float32
BF16 = jnp.bfloat16
NT_DIMS = (((1,), (1,)), ((), ()))


def chebyshev_nodes(extent):
    return [
        extent * 0.5 + extent * 0.5 * math.cos((2.0 * a + 1.0) * (math.pi / 8.0)) for a in range(4)
    ]


def lagrange(points, nodes, a):
    factor = 1.0
    for b in range(4):
        if b != a:
            factor = factor * ((points - nodes[b]) * (1.0 / (nodes[a] - nodes[b])))
    return factor


def select_by(index, values):
    out = values[0]
    for k in range(1, len(values)):
        out = jnp.where(index == k, values[k], out)
    return out


def basis_by_plane():
    row = lax.broadcasted_iota(jnp.int32, (16, 128), 0)
    lane = lax.broadcasted_iota(jnp.int32, (16, 128), 1)
    short, tall = chebyshev_nodes(8.0), chebyshev_nodes(16.0)
    y = lax.shift_right_logical(lane, 4).astype(F32) + 0.5
    z = jnp.bitwise_and(lane, 15).astype(F32) + 0.5
    along_y = select_by(lax.shift_right_logical(row, 2), [lagrange(y, short, k) for k in range(4)])
    along_z = select_by(jnp.bitwise_and(row, 3), [lagrange(z, tall, k) for k in range(4)])
    plane = along_y * along_z
    return [
        jnp.concatenate([plane * float(lagrange(x + 0.5, short, a)) for a in range(4)], axis=0)
        for x in range(8)
    ]


def node_offset(index):
    short, tall = chebyshev_nodes(8.0), chebyshev_nodes(16.0)
    return [
        select_by(lax.shift_right_logical(index, 4), short),
        select_by(jnp.bitwise_and(lax.shift_right_logical(index, 2), 3), short),
        select_by(jnp.bitwise_and(index, 3), tall),
    ]


def split_two(value):
    high = value.astype(BF16)
    return high, (value - high.astype(F32)).astype(BF16)


def near_tables(table, table_out, sems):
    row = lax.broadcasted_iota(jnp.int32, (128, 128), 0)
    lane = lax.broadcasted_iota(jnp.int32, (128, 128), 1)
    step_y = lax.shift_right_logical(lane, 4) - lax.shift_right_logical(row, 4)
    step_z = jnp.bitwise_and(lane, 15) - jnp.bitwise_and(row, 15)

    def one(o, carry):
        dy = step_y - 8 * (lax.div(o, 3) - 1)
        dz = step_z - 16 * (lax.rem(o, 3) - 1)
        base = (dy * dy + dz * dz).astype(F32)
        for delta in range(16):
            value = 0.05 * lax.rsqrt(base + float(delta * delta + 1))
            table[o, :, delta * 128 : (delta + 1) * 128] = value.astype(BF16)
        pltpu.make_async_copy(table.at[o], table_out.at[o], sems.at[o]).start()
        return carry

    lax.fori_loop(0, 9, one, 0)


def far_tables(coords, i, j, phi, phi_out, sem):
    lane = lax.broadcasted_iota(jnp.int32, (1, TL * NODES), 1)
    slot = lax.shift_right_logical(lane, 6)
    spacing = (8.0, 8.0, 16.0)
    box_at = [select_by(slot, [coords[d, i * TL + t] for t in range(TL)]) for d in range(3)]
    offset = node_offset(jnp.bitwise_and(lane, 63))
    node_at = [box_at[d].astype(F32) * spacing[d] + offset[d] for d in range(3)]
    source = node_offset(lax.broadcasted_iota(jnp.int32, (NODES, TL * NODES), 0))

    def one(s, carry):
        distance = 1.0
        close = None
        for d in range(3):
            box = coords[d, j * SL + s]
            inside = jnp.abs(box_at[d] - box) <= 1
            close = inside if close is None else close & inside
            between = (node_at[d] - box.astype(F32) * spacing[d]) - source[d]
            distance = distance + between * between
        high, low = split_two(jnp.where(close, 0.0, 0.05) * lax.rsqrt(distance))
        phi[0, s] = high
        phi[1, s] = low
        return carry

    lax.fori_loop(0, SL, one, 0)
    pltpu.make_async_copy(phi, phi_out, sem).start()


def exchange_kernel(
    coords, order_ref, w_ref, inv_ref, sq_ref, table_out, phi_out, mine, buf, table, phi, send_a, recv_a, send_b, recv_b, table_sem, phi_sem
):
    a = lax.axis_index("tgt")
    b = lax.axis_index("src")
    barrier = pltpu.get_barrier_semaphore()
    home = lax.rem(a, 2) * NS + b
    column = lax.div(a, 2)
    loops_back = b == column

    def signal_sender(k, carry):
        pl.semaphore_signal(
            barrier, 1, device_id=(2 * b + lax.div(k, NS), lax.rem(k, NS)), device_id_type=MESH
        )
        return carry

    def signal_peer(k, carry):
        pl.semaphore_signal(barrier, 1, device_id=(lax.rem(a + k, NT), b), device_id_type=MESH)
        return carry

    own_sender = lax.rem(a, 2) * NS + b
    sends_to_me = lax.div(a, 2) == b

    def signal_other(k, carry):
        at = lax.rem(own_sender + k, NT)
        return signal_sender(at, carry)

    @pl.when(jnp.logical_not(sends_to_me))
    def _():
        signal_other(0, 0)

    lax.fori_loop(1, NT, signal_other, 0)
    lax.fori_loop(1, NT, signal_peer, 0)

    rows = lax.broadcasted_iota(jnp.int32, (8, 128), 0)
    lanes = lax.broadcasted_iota(jnp.int32, (8, 128), 1)
    low_rows = lax.broadcasted_iota(jnp.int32, (128, 128), 0)
    weights = w_ref[pl.ds(pl.multiple_of(b * 8, 8), 8), :]
    square = weights * weights
    placed = jnp.zeros((40, 128), F32)
    for c in range(8):
        order = order_ref[0:1, c * 128 : (c + 1) * 128]
        hit = lax.shift_right_logical(jnp.broadcast_to(order, (8, 128)), 7) == rows
        value = jnp.broadcast_to(square[c : c + 1, :], (8, 128))
        first = value.astype(BF16).astype(F32)
        rest = value - first
        second = rest.astype(BF16).astype(F32)
        third = rest - second
        parts = [jnp.full((8, 128), float(c), F32), lanes.astype(F32), first, second, third]
        left = jnp.concatenate([jnp.where(hit, part, 0.0) for part in parts], axis=0)
        low = jnp.broadcast_to(jnp.bitwise_and(order, 127), (128, 128)) == low_rows
        right = jnp.where(low, 1.0, 0.0).astype(BF16)
        placed = placed + lax.dot_general(
            left.astype(BF16), right, NT_DIMS, preferred_element_type=F32
        )
    inverse = (placed[0:8] * 128.0 + placed[8:16]).astype(jnp.int32)
    mine[...] = inverse
    buf[a] = placed[16:24] + placed[24:32] + placed[32:40]

    pl.semaphore_wait(
        barrier, jnp.where(loops_back, 2 * NT - 2, 2 * NT - 1).astype(jnp.int32)
    )

    def order_copy(k):
        at = lax.rem(a + k, NT)
        return pltpu.make_async_remote_copy(
            src_ref=mine,
            dst_ref=inv_ref.at[home],
            send_sem=send_a.at[k],
            recv_sem=recv_a.at[home],
            device_id=(at, column),
            device_id_type=MESH,
        )

    def square_copy(k):
        return pltpu.make_async_remote_copy(
            src_ref=buf.at[a],
            dst_ref=buf.at[a],
            send_sem=send_b.at[k],
            recv_sem=recv_b.at[a],
            device_id=(lax.rem(a + k, NT), b),
            device_id_type=MESH,
        )

    @pl.when(jnp.logical_not(loops_back))
    def _():
        order_copy(0).start()

    @pl.when(loops_back)
    def _():
        inv_ref[home] = inverse

    def start_both(k, carry):
        order_copy(k).start()
        square_copy(k).start()
        return carry

    lax.fori_loop(1, NT, start_both, 0)
    far_tables(coords, a, b, phi, phi_out, phi_sem)
    near_tables(table, table_out, table_sem)

    def order_arrival(slot):
        pltpu.make_async_remote_copy(
            src_ref=mine,
            dst_ref=inv_ref.at[slot],
            send_sem=send_a.at[0],
            recv_sem=recv_a.at[slot],
            device_id=(a, b),
            device_id_type=MESH,
        ).wait_recv()

    def square_arrival(slot):
        pltpu.make_async_remote_copy(
            src_ref=mine,
            dst_ref=buf.at[slot],
            send_sem=send_b.at[0],
            recv_sem=recv_b.at[slot],
            device_id=(a, b),
            device_id_type=MESH,
        ).wait_recv()

    @pl.when(jnp.logical_not(loops_back))
    def _():
        order_arrival(home)
        order_copy(0).wait_send()

    def wait_both(k, carry):
        order_arrival(lax.rem(home + k, NT))
        square_arrival(lax.rem(a + k, NT))
        order_copy(k).wait_send()
        square_copy(k).wait_send()
        return carry

    lax.fori_loop(1, NT, wait_both, 0)
    total = buf[0]
    for k in range(1, NT):
        total = total + buf[k]
    sq_ref[...] = total
    pltpu.make_async_copy(phi, phi_out, phi_sem).wait()
    for o in range(9):
        pltpu.make_async_copy(table.at[o], table_out.at[o], table_sem.at[o]).wait()


def exchange(coords, order, weights):
    vmem = pl.BlockSpec(memory_space=pltpu.VMEM)
    hbm = pl.BlockSpec(memory_space=pltpu.HBM)
    return pl.pallas_call(
        exchange_kernel,
        out_shape=(
            jax.ShapeDtypeStruct((SL, 8, 128), jnp.int32),
            jax.ShapeDtypeStruct((8, 128), F32),
            jax.ShapeDtypeStruct((9, 128, 2048), BF16),
            jax.ShapeDtypeStruct((2, SL, NODES, TL * NODES), BF16),
        ),
        in_specs=[pl.BlockSpec(memory_space=pltpu.SMEM), vmem, vmem],
        out_specs=(vmem, vmem, hbm, hbm),
        scratch_shapes=[
            pltpu.VMEM((8, 128), jnp.int32),
            pltpu.VMEM((NT, 8, 128), F32),
            pltpu.VMEM((9, 128, 2048), BF16),
            pltpu.VMEM((2, SL, NODES, TL * NODES), BF16),
            pltpu.SemaphoreType.DMA((NT,)),
            pltpu.SemaphoreType.DMA((NT,)),
            pltpu.SemaphoreType.DMA((NT,)),
            pltpu.SemaphoreType.DMA((NT,)),
            pltpu.SemaphoreType.DMA((9,)),
            pltpu.SemaphoreType.DMA,
        ],
        compiler_params=pltpu.CompilerParams(
            collective_id=0, has_side_effects=True, vmem_limit_bytes=VMEM
        ),
        name="exchange",
    )(coords, order, weights)


def lane_gather(block, lane):
    return jnp.take_along_axis(block, lane, axis=1, mode="promise_in_bounds")


def permute_row(blocks, index):
    block = lax.shift_right_logical(index, 7)
    lane = jnp.bitwise_and(index, 127)
    out = lane_gather(blocks[0], lane)
    for k in range(1, 8):
        out = jnp.where(block == k, lane_gather(blocks[k], lane), out)
    return out


def local_kernel(
    coords, charges_hbm, inv_hbm, table_hbm, phi_hbm, out, charges, inv, table, phi, qf, qb, pairs, counts, sems
):
    i = lax.axis_index("tgt")
    j = lax.axis_index("src")
    fetches = [
        pltpu.make_async_copy(source, target, sems.at[k])
        for k, (source, target) in enumerate(
            [(charges_hbm, charges), (inv_hbm, inv), (phi_hbm, phi), (table_hbm, table)]
        )
    ]
    for fetch in fetches:
        fetch.start()

    def list_target(t, carry):
        box = [coords[d, i * TL + t] for d in range(3)]
        for s in range(SL):
            step = [coords[d, j * SL + s] - box[d] for d in range(3)]
            close = jnp.maximum(jnp.maximum(jnp.abs(step[0]), jnp.abs(step[1])), jnp.abs(step[2])) <= 1
            row = jnp.clip(step[0] + 1, 0, 2)
            count = counts[row]
            pairs[row, count] = t + 8 * s + 256 * ((step[1] + 1) * 3 + step[2] + 1)
            counts[row] = count + close.astype(jnp.int32)
        return carry

    for k in range(3):
        counts[k] = 0
    lax.fori_loop(0, TL, list_target, 0)
    for k in range(3):
        pairs[k, counts[k]] = 8 * SL
    qb[SL] = jnp.zeros((64, 128), BF16)

    fetches[0].wait()
    fetches[1].wait()

    def canonical(leaf, carry):
        base = pl.multiple_of(leaf * LEAF, LEAF)
        raw = charges[:, pl.ds(base, LEAF)].astype(F32)
        blocks = [raw[:, k * 128 : (k + 1) * 128] for k in range(8)]
        order = inv[leaf]
        pieces = [
            permute_row(blocks, jnp.broadcast_to(order[x : x + 1, :], (8, 128))) for x in range(8)
        ]
        rows = jnp.concatenate(pieces, axis=0)
        qf[leaf] = rows
        qb[leaf] = rows.astype(BF16)
        return carry

    lax.fori_loop(0, SL, canonical, 0)

    basis = [split_two(plane) for plane in basis_by_plane()]
    moments = jnp.zeros((SL * SCEN, NODES), F32)
    for x in range(8):
        rows = qf[:, x * 8 : (x + 1) * 8, :].reshape(SL * SCEN, 128).astype(BF16)
        for part in basis[x]:
            moments = moments + lax.dot_general(rows, part, NT_DIMS, preferred_element_type=F32)

    fetches[2].wait()
    coeff = jnp.zeros((SCEN, TL * NODES), F32)
    for s in range(SL):
        high, low = phi[0, s], phi[1, s]
        part_high, part_low = split_two(moments[s * 8 : (s + 1) * 8, :])
        twice = jnp.concatenate([part_high.astype(F32), part_low.astype(F32)], axis=0).astype(BF16)
        product = jnp.dot(twice, high, preferred_element_type=F32)
        coeff = coeff + product[:8] + product[8:]
        coeff = coeff + jnp.dot(part_high, low, preferred_element_type=F32)

    stacked = jnp.concatenate(
        [coeff[:, t * NODES : (t + 1) * NODES] for t in range(TL)], axis=0
    )
    stacked_high, stacked_low = split_two(stacked)
    for x in range(8):
        high, low = basis[x]
        far = jnp.dot(stacked_high, high, preferred_element_type=F32)
        far = far + jnp.dot(stacked_low, high, preferred_element_type=F32)
        far = far + jnp.dot(stacked_high, low, preferred_element_type=F32)
        for t in range(TL):
            out[t, :, x * 128 : (x + 1) * 128] = far[t * 8 : (t + 1) * 8, :]

    fetches[3].wait()

    def near_pairs(value):
        def contribution(code):
            s = jnp.bitwise_and(lax.shift_right_logical(code, 3), 31)
            which = lax.shift_right_logical(code, 8)
            left = qb[s]
            total = [None] * 8
            for chunk in range(4 if value == 1 else 8):
                product = jnp.dot(
                    left,
                    table[which, :, chunk * 256 : (chunk + 1) * 256],
                    preferred_element_type=F32,
                )
                for half in range(2):
                    delta = 2 * chunk + half
                    for sx in range(8):
                        piece = product[sx * 8 : (sx + 1) * 8, half * 128 : (half + 1) * 128]
                        if value == 1:
                            hits = {sx - delta, sx + delta}
                        elif value == 2:
                            hits = {8 + sx - delta}
                        else:
                            hits = {delta - 8 + sx}
                        for x in sorted(hits):
                            if 0 <= x < 8:
                                total[x] = piece if total[x] is None else total[x] + piece
            return total

        def two(n, carry):
            codes = [pairs[value, 2 * n], pairs[value, 2 * n + 1]]
            totals = [contribution(code) for code in codes]
            for code, total in zip(codes, totals):
                t = jnp.bitwise_and(code, 7)
                for x in range(8):
                    out[t, :, x * 128 : (x + 1) * 128] += total[x]
            return carry

        lax.fori_loop(0, lax.shift_right_logical(counts[value] + 1, 1), two, 0)

    for value in range(3):
        near_pairs(value)


def local_part(leaf_coords, charges, inverse, table, phi):
    hbm = pl.BlockSpec(memory_space=pltpu.HBM)
    return pl.pallas_call(
        local_kernel,
        out_shape=jax.ShapeDtypeStruct((TL, SCEN, LEAF), F32),
        in_specs=[pl.BlockSpec(memory_space=pltpu.SMEM)] + [hbm] * 4,
        out_specs=pl.BlockSpec(memory_space=pltpu.VMEM),
        scratch_shapes=[
            pltpu.VMEM((SCEN, SL * LEAF), BF16),
            pltpu.VMEM((SL, 8, 128), jnp.int32),
            pltpu.VMEM((9, 128, 2048), BF16),
            pltpu.VMEM((2, SL, NODES, TL * NODES), BF16),
            pltpu.VMEM((SL, 64, 128), F32),
            pltpu.VMEM((SL + 1, 64, 128), BF16),
            pltpu.SMEM((3, 136), jnp.int32),
            pltpu.SMEM((8,), jnp.int32),
            pltpu.SemaphoreType.DMA((4,)),
        ],
        compiler_params=pltpu.CompilerParams(vmem_limit_bytes=VMEM),
        name="local_part",
    )(leaf_coords, charges, inverse, table, phi)


def cholesky(gram, root_ref):
    full = (8, NODES)
    lane = lax.broadcasted_iota(jnp.int32, full, 1)
    row_at = lax.broadcasted_iota(jnp.int32, full, 0)
    left = [gram[8 * k : 8 * k + 8, :] for k in range(8)]
    scale = 1.0 / math.sqrt(CELLS)
    for kb in range(8):
        base = 8 * kb
        rows = [jnp.broadcast_to(left[kb][r : r + 1, :], full) for r in range(8)]
        cols = [
            [jnp.broadcast_to(left[m][:, base + q : base + q + 1], full) for q in range(8)]
            for m in range(kb, 8)
        ]
        splat = [
            [jnp.broadcast_to(cols[0][q][r : r + 1, :], full) if q >= r else None for q in range(8)]
            for r in range(8)
        ]
        out = jnp.zeros(full, F32)
        for r in range(8):
            root = lax.rsqrt(splat[r][r])
            inverse = root * root
            for q in range(r + 1, 8):
                factor = splat[r][q] * inverse
                for p in range(q, 8):
                    splat[q][p] = splat[q][p] - factor * splat[r][p]
                rows[q] = rows[q] - factor * rows[r]
                for m in range(1, len(cols)):
                    cols[m][q] = cols[m][q] - factor * cols[m][r]
            here = (row_at == r) & (lane >= base + r)
            out = jnp.where(here, rows[r] * (root * scale), out)
            for m in range(1, len(cols)):
                left[kb + m] = left[kb + m] - cols[m][r] * (rows[r] * inverse)
        root_ref[base : base + 8, :] = out


def reduce_kernel(
    part_ref, sq_ref, order_ref, w_ref, pot_ref, root_ref, recv, buf, send_a, recv_a, send_b, recv_b, own_sem
):
    a = lax.axis_index("tgt")
    b = lax.axis_index("src")
    barrier = pltpu.get_barrier_semaphore()

    def greet(k, carry):
        pl.semaphore_signal(barrier, 1, device_id=(a, lax.rem(b + k, NS)), device_id_type=MESH)
        return carry

    lax.fori_loop(1, NS, greet, 0)
    buf[b] = sq_ref[...]
    pl.semaphore_wait(barrier, NS - 1)

    def square_copy(k):
        return pltpu.make_async_remote_copy(
            src_ref=buf.at[b],
            dst_ref=buf.at[b],
            send_sem=send_b.at[k],
            recv_sem=recv_b.at[b],
            device_id=(a, lax.rem(b + k, NS)),
            device_id_type=MESH,
        )

    def part_copy(k):
        at = lax.rem(b + k, NS)
        return pltpu.make_async_remote_copy(
            src_ref=part_ref.at[at],
            dst_ref=recv.at[b],
            send_sem=send_a.at[k],
            recv_sem=recv_a.at[b],
            device_id=(a, at),
            device_id_type=MESH,
        )

    def start(copy):
        def step(k, carry):
            copy(k).start()
            return carry

        lax.fori_loop(1, NS, step, 0)

    start(square_copy)
    start(part_copy)
    own_copy = pltpu.make_async_copy(part_ref.at[b], recv.at[b], own_sem)
    own_copy.start()
    planes = basis_by_plane()

    def square_wait(k, carry):
        slot = lax.rem(b + k, NS)
        pltpu.make_async_remote_copy(
            src_ref=buf.at[b],
            dst_ref=buf.at[slot],
            send_sem=send_b.at[0],
            recv_sem=recv_b.at[slot],
            device_id=(a, b),
            device_id_type=MESH,
        ).wait_recv()
        square_copy(k).wait_send()
        return carry

    lax.fori_loop(1, NS, square_wait, 0)
    square = buf[0]
    for k in range(1, NS):
        square = square + buf[k]
    basis = jnp.concatenate(planes, axis=1)
    scaled = jnp.concatenate([planes[k] * square[k : k + 1, :] for k in range(8)], axis=1)
    gram = lax.dot_general(
        scaled, basis, NT_DIMS, precision=lax.Precision.HIGHEST, preferred_element_type=F32
    )
    cholesky(gram, root_ref)

    def part_wait(k, carry):
        slot = lax.rem(b + k, NS)
        pltpu.make_async_remote_copy(
            src_ref=part_ref.at[0],
            dst_ref=recv.at[slot],
            send_sem=send_a.at[0],
            recv_sem=recv_a.at[slot],
            device_id=(a, b),
            device_id_type=MESH,
        ).wait_recv()
        part_copy(k).wait_send()
        return carry

    own_copy.wait()
    lax.fori_loop(1, NS, part_wait, 0)
    total = recv[0]
    for k in range(1, NS):
        total = total + recv[k]
    blocks = [total[:, k * 128 : (k + 1) * 128] for k in range(8)]
    weights = w_ref[pl.ds(pl.multiple_of(b * 8, 8), 8), :]
    for c in range(8):
        index = jnp.broadcast_to(order_ref[0:1, c * 128 : (c + 1) * 128], (8, 128))
        value = permute_row(blocks, index) * weights[c : c + 1, :]
        pot_ref[:, c * 128 : (c + 1) * 128] = value.astype(BF16)


def reduce_part(part, square, order, weights):
    vmem = pl.BlockSpec(memory_space=pltpu.VMEM)
    return pl.pallas_call(
        reduce_kernel,
        out_shape=(
            jax.ShapeDtypeStruct((SCEN, LEAF), BF16),
            jax.ShapeDtypeStruct((NODES, NODES), F32),
        ),
        in_specs=[pl.BlockSpec(memory_space=pltpu.HBM)] + [vmem] * 3,
        out_specs=(vmem, vmem),
        scratch_shapes=[
            pltpu.VMEM((NS, SCEN, LEAF), F32),
            pltpu.VMEM((NS, 8, 128), F32),
            pltpu.SemaphoreType.DMA((NS,)),
            pltpu.SemaphoreType.DMA((NS,)),
            pltpu.SemaphoreType.DMA((NS,)),
            pltpu.SemaphoreType.DMA((NS,)),
            pltpu.SemaphoreType.DMA,
        ],
        compiler_params=pltpu.CompilerParams(
            collective_id=1, has_side_effects=True, vmem_limit_bytes=VMEM
        ),
        name="reduce_part",
    )(part, square, order, weights)


def shards(charges, weights, cell_order, leaf_coords, near_src):
    weights = weights.reshape(TL * 8, 128)
    inverse, square, table, phi = exchange(leaf_coords, cell_order, weights)
    part = local_part(leaf_coords, charges, inverse, table, phi)
    return tuple(reduce_part(part, square, cell_order, weights))


def solution(mesh):
    placed = (P(None, "src"), P("tgt"), P(("tgt", "src"), None), P(), P("tgt", None))
    return jax.shard_map(
        shards,
        mesh=mesh,
        in_specs=placed,
        out_specs=(P(None, ("tgt", "src")), P()),
        check_vma=False,
    )
```

```python
import math

import jax
import jax.numpy as jnp
import numpy as np
from jax import lax
from jax.experimental import pallas as pl
from jax.experimental.pallas import tpu as pltpu
from jax.sharding import PartitionSpec as P

EDGE = 8
LEAF = 1024
SCEN = 8
LV = 128
NT = 16
NS = 8
TL = LV // NT
SL = LV // NS
NODES = 64
CELLS = LV * LEAF
VMEM = 60 << 20
MESH = pl.DeviceIdType.MESH
F32 = jnp.float32
BF16 = jnp.bfloat16
NT_DIMS = (((1,), (1,)), ((), ()))


def chebyshev_nodes(extent):
    return [
        extent * 0.5 + extent * 0.5 * math.cos((2.0 * a + 1.0) * (math.pi / 8.0)) for a in range(4)
    ]


def lagrange(points, nodes, a):
    factor = 1.0
    for b in range(4):
        if b != a:
            factor = factor * ((points - nodes[b]) * (1.0 / (nodes[a] - nodes[b])))
    return factor


def select_by(index, values):
    out = values[0]
    for k in range(1, len(values)):
        out = jnp.where(index == k, values[k], out)
    return out


def basis_by_plane():
    row = lax.broadcasted_iota(jnp.int32, (16, 128), 0)
    lane = lax.broadcasted_iota(jnp.int32, (16, 128), 1)
    short, tall = chebyshev_nodes(8.0), chebyshev_nodes(16.0)
    y = lax.shift_right_logical(lane, 4).astype(F32) + 0.5
    z = jnp.bitwise_and(lane, 15).astype(F32) + 0.5
    along_y = select_by(lax.shift_right_logical(row, 2), [lagrange(y, short, k) for k in range(4)])
    along_z = select_by(jnp.bitwise_and(row, 3), [lagrange(z, tall, k) for k in range(4)])
    plane = along_y * along_z
    return [
        jnp.concatenate([plane * float(lagrange(x + 0.5, short, a)) for a in range(4)], axis=0)
        for x in range(8)
    ]


def node_offset(index):
    short, tall = chebyshev_nodes(8.0), chebyshev_nodes(16.0)
    return [
        select_by(lax.shift_right_logical(index, 4), short),
        select_by(jnp.bitwise_and(lax.shift_right_logical(index, 2), 3), short),
        select_by(jnp.bitwise_and(index, 3), tall),
    ]


def split_two(value):
    high = value.astype(BF16)
    return high, (value - high.astype(F32)).astype(BF16)


def near_tables(table, table_out, sems):
    row = lax.broadcasted_iota(jnp.int32, (128, 128), 0)
    lane = lax.broadcasted_iota(jnp.int32, (128, 128), 1)
    step_y = lax.shift_right_logical(lane, 4) - lax.shift_right_logical(row, 4)
    step_z = jnp.bitwise_and(lane, 15) - jnp.bitwise_and(row, 15)

    def one(o, carry):
        dy = step_y - 8 * (lax.div(o, 3) - 1)
        dz = step_z - 16 * (lax.rem(o, 3) - 1)
        base = (dy * dy + dz * dz).astype(F32)
        for delta in range(16):
            value = 0.05 * lax.rsqrt(base + float(delta * delta + 1))
            table[o, :, delta * 128 : (delta + 1) * 128] = value.astype(BF16)
        pltpu.make_async_copy(table.at[o], table_out.at[o], sems.at[o]).start()
        return carry

    lax.fori_loop(0, 9, one, 0)


def far_tables(coords, i, j, phi, phi_out, sem):
    lane = lax.broadcasted_iota(jnp.int32, (1, TL * NODES), 1)
    slot = lax.shift_right_logical(lane, 6)
    spacing = (8.0, 8.0, 16.0)
    box_at = [select_by(slot, [coords[d, i * TL + t] for t in range(TL)]) for d in range(3)]
    offset = node_offset(jnp.bitwise_and(lane, 63))
    node_at = [box_at[d].astype(F32) * spacing[d] + offset[d] for d in range(3)]
    source = node_offset(lax.broadcasted_iota(jnp.int32, (NODES, TL * NODES), 0))

    def one(s, carry):
        distance = 1.0
        close = None
        for d in range(3):
            box = coords[d, j * SL + s]
            inside = jnp.abs(box_at[d] - box) <= 1
            close = inside if close is None else close & inside
            between = (node_at[d] - box.astype(F32) * spacing[d]) - source[d]
            distance = distance + between * between
        high, low = split_two(jnp.where(close, 0.0, 0.05) * lax.rsqrt(distance))
        phi[0, s] = high
        phi[1, s] = low
        return carry

    lax.fori_loop(0, SL, one, 0)
    pltpu.make_async_copy(phi, phi_out, sem).start()


def exchange_kernel(
    coords_hbm, order_hbm, w_hbm, inv_ref, sq_ref, table_out, phi_out,
    coords, order_ref, w_ref, mine, buf, table, phi,
    send_a, recv_a, send_b, recv_b, table_sem, phi_sem, in_sem, own_sem, sq_sem,
):
    a = lax.axis_index("tgt")
    b = lax.axis_index("src")
    barrier = pltpu.get_barrier_semaphore()
    home = lax.rem(a, 2) * NS + b
    column = lax.div(a, 2)
    loops_back = b == column

    def signal_sender(k, carry):
        pl.semaphore_signal(
            barrier, 1, device_id=(2 * b + lax.div(k, NS), lax.rem(k, NS)), device_id_type=MESH
        )
        return carry

    def signal_peer(k, carry):
        pl.semaphore_signal(barrier, 1, device_id=(lax.rem(a + k, NT), b), device_id_type=MESH)
        return carry

    own_sender = lax.rem(a, 2) * NS + b
    sends_to_me = lax.div(a, 2) == b

    def signal_other(k, carry):
        at = lax.rem(own_sender + k, NT)
        return signal_sender(at, carry)

    @pl.when(jnp.logical_not(sends_to_me))
    def _():
        signal_other(0, 0)

    lax.fori_loop(1, NT, signal_other, 0)
    lax.fori_loop(1, NT, signal_peer, 0)

    fetches = [
        pltpu.make_async_copy(order_hbm, order_ref, in_sem.at[0]),
        pltpu.make_async_copy(w_hbm.at[pl.ds(pl.multiple_of(b * 8, 8), 8)], w_ref, in_sem.at[1]),
        pltpu.make_async_copy(coords_hbm, coords, in_sem.at[2]),
    ]
    for fetch in fetches:
        fetch.start()
    for fetch in fetches:
        fetch.wait()

    rows = lax.broadcasted_iota(jnp.int32, (8, 128), 0)
    lanes = lax.broadcasted_iota(jnp.int32, (8, 128), 1)
    low_rows = lax.broadcasted_iota(jnp.int32, (128, 128), 0)
    weights = w_ref[...]
    square = weights * weights
    placed = jnp.zeros((40, 128), F32)
    for c in range(8):
        order = order_ref[0:1, c * 128 : (c + 1) * 128]
        hit = lax.shift_right_logical(jnp.broadcast_to(order, (8, 128)), 7) == rows
        value = jnp.broadcast_to(square[c : c + 1, :], (8, 128))
        first = value.astype(BF16).astype(F32)
        rest = value - first
        second = rest.astype(BF16).astype(F32)
        third = rest - second
        parts = [jnp.full((8, 128), float(c), F32), lanes.astype(F32), first, second, third]
        left = jnp.concatenate([jnp.where(hit, part, 0.0) for part in parts], axis=0)
        low = jnp.broadcast_to(jnp.bitwise_and(order, 127), (128, 128)) == low_rows
        right = jnp.where(low, 1.0, 0.0).astype(BF16)
        placed = placed + lax.dot_general(
            left.astype(BF16), right, NT_DIMS, preferred_element_type=F32
        )
    inverse = (placed[0:8] * 128.0 + placed[8:16]).astype(jnp.int32)
    mine[...] = inverse
    buf[a] = placed[16:24] + placed[24:32] + placed[32:40]

    pl.semaphore_wait(
        barrier, jnp.where(loops_back, 2 * NT - 2, 2 * NT - 1).astype(jnp.int32)
    )

    def order_copy(k):
        at = lax.rem(a + k, NT)
        return pltpu.make_async_remote_copy(
            src_ref=mine,
            dst_ref=inv_ref.at[home],
            send_sem=send_a.at[k],
            recv_sem=recv_a.at[home],
            device_id=(at, column),
            device_id_type=MESH,
        )

    def square_copy(k):
        return pltpu.make_async_remote_copy(
            src_ref=buf.at[a],
            dst_ref=buf.at[a],
            send_sem=send_b.at[k],
            recv_sem=recv_b.at[a],
            device_id=(lax.rem(a + k, NT), b),
            device_id_type=MESH,
        )

    @pl.when(jnp.logical_not(loops_back))
    def _():
        order_copy(0).start()

    own_copy = pltpu.make_async_copy(mine, inv_ref.at[home], own_sem)

    @pl.when(loops_back)
    def _():
        own_copy.start()

    def start_both(k, carry):
        order_copy(k).start()
        square_copy(k).start()
        return carry

    lax.fori_loop(1, NT, start_both, 0)
    far_tables(coords, a, b, phi, phi_out, phi_sem)
    near_tables(table, table_out, table_sem)

    def order_arrival(slot):
        pltpu.make_async_remote_copy(
            src_ref=mine,
            dst_ref=inv_ref.at[slot],
            send_sem=send_a.at[0],
            recv_sem=recv_a.at[slot],
            device_id=(a, b),
            device_id_type=MESH,
        ).wait_recv()

    def square_arrival(slot):
        pltpu.make_async_remote_copy(
            src_ref=mine,
            dst_ref=buf.at[slot],
            send_sem=send_b.at[0],
            recv_sem=recv_b.at[slot],
            device_id=(a, b),
            device_id_type=MESH,
        ).wait_recv()

    @pl.when(jnp.logical_not(loops_back))
    def _():
        order_arrival(home)
        order_copy(0).wait_send()

    def wait_both(k, carry):
        order_arrival(lax.rem(home + k, NT))
        square_arrival(lax.rem(a + k, NT))
        order_copy(k).wait_send()
        square_copy(k).wait_send()
        return carry

    @pl.when(loops_back)
    def _():
        own_copy.wait()

    lax.fori_loop(1, NT, wait_both, 0)
    total = buf[0]
    for k in range(1, NT):
        total = total + buf[k]
    mine_sq = buf.at[NT]
    mine_sq[...] = total
    sq_copy = pltpu.make_async_copy(mine_sq, sq_ref, sq_sem)
    sq_copy.start()
    sq_copy.wait()
    pltpu.make_async_copy(phi, phi_out, phi_sem).wait()
    for o in range(9):
        pltpu.make_async_copy(table.at[o], table_out.at[o], table_sem.at[o]).wait()


def exchange(coords, order, weights):
    hbm = pl.BlockSpec(memory_space=pltpu.HBM)
    return pl.pallas_call(
        exchange_kernel,
        out_shape=(
            jax.ShapeDtypeStruct((SL, 8, 128), jnp.int32),
            jax.ShapeDtypeStruct((8, 128), F32),
            jax.ShapeDtypeStruct((9, 128, 2048), BF16),
            jax.ShapeDtypeStruct((2, SL, NODES, TL * NODES), BF16),
        ),
        in_specs=[hbm] * 3,
        out_specs=(hbm,) * 4,
        scratch_shapes=[
            pltpu.SMEM((3, LV), jnp.int32),
            pltpu.VMEM((1, LEAF), jnp.int32),
            pltpu.VMEM((8, 128), F32),
            pltpu.VMEM((8, 128), jnp.int32),
            pltpu.VMEM((NT + 1, 8, 128), F32),
            pltpu.VMEM((9, 128, 2048), BF16),
            pltpu.VMEM((2, SL, NODES, TL * NODES), BF16),
            pltpu.SemaphoreType.DMA((NT,)),
            pltpu.SemaphoreType.DMA((NT,)),
            pltpu.SemaphoreType.DMA((NT,)),
            pltpu.SemaphoreType.DMA((NT,)),
            pltpu.SemaphoreType.DMA((9,)),
            pltpu.SemaphoreType.DMA,
            pltpu.SemaphoreType.DMA((3,)),
            pltpu.SemaphoreType.DMA,
            pltpu.SemaphoreType.DMA,
        ],
        compiler_params=pltpu.CompilerParams(
            collective_id=0, has_side_effects=True, vmem_limit_bytes=VMEM
        ),
        name="exchange",
    )(coords, order, weights)


def lane_gather(block, lane):
    return jnp.take_along_axis(block, lane, axis=1, mode="promise_in_bounds")


def permute_row(blocks, index):
    block = lax.shift_right_logical(index, 7)
    lane = jnp.bitwise_and(index, 127)
    out = lane_gather(blocks[0], lane)
    for k in range(1, 8):
        out = jnp.where(block == k, lane_gather(blocks[k], lane), out)
    return out


def local_kernel(
    coords, charges_hbm, inv_hbm, table_hbm, phi_hbm, out, charges, inv, table, phi, qf, qb, pairs, counts, sems
):
    i = lax.axis_index("tgt")
    j = lax.axis_index("src")
    fetches = [
        pltpu.make_async_copy(source, target, sems.at[k])
        for k, (source, target) in enumerate(
            [(charges_hbm, charges), (inv_hbm, inv), (phi_hbm, phi), (table_hbm, table)]
        )
    ]
    for fetch in fetches:
        fetch.start()

    def list_target(t, carry):
        box = [coords[d, i * TL + t] for d in range(3)]
        for s in range(SL):
            step = [coords[d, j * SL + s] - box[d] for d in range(3)]
            close = jnp.maximum(jnp.maximum(jnp.abs(step[0]), jnp.abs(step[1])), jnp.abs(step[2])) <= 1
            row = jnp.clip(step[0] + 1, 0, 2)
            count = counts[row]
            pairs[row, count] = t + 8 * s + 256 * ((step[1] + 1) * 3 + step[2] + 1)
            counts[row] = count + close.astype(jnp.int32)
        return carry

    for k in range(3):
        counts[k] = 0
    lax.fori_loop(0, TL, list_target, 0)
    for k in range(3):
        pairs[k, counts[k]] = 8 * SL
    qb[SL] = jnp.zeros((64, 128), BF16)

    fetches[0].wait()
    fetches[1].wait()

    def canonical(leaf, carry):
        base = pl.multiple_of(leaf * LEAF, LEAF)
        raw = charges[:, pl.ds(base, LEAF)].astype(F32)
        blocks = [raw[:, k * 128 : (k + 1) * 128] for k in range(8)]
        order = inv[leaf]
        pieces = [
            permute_row(blocks, jnp.broadcast_to(order[x : x + 1, :], (8, 128))) for x in range(8)
        ]
        rows = jnp.concatenate(pieces, axis=0)
        qf[leaf] = rows
        qb[leaf] = rows.astype(BF16)
        return carry

    lax.fori_loop(0, SL, canonical, 0)

    basis = [split_two(plane) for plane in basis_by_plane()]
    moments = jnp.zeros((SL * SCEN, NODES), F32)
    for x in range(8):
        rows = qf[:, x * 8 : (x + 1) * 8, :].reshape(SL * SCEN, 128).astype(BF16)
        for part in basis[x]:
            moments = moments + lax.dot_general(rows, part, NT_DIMS, preferred_element_type=F32)

    fetches[2].wait()
    coeff = jnp.zeros((SCEN, TL * NODES), F32)
    for s in range(SL):
        high, low = phi[0, s], phi[1, s]
        part_high, part_low = split_two(moments[s * 8 : (s + 1) * 8, :])
        twice = jnp.concatenate([part_high.astype(F32), part_low.astype(F32)], axis=0).astype(BF16)
        product = jnp.dot(twice, high, preferred_element_type=F32)
        coeff = coeff + product[:8] + product[8:]
        coeff = coeff + jnp.dot(part_high, low, preferred_element_type=F32)

    stacked = jnp.concatenate(
        [coeff[:, t * NODES : (t + 1) * NODES] for t in range(TL)], axis=0
    )
    stacked_high, stacked_low = split_two(stacked)
    left = jnp.concatenate([stacked_high, stacked_low, stacked_high], axis=1)
    right = jnp.concatenate(
        [jnp.concatenate([basis[x][k] for x in range(8)], axis=1) for k in (0, 0, 1)], axis=0
    )
    far = jnp.dot(left, right, preferred_element_type=F32)
    for t in range(TL):
        out[t] = far[t * 8 : (t + 1) * 8, :]

    fetches[3].wait()

    def near_pairs(value):
        def contribution(code):
            s = jnp.bitwise_and(lax.shift_right_logical(code, 3), 31)
            which = lax.shift_right_logical(code, 8)
            left = qb[s]
            total = [None] * 8
            for chunk in range(4 if value == 1 else 8):
                product = jnp.dot(
                    left,
                    table[which, :, chunk * 256 : (chunk + 1) * 256],
                    preferred_element_type=F32,
                )
                for half in range(2):
                    delta = 2 * chunk + half
                    for sx in range(8):
                        piece = product[sx * 8 : (sx + 1) * 8, half * 128 : (half + 1) * 128]
                        if value == 1:
                            hits = {sx - delta, sx + delta}
                        elif value == 2:
                            hits = {8 + sx - delta}
                        else:
                            hits = {delta - 8 + sx}
                        for x in sorted(hits):
                            if 0 <= x < 8:
                                total[x] = piece if total[x] is None else total[x] + piece
            return total

        def two(n, carry):
            codes = [pairs[value, 2 * n], pairs[value, 2 * n + 1]]
            totals = [contribution(code) for code in codes]
            for code, total in zip(codes, totals):
                t = jnp.bitwise_and(code, 7)
                for x in range(8):
                    out[t, :, x * 128 : (x + 1) * 128] += total[x]
            return carry

        lax.fori_loop(0, lax.shift_right_logical(counts[value] + 1, 1), two, 0)

    for value in range(3):
        near_pairs(value)


def local_part(leaf_coords, charges, inverse, table, phi):
    hbm = pl.BlockSpec(memory_space=pltpu.HBM)
    return pl.pallas_call(
        local_kernel,
        out_shape=jax.ShapeDtypeStruct((TL, SCEN, LEAF), F32),
        in_specs=[pl.BlockSpec(memory_space=pltpu.SMEM)] + [hbm] * 4,
        out_specs=pl.BlockSpec(memory_space=pltpu.VMEM),
        scratch_shapes=[
            pltpu.VMEM((SCEN, SL * LEAF), BF16),
            pltpu.VMEM((SL, 8, 128), jnp.int32),
            pltpu.VMEM((9, 128, 2048), BF16),
            pltpu.VMEM((2, SL, NODES, TL * NODES), BF16),
            pltpu.VMEM((SL, 64, 128), F32),
            pltpu.VMEM((SL + 1, 64, 128), BF16),
            pltpu.SMEM((3, 136), jnp.int32),
            pltpu.SMEM((8,), jnp.int32),
            pltpu.SemaphoreType.DMA((4,)),
        ],
        compiler_params=pltpu.CompilerParams(vmem_limit_bytes=VMEM),
        name="local_part",
    )(leaf_coords, charges, inverse, table, phi)


def cholesky(gram, root_ref):
    full = (8, NODES)
    lane = lax.broadcasted_iota(jnp.int32, full, 1)
    row_at = lax.broadcasted_iota(jnp.int32, full, 0)
    left = [gram[8 * k : 8 * k + 8, :] for k in range(8)]
    scale = 1.0 / math.sqrt(CELLS)
    for kb in range(8):
        base = 8 * kb
        rows = [jnp.broadcast_to(left[kb][r : r + 1, :], full) for r in range(8)]
        cols = [
            [jnp.broadcast_to(left[m][:, base + q : base + q + 1], full) for q in range(8)]
            for m in range(kb, 8)
        ]
        splat = [
            [jnp.broadcast_to(cols[0][q][r : r + 1, :], full) if q >= r else None for q in range(8)]
            for r in range(8)
        ]
        out = jnp.zeros(full, F32)
        for r in range(8):
            root = lax.rsqrt(splat[r][r])
            inverse = root * root
            for q in range(r + 1, 8):
                factor = splat[r][q] * inverse
                for p in range(q, 8):
                    splat[q][p] = splat[q][p] - factor * splat[r][p]
                rows[q] = rows[q] - factor * rows[r]
                for m in range(1, len(cols)):
                    cols[m][q] = cols[m][q] - factor * cols[m][r]
            here = (row_at == r) & (lane >= base + r)
            out = jnp.where(here, rows[r] * (root * scale), out)
            for m in range(1, len(cols)):
                left[kb + m] = left[kb + m] - cols[m][r] * (rows[r] * inverse)
        root_ref[base : base + 8, :] = out


def reduce_kernel(part_ref, sq_hbm, recv, root_out, buf, root, send_a, recv_a, send_b, recv_b, own_sem):
    a = lax.axis_index("tgt")
    b = lax.axis_index("src")
    barrier = pltpu.get_barrier_semaphore()

    def greet(k, carry):
        pl.semaphore_signal(barrier, 1, device_id=(a, lax.rem(b + k, NS)), device_id_type=MESH)
        return carry

    lax.fori_loop(1, NS, greet, 0)
    sq_copy = pltpu.make_async_copy(sq_hbm, buf.at[b], own_sem.at[0])
    own_copy = pltpu.make_async_copy(part_ref.at[b], recv.at[b], own_sem.at[1])
    sq_copy.start()
    own_copy.start()
    sq_copy.wait()
    pl.semaphore_wait(barrier, NS - 1)

    def square_copy(k):
        return pltpu.make_async_remote_copy(
            src_ref=buf.at[b],
            dst_ref=buf.at[b],
            send_sem=send_b.at[k],
            recv_sem=recv_b.at[b],
            device_id=(a, lax.rem(b + k, NS)),
            device_id_type=MESH,
        )

    def part_copy(k):
        at = lax.rem(b + k, NS)
        return pltpu.make_async_remote_copy(
            src_ref=part_ref.at[at],
            dst_ref=recv.at[b],
            send_sem=send_a.at[k],
            recv_sem=recv_a.at[b],
            device_id=(a, at),
            device_id_type=MESH,
        )

    def start(copy):
        def step(k, carry):
            copy(k).start()
            return carry

        lax.fori_loop(1, NS, step, 0)

    start(square_copy)
    start(part_copy)
    planes = basis_by_plane()

    def square_wait(k, carry):
        slot = lax.rem(b + k, NS)
        pltpu.make_async_remote_copy(
            src_ref=buf.at[b],
            dst_ref=buf.at[slot],
            send_sem=send_b.at[0],
            recv_sem=recv_b.at[slot],
            device_id=(a, b),
            device_id_type=MESH,
        ).wait_recv()
        square_copy(k).wait_send()
        return carry

    lax.fori_loop(1, NS, square_wait, 0)
    square = buf[0]
    for k in range(1, NS):
        square = square + buf[k]
    basis = jnp.concatenate(planes, axis=1)
    scaled = jnp.concatenate([planes[k] * square[k : k + 1, :] for k in range(8)], axis=1)
    gram = lax.dot_general(
        scaled, basis, NT_DIMS, precision=lax.Precision.HIGHEST, preferred_element_type=F32
    )
    cholesky(gram, root)
    root_copy = pltpu.make_async_copy(root, root_out, own_sem.at[2])
    root_copy.start()

    def part_wait(k, carry):
        slot = lax.rem(b + k, NS)
        pltpu.make_async_remote_copy(
            src_ref=part_ref.at[0],
            dst_ref=recv.at[slot],
            send_sem=send_a.at[0],
            recv_sem=recv_a.at[slot],
            device_id=(a, b),
            device_id_type=MESH,
        ).wait_recv()
        part_copy(k).wait_send()
        return carry

    own_copy.wait()
    lax.fori_loop(1, NS, part_wait, 0)
    root_copy.wait()


def reduce_part(part, square):
    hbm = pl.BlockSpec(memory_space=pltpu.HBM)
    return pl.pallas_call(
        reduce_kernel,
        out_shape=(
            jax.ShapeDtypeStruct((NS, SCEN, LEAF), F32),
            jax.ShapeDtypeStruct((NODES, NODES), F32),
        ),
        in_specs=[hbm] * 2,
        out_specs=(hbm,) * 2,
        scratch_shapes=[
            pltpu.VMEM((NS, 8, 128), F32),
            pltpu.VMEM((NODES, NODES), F32),
            pltpu.SemaphoreType.DMA((NS,)),
            pltpu.SemaphoreType.DMA((NS,)),
            pltpu.SemaphoreType.DMA((NS,)),
            pltpu.SemaphoreType.DMA((NS,)),
            pltpu.SemaphoreType.DMA((3,)),
        ],
        compiler_params=pltpu.CompilerParams(
            collective_id=1, has_side_effects=True, vmem_limit_bytes=VMEM
        ),
        name="reduce_part",
    )(part, square)


def finish_kernel(recv, root, order_ref, w_ref, pot_ref, root_ref):
    b = lax.axis_index("src")
    total = recv[0]
    for k in range(1, NS):
        total = total + recv[k]
    blocks = [total[:, k * 128 : (k + 1) * 128] for k in range(8)]
    weights = w_ref[pl.ds(pl.multiple_of(b * 8, 8), 8), :]
    for c in range(8):
        index = jnp.broadcast_to(order_ref[0:1, c * 128 : (c + 1) * 128], (8, 128))
        value = permute_row(blocks, index) * weights[c : c + 1, :]
        pot_ref[:, c * 128 : (c + 1) * 128] = value.astype(BF16)
    root_ref[...] = root[...]


def finish(recv, root, order, weights):
    vmem = pl.BlockSpec(memory_space=pltpu.VMEM)
    return pl.pallas_call(
        finish_kernel,
        out_shape=(
            jax.ShapeDtypeStruct((SCEN, LEAF), BF16),
            jax.ShapeDtypeStruct((NODES, NODES), F32),
        ),
        in_specs=[vmem] * 4,
        out_specs=(vmem, vmem),
        compiler_params=pltpu.CompilerParams(vmem_limit_bytes=VMEM),
        name="finish",
    )(recv, root, order, weights)


def shards(charges, weights, cell_order, leaf_coords, near_src):
    weights = weights.reshape(TL * 8, 128)
    inverse, square, table, phi = exchange(leaf_coords, cell_order, weights)
    part = local_part(leaf_coords, charges, inverse, table, phi)
    recv, root = reduce_part(part, square)
    return tuple(finish(recv, root, cell_order, weights))


def solution(mesh):
    placed = (P(None, "src"), P("tgt"), P(("tgt", "src"), None), P(), P("tgt", None))
    return jax.shard_map(
        shards,
        mesh=mesh,
        in_specs=placed,
        out_specs=(P(None, ("tgt", "src")), P()),
        check_vma=False,
    )
```

```python
import math

import jax
import jax.numpy as jnp
import numpy as np
from jax import lax
from jax.experimental import pallas as pl
from jax.experimental.pallas import tpu as pltpu
from jax.sharding import PartitionSpec as P

EDGE = 8
LEAF = 1024
SCEN = 8
LV = 128
NT = 16
NS = 8
TL = LV // NT
SL = LV // NS
NODES = 64
CELLS = LV * LEAF
VMEM = 60 << 20
MESH = pl.DeviceIdType.MESH
F32 = jnp.float32
BF16 = jnp.bfloat16
NT_DIMS = (((1,), (1,)), ((), ()))


def chebyshev_nodes(extent):
    return [
        extent * 0.5 + extent * 0.5 * math.cos((2.0 * a + 1.0) * (math.pi / 8.0)) for a in range(4)
    ]


def lagrange(points, nodes, a):
    factor = 1.0
    for b in range(4):
        if b != a:
            factor = factor * ((points - nodes[b]) * (1.0 / (nodes[a] - nodes[b])))
    return factor


def select_by(index, values):
    out = values[0]
    for k in range(1, len(values)):
        out = jnp.where(index == k, values[k], out)
    return out


def basis_by_plane():
    row = lax.broadcasted_iota(jnp.int32, (16, 128), 0)
    lane = lax.broadcasted_iota(jnp.int32, (16, 128), 1)
    short, tall = chebyshev_nodes(8.0), chebyshev_nodes(16.0)
    y = lax.shift_right_logical(lane, 4).astype(F32) + 0.5
    z = jnp.bitwise_and(lane, 15).astype(F32) + 0.5
    along_y = select_by(lax.shift_right_logical(row, 2), [lagrange(y, short, k) for k in range(4)])
    along_z = select_by(jnp.bitwise_and(row, 3), [lagrange(z, tall, k) for k in range(4)])
    plane = along_y * along_z
    return [
        jnp.concatenate([plane * float(lagrange(x + 0.5, short, a)) for a in range(4)], axis=0)
        for x in range(8)
    ]


def node_offset(index):
    short, tall = chebyshev_nodes(8.0), chebyshev_nodes(16.0)
    return [
        select_by(lax.shift_right_logical(index, 4), short),
        select_by(jnp.bitwise_and(lax.shift_right_logical(index, 2), 3), short),
        select_by(jnp.bitwise_and(index, 3), tall),
    ]


def split_two(value):
    high = value.astype(BF16)
    return high, (value - high.astype(F32)).astype(BF16)


def near_tables(table, table_out, sems):
    row = lax.broadcasted_iota(jnp.int32, (128, 128), 0)
    lane = lax.broadcasted_iota(jnp.int32, (128, 128), 1)
    step_y = lax.shift_right_logical(lane, 4) - lax.shift_right_logical(row, 4)
    step_z = jnp.bitwise_and(lane, 15) - jnp.bitwise_and(row, 15)

    def one(o, carry):
        dy = step_y - 8 * (lax.div(o, 3) - 1)
        dz = step_z - 16 * (lax.rem(o, 3) - 1)
        base = (dy * dy + dz * dz).astype(F32)
        for delta in range(16):
            value = 0.05 * lax.rsqrt(base + float(delta * delta + 1))
            table[o, :, delta * 128 : (delta + 1) * 128] = value.astype(BF16)
        pltpu.make_async_copy(table.at[o], table_out.at[o], sems.at[o]).start()
        return carry

    lax.fori_loop(0, 9, one, 0)


def far_tables(coords, i, j, phi, phi_out, sem):
    lane = lax.broadcasted_iota(jnp.int32, (1, TL * NODES), 1)
    slot = lax.shift_right_logical(lane, 6)
    spacing = (8.0, 8.0, 16.0)
    box_at = [select_by(slot, [coords[d, i * TL + t] for t in range(TL)]) for d in range(3)]
    offset = node_offset(jnp.bitwise_and(lane, 63))
    node_at = [box_at[d].astype(F32) * spacing[d] + offset[d] for d in range(3)]
    source = node_offset(lax.broadcasted_iota(jnp.int32, (NODES, TL * NODES), 0))

    def one(s, carry):
        distance = 1.0
        close = None
        for d in range(3):
            box = coords[d, j * SL + s]
            inside = jnp.abs(box_at[d] - box) <= 1
            close = inside if close is None else close & inside
            between = (node_at[d] - box.astype(F32) * spacing[d]) - source[d]
            distance = distance + between * between
        high, low = split_two(jnp.where(close, 0.0, 0.05) * lax.rsqrt(distance))
        phi[0, s] = high
        phi[1, s] = low
        return carry

    lax.fori_loop(0, SL, one, 0)
    pltpu.make_async_copy(phi, phi_out, sem).start()


def pair_lists(coords, i, j):
    lane = lax.broadcasted_iota(jnp.int32, (1, 128), 1)
    t, s = lax.shift_right_logical(lane, 4), jnp.bitwise_and(lane, 15)
    step = [
        select_by(s, [coords[d, j * SL + k] for k in range(SL)])
        - select_by(t, [coords[d, i * TL + k] for k in range(TL)])
        for d in range(3)
    ]
    close = (jnp.abs(step[0]) <= 1) & (jnp.abs(step[1]) <= 1) & (jnp.abs(step[2]) <= 1)
    row = lax.broadcasted_iota(jnp.int32, (8, 128), 0)
    member = jnp.where(jnp.broadcast_to(jnp.where(close, step[0] + 1, 9), (8, 128)) == row, 1.0, 0.0)
    ahead = lax.broadcasted_iota(jnp.int32, (128, 128), 0) < lax.broadcasted_iota(jnp.int32, (128, 128), 1)
    rank = jnp.dot(
        member.astype(BF16), jnp.where(ahead, 1.0, 0.0).astype(BF16), preferred_element_type=F32
    )
    place = jnp.full((1, 128), 511.0, F32)
    for v in range(3):
        place = jnp.where(member[v : v + 1, :] > 0.5, rank[v : v + 1, :] + float(136 * v), place)
    position = lax.broadcasted_iota(jnp.int32, (512, 128), 0)
    spread = jnp.where(jnp.broadcast_to(place.astype(jnp.int32), (512, 128)) == position, 1.0, 0.0)
    parts = [t + 8 * s, (step[1] + 1) * 3 + step[2] + 1, jnp.full((1, 128), 1, jnp.int32)]
    left = select_by(row, [jnp.broadcast_to(part, (8, 128)) for part in parts]).astype(F32)
    listed = lax.dot_general(
        left.astype(BF16), spread.astype(BF16), NT_DIMS, preferred_element_type=F32
    ).astype(jnp.int32)
    out = jnp.where(listed[2:3, :] > 0, listed[0:1, :] + 256 * listed[1:2, :], 8 * SL)
    at = lax.broadcasted_iota(jnp.int32, (1, 512), 1)
    for v in range(3):
        length = jnp.sum(member[v : v + 1, :], axis=1, keepdims=True).astype(jnp.int32)
        out = jnp.where(at == 408 + v, length, out)
    return out


def exchange_kernel(
    coords_hbm, order_hbm, w_hbm, block_ref, table_out, phi_out, list_out,
    coords, order_ref, w_ref, mine, table, phi, lists,
    send_a, recv_a, table_sem, phi_sem, in_sem, own_sem, list_sem,
):
    a = lax.axis_index("tgt")
    b = lax.axis_index("src")
    barrier = pltpu.get_barrier_semaphore()
    home = lax.rem(a, 2) * NS + b
    column = lax.div(a, 2)
    loops_back = b == column

    def signal_sender(k, carry):
        at = lax.rem(home + k, NT)
        pl.semaphore_signal(
            barrier, 1, device_id=(2 * b + lax.div(at, NS), lax.rem(at, NS)), device_id_type=MESH
        )
        return carry

    @pl.when(jnp.logical_not(loops_back))
    def _():
        signal_sender(0, 0)

    lax.fori_loop(1, NT, signal_sender, 0)
    fetches = [
        pltpu.make_async_copy(order_hbm, order_ref, in_sem.at[0]),
        pltpu.make_async_copy(w_hbm.at[pl.ds(pl.multiple_of(b * 8, 8), 8)], w_ref, in_sem.at[1]),
        pltpu.make_async_copy(coords_hbm, coords, in_sem.at[2]),
    ]
    for fetch in fetches:
        fetch.start()
    for fetch in fetches:
        fetch.wait()

    rows = lax.broadcasted_iota(jnp.int32, (8, 128), 0)
    lanes = lax.broadcasted_iota(jnp.int32, (8, 128), 1)
    low_rows = lax.broadcasted_iota(jnp.int32, (128, 128), 0)
    square = w_ref[...] * w_ref[...]
    placed = jnp.zeros((40, 128), F32)
    for c in range(8):
        order = order_ref[0:1, c * 128 : (c + 1) * 128]
        hit = lax.shift_right_logical(jnp.broadcast_to(order, (8, 128)), 7) == rows
        value = jnp.broadcast_to(square[c : c + 1, :], (8, 128))
        first = value.astype(BF16).astype(F32)
        rest = value - first
        second = rest.astype(BF16).astype(F32)
        third = rest - second
        parts = [jnp.full((8, 128), float(c), F32), lanes.astype(F32), first, second, third]
        left = jnp.concatenate([jnp.where(hit, part, 0.0) for part in parts], axis=0)
        low = jnp.broadcast_to(jnp.bitwise_and(order, 127), (128, 128)) == low_rows
        right = jnp.where(low, 1.0, 0.0).astype(BF16)
        placed = placed + lax.dot_general(
            left.astype(BF16), right, NT_DIMS, preferred_element_type=F32
        )
    mine[0:8, :] = placed[0:8] * 128.0 + placed[8:16]
    mine[8:16, :] = placed[16:24] + placed[24:32] + placed[32:40]

    pl.semaphore_wait(barrier, jnp.where(loops_back, NT - 1, NT).astype(jnp.int32))

    def block_copy(k):
        return pltpu.make_async_remote_copy(
            src_ref=mine,
            dst_ref=block_ref.at[home],
            send_sem=send_a.at[k],
            recv_sem=recv_a.at[home],
            device_id=(lax.rem(a + k, NT), column),
            device_id_type=MESH,
        )

    def start_block(k, carry):
        block_copy(k).start()
        return carry

    lax.fori_loop(1, NT, start_block, 0)

    @pl.when(jnp.logical_not(loops_back))
    def _():
        block_copy(0).start()

    own_copy = pltpu.make_async_copy(mine, block_ref.at[home], own_sem)

    @pl.when(loops_back)
    def _():
        own_copy.start()

    lists[...] = pair_lists(coords, a, b)
    list_copy = pltpu.make_async_copy(lists, list_out, list_sem)
    list_copy.start()
    far_tables(coords, a, b, phi, phi_out, phi_sem)
    near_tables(table, table_out, table_sem)
    list_copy.wait()
    pltpu.make_async_copy(phi, phi_out, phi_sem).wait()
    for o in range(9):
        pltpu.make_async_copy(table.at[o], table_out.at[o], table_sem.at[o]).wait()

    def block_arrival(slot):
        pltpu.make_async_remote_copy(
            src_ref=mine,
            dst_ref=block_ref.at[slot],
            send_sem=send_a.at[0],
            recv_sem=recv_a.at[slot],
            device_id=(a, b),
            device_id_type=MESH,
        ).wait_recv()

    @pl.when(jnp.logical_not(loops_back))
    def _():
        block_arrival(home)
        block_copy(0).wait_send()

    @pl.when(loops_back)
    def _():
        own_copy.wait()

    def wait_block(k, carry):
        block_arrival(lax.rem(home + k, NT))
        block_copy(k).wait_send()
        return carry

    lax.fori_loop(1, NT, wait_block, 0)


def exchange(coords, order, weights):
    hbm = pl.BlockSpec(memory_space=pltpu.HBM)
    return pl.pallas_call(
        exchange_kernel,
        out_shape=(
            jax.ShapeDtypeStruct((SL, 16, 128), F32),
            jax.ShapeDtypeStruct((9, 128, 2048), BF16),
            jax.ShapeDtypeStruct((2, SL, NODES, TL * NODES), BF16),
            jax.ShapeDtypeStruct((1, 512), jnp.int32),
        ),
        in_specs=[hbm] * 3,
        out_specs=(hbm,) * 4,
        scratch_shapes=[
            pltpu.SMEM((3, LV), jnp.int32),
            pltpu.VMEM((1, LEAF), jnp.int32),
            pltpu.VMEM((8, 128), F32),
            pltpu.VMEM((16, 128), F32),
            pltpu.VMEM((9, 128, 2048), BF16),
            pltpu.VMEM((2, SL, NODES, TL * NODES), BF16),
            pltpu.VMEM((1, 512), jnp.int32),
            pltpu.SemaphoreType.DMA((NT,)),
            pltpu.SemaphoreType.DMA((NT,)),
            pltpu.SemaphoreType.DMA((9,)),
            pltpu.SemaphoreType.DMA,
            pltpu.SemaphoreType.DMA((3,)),
            pltpu.SemaphoreType.DMA,
            pltpu.SemaphoreType.DMA,
        ],
        compiler_params=pltpu.CompilerParams(
            collective_id=0, has_side_effects=True, vmem_limit_bytes=VMEM
        ),
        name="exchange",
    )(coords, order, weights)


def lane_gather(block, lane):
    return jnp.take_along_axis(block, lane, axis=1, mode="promise_in_bounds")


def permute_row(blocks, index):
    block = lax.shift_right_logical(index, 7)
    lane = jnp.bitwise_and(index, 127)
    out = lane_gather(blocks[0], lane)
    for k in range(1, 8):
        out = jnp.where(block == k, lane_gather(blocks[k], lane), out)
    return out


def local_kernel(
    charges_hbm, block_hbm, table_hbm, phi_hbm, list_hbm, out, sq_out,
    charges, block, table, phi, qf, qb, pairs, sems,
):
    fetches = [
        pltpu.make_async_copy(source, target, sems.at[k])
        for k, (source, target) in enumerate(
            [(charges_hbm, charges), (block_hbm, block), (phi_hbm, phi), (table_hbm, table), (list_hbm, pairs)]
        )
    ]
    for fetch in fetches:
        fetch.start()
    qb[SL] = jnp.zeros((64, 128), BF16)

    fetches[0].wait()
    fetches[1].wait()

    def canonical(leaf, carry):
        base = pl.multiple_of(leaf * LEAF, LEAF)
        raw = charges[:, pl.ds(base, LEAF)].astype(F32)
        blocks = [raw[:, k * 128 : (k + 1) * 128] for k in range(8)]
        order = block[leaf, 0:8, :].astype(jnp.int32)
        pieces = [
            permute_row(blocks, jnp.broadcast_to(order[x : x + 1, :], (8, 128))) for x in range(8)
        ]
        rows = jnp.concatenate(pieces, axis=0)
        qf[leaf] = rows
        qb[leaf] = rows.astype(BF16)
        return carry

    lax.fori_loop(0, SL, canonical, 0, unroll=4)
    square = block[0, 8:16, :]
    for leaf in range(1, SL):
        square = square + block[leaf, 8:16, :]
    sq_out[...] = square

    basis = [split_two(plane) for plane in basis_by_plane()]
    moments = jnp.zeros((SL * SCEN, NODES), F32)
    for x in range(8):
        rows = qf[:, x * 8 : (x + 1) * 8, :].reshape(SL * SCEN, 128).astype(BF16)
        for part in basis[x]:
            moments = moments + lax.dot_general(rows, part, NT_DIMS, preferred_element_type=F32)

    fetches[2].wait()
    coeff = jnp.zeros((SCEN, TL * NODES), F32)
    for s in range(SL):
        high, low = phi[0, s], phi[1, s]
        part_high, part_low = split_two(moments[s * 8 : (s + 1) * 8, :])
        twice = jnp.concatenate([part_high.astype(F32), part_low.astype(F32)], axis=0).astype(BF16)
        product = jnp.dot(twice, high, preferred_element_type=F32)
        coeff = coeff + product[:8] + product[8:]
        coeff = coeff + jnp.dot(part_high, low, preferred_element_type=F32)

    stacked = jnp.concatenate(
        [coeff[:, t * NODES : (t + 1) * NODES] for t in range(TL)], axis=0
    )
    stacked_high, stacked_low = split_two(stacked)
    left = jnp.concatenate([stacked_high, stacked_low, stacked_high], axis=1)
    right = jnp.concatenate(
        [jnp.concatenate([basis[x][k] for x in range(8)], axis=1) for k in (0, 0, 1)], axis=0
    )
    far = jnp.dot(left, right, preferred_element_type=F32)
    for t in range(TL):
        out[t] = far[t * 8 : (t + 1) * 8, :]

    fetches[3].wait()
    fetches[4].wait()

    def near_pairs(value):
        def contribution(code):
            s = jnp.bitwise_and(lax.shift_right_logical(code, 3), 31)
            which = lax.shift_right_logical(code, 8)
            left = qb[s]
            total = [None] * 8
            for chunk in range(4 if value == 1 else 8):
                product = jnp.dot(
                    left,
                    table[which, :, chunk * 256 : (chunk + 1) * 256],
                    preferred_element_type=F32,
                )
                for half in range(2):
                    delta = 2 * chunk + half
                    for sx in range(8):
                        piece = product[sx * 8 : (sx + 1) * 8, half * 128 : (half + 1) * 128]
                        if value == 1:
                            hits = {sx - delta, sx + delta}
                        elif value == 2:
                            hits = {8 + sx - delta}
                        else:
                            hits = {delta - 8 + sx}
                        for x in sorted(hits):
                            if 0 <= x < 8:
                                total[x] = piece if total[x] is None else total[x] + piece
            return total

        def two(n, carry):
            codes = [pairs[0, 136 * value + 2 * n + k] for k in range(2)]
            totals = [contribution(code) for code in codes]
            for code, total in zip(codes, totals):
                t = jnp.bitwise_and(code, 7)
                for x in range(8):
                    out[t, :, x * 128 : (x + 1) * 128] += total[x]
            return carry

        lax.fori_loop(0, lax.shift_right_logical(pairs[0, 408 + value] + 1, 1), two, 0)

    for value in range(3):
        near_pairs(value)


def local_part(charges, block, table, phi, lists):
    hbm = pl.BlockSpec(memory_space=pltpu.HBM)
    vmem = pl.BlockSpec(memory_space=pltpu.VMEM)
    return pl.pallas_call(
        local_kernel,
        out_shape=(
            jax.ShapeDtypeStruct((TL, SCEN, LEAF), F32),
            jax.ShapeDtypeStruct((8, 128), F32),
        ),
        in_specs=[hbm] * 5,
        out_specs=(vmem, vmem),
        scratch_shapes=[
            pltpu.VMEM((SCEN, SL * LEAF), BF16),
            pltpu.VMEM((SL, 16, 128), F32),
            pltpu.VMEM((9, 128, 2048), BF16),
            pltpu.VMEM((2, SL, NODES, TL * NODES), BF16),
            pltpu.VMEM((SL, 64, 128), F32),
            pltpu.VMEM((SL + 1, 64, 128), BF16),
            pltpu.SMEM((1, 512), jnp.int32),
            pltpu.SemaphoreType.DMA((5,)),
        ],
        compiler_params=pltpu.CompilerParams(vmem_limit_bytes=VMEM),
        name="local_part",
    )(charges, block, table, phi, lists)


def cholesky(gram, root_ref):
    full = (8, NODES)
    lane = lax.broadcasted_iota(jnp.int32, full, 1)
    row_at = lax.broadcasted_iota(jnp.int32, full, 0)
    left = [gram[8 * k : 8 * k + 8, :] for k in range(8)]
    scale = 1.0 / math.sqrt(CELLS)
    for kb in range(8):
        base = 8 * kb
        rows = [jnp.broadcast_to(left[kb][r : r + 1, :], full) for r in range(8)]
        cols = [
            [jnp.broadcast_to(left[m][:, base + q : base + q + 1], full) for q in range(8)]
            for m in range(kb, 8)
        ]
        splat = [
            [jnp.broadcast_to(cols[0][q][r : r + 1, :], full) if q >= r else None for q in range(8)]
            for r in range(8)
        ]
        out = jnp.zeros(full, F32)
        for r in range(8):
            root = lax.rsqrt(splat[r][r])
            inverse = root * root
            for q in range(r + 1, 8):
                factor = splat[r][q] * inverse
                for p in range(q, 8):
                    splat[q][p] = splat[q][p] - factor * splat[r][p]
                rows[q] = rows[q] - factor * rows[r]
                for m in range(1, len(cols)):
                    cols[m][q] = cols[m][q] - factor * cols[m][r]
            here = (row_at == r) & (lane >= base + r)
            out = jnp.where(here, rows[r] * (root * scale), out)
            for m in range(1, len(cols)):
                left[kb + m] = left[kb + m] - cols[m][r] * (rows[r] * inverse)
        root_ref[base : base + 8, :] = out


def reduce_kernel(part_ref, sq_hbm, recv, root_out, buf, root, send_a, recv_a, send_b, recv_b, own_sem):
    a = lax.axis_index("tgt")
    b = lax.axis_index("src")
    barrier = pltpu.get_barrier_semaphore()

    def greet(k, carry):
        pl.semaphore_signal(barrier, 1, device_id=(a, lax.rem(b + k, NS)), device_id_type=MESH)
        return carry

    lax.fori_loop(1, NS, greet, 0)
    sq_copy = pltpu.make_async_copy(sq_hbm, buf.at[b], own_sem.at[0])
    own_copy = pltpu.make_async_copy(part_ref.at[b], recv.at[b], own_sem.at[1])
    sq_copy.start()
    own_copy.start()
    sq_copy.wait()
    pl.semaphore_wait(barrier, NS - 1)

    def square_copy(k):
        return pltpu.make_async_remote_copy(
            src_ref=buf.at[b],
            dst_ref=buf.at[b],
            send_sem=send_b.at[k],
            recv_sem=recv_b.at[b],
            device_id=(a, lax.rem(b + k, NS)),
            device_id_type=MESH,
        )

    def part_copy(k):
        at = lax.rem(b + k, NS)
        return pltpu.make_async_remote_copy(
            src_ref=part_ref.at[at],
            dst_ref=recv.at[b],
            send_sem=send_a.at[k],
            recv_sem=recv_a.at[b],
            device_id=(a, at),
            device_id_type=MESH,
        )

    def start(copy):
        def step(k, carry):
            copy(k).start()
            return carry

        lax.fori_loop(1, NS, step, 0)

    start(square_copy)
    start(part_copy)
    planes = basis_by_plane()

    def square_wait(k, carry):
        slot = lax.rem(b + k, NS)
        pltpu.make_async_remote_copy(
            src_ref=buf.at[b],
            dst_ref=buf.at[slot],
            send_sem=send_b.at[0],
            recv_sem=recv_b.at[slot],
            device_id=(a, b),
            device_id_type=MESH,
        ).wait_recv()
        square_copy(k).wait_send()
        return carry

    lax.fori_loop(1, NS, square_wait, 0)
    square = buf[0]
    for k in range(1, NS):
        square = square + buf[k]
    basis = jnp.concatenate(planes, axis=1)
    scaled = jnp.concatenate([planes[k] * square[k : k + 1, :] for k in range(8)], axis=1)
    gram = lax.dot_general(
        scaled, basis, NT_DIMS, precision=lax.Precision.HIGHEST, preferred_element_type=F32
    )
    cholesky(gram, root)
    root_copy = pltpu.make_async_copy(root, root_out, own_sem.at[2])
    root_copy.start()

    def part_wait(k, carry):
        slot = lax.rem(b + k, NS)
        pltpu.make_async_remote_copy(
            src_ref=part_ref.at[0],
            dst_ref=recv.at[slot],
            send_sem=send_a.at[0],
            recv_sem=recv_a.at[slot],
            device_id=(a, b),
            device_id_type=MESH,
        ).wait_recv()
        part_copy(k).wait_send()
        return carry

    own_copy.wait()
    lax.fori_loop(1, NS, part_wait, 0)
    root_copy.wait()


def reduce_part(part, square):
    hbm = pl.BlockSpec(memory_space=pltpu.HBM)
    return pl.pallas_call(
        reduce_kernel,
        out_shape=(
            jax.ShapeDtypeStruct((NS, SCEN, LEAF), F32),
            jax.ShapeDtypeStruct((NODES, NODES), F32),
        ),
        in_specs=[hbm] * 2,
        out_specs=(hbm,) * 2,
        scratch_shapes=[
            pltpu.VMEM((NS, 8, 128), F32),
            pltpu.VMEM((NODES, NODES), F32),
            pltpu.SemaphoreType.DMA((NS,)),
            pltpu.SemaphoreType.DMA((NS,)),
            pltpu.SemaphoreType.DMA((NS,)),
            pltpu.SemaphoreType.DMA((NS,)),
            pltpu.SemaphoreType.DMA((3,)),
        ],
        compiler_params=pltpu.CompilerParams(
            collective_id=1, has_side_effects=True, vmem_limit_bytes=VMEM
        ),
        name="reduce_part",
    )(part, square)


def finish_kernel(recv, root, order_ref, w_ref, pot_ref, root_ref):
    b = lax.axis_index("src")
    total = recv[0]
    for k in range(1, NS):
        total = total + recv[k]
    blocks = [total[:, k * 128 : (k + 1) * 128] for k in range(8)]
    weights = w_ref[pl.ds(pl.multiple_of(b * 8, 8), 8), :]
    for c in range(8):
        index = jnp.broadcast_to(order_ref[0:1, c * 128 : (c + 1) * 128], (8, 128))
        value = permute_row(blocks, index) * weights[c : c + 1, :]
        pot_ref[:, c * 128 : (c + 1) * 128] = value.astype(BF16)
    root_ref[...] = root[...]


def finish(recv, root, order, weights):
    vmem = pl.BlockSpec(memory_space=pltpu.VMEM)
    return pl.pallas_call(
        finish_kernel,
        out_shape=(
            jax.ShapeDtypeStruct((SCEN, LEAF), BF16),
            jax.ShapeDtypeStruct((NODES, NODES), F32),
        ),
        in_specs=[vmem] * 4,
        out_specs=(vmem, vmem),
        compiler_params=pltpu.CompilerParams(vmem_limit_bytes=VMEM),
        name="finish",
    )(recv, root, order, weights)


def shards(charges, weights, cell_order, leaf_coords, near_src):
    weights = weights.reshape(TL * 8, 128)
    block, table, phi, lists = exchange(leaf_coords, cell_order, weights)
    part, square = local_part(charges, block, table, phi, lists)
    recv, root = reduce_part(part, square)
    return tuple(finish(recv, root, cell_order, weights))


def solution(mesh):
    placed = (P(None, "src"), P("tgt"), P(("tgt", "src"), None), P(), P("tgt", None))
    return jax.shard_map(
        shards,
        mesh=mesh,
        in_specs=placed,
        out_specs=(P(None, ("tgt", "src")), P()),
        check_vma=False,
    )
```

```python
import math

import jax
import jax.numpy as jnp
import numpy as np
from jax import lax
from jax.experimental import pallas as pl
from jax.experimental.pallas import tpu as pltpu
from jax.sharding import PartitionSpec as P

EDGE = 8
LEAF = 1024
SCEN = 8
LV = 128
NT = 16
NS = 8
TL = LV // NT
SL = LV // NS
NODES = 64
CELLS = LV * LEAF
VMEM = 60 << 20
MESH = pl.DeviceIdType.MESH
F32 = jnp.float32
BF16 = jnp.bfloat16
NT_DIMS = (((1,), (1,)), ((), ()))


def chebyshev_nodes(extent):
    return [
        extent * 0.5 + extent * 0.5 * math.cos((2.0 * a + 1.0) * (math.pi / 8.0)) for a in range(4)
    ]


def lagrange(points, nodes, a):
    factor = 1.0
    for b in range(4):
        if b != a:
            factor = factor * ((points - nodes[b]) * (1.0 / (nodes[a] - nodes[b])))
    return factor


def select_by(index, values):
    out = values[0]
    for k in range(1, len(values)):
        out = jnp.where(index == k, values[k], out)
    return out


def basis_by_plane():
    row = lax.broadcasted_iota(jnp.int32, (16, 128), 0)
    lane = lax.broadcasted_iota(jnp.int32, (16, 128), 1)
    short, tall = chebyshev_nodes(8.0), chebyshev_nodes(16.0)
    y = lax.shift_right_logical(lane, 4).astype(F32) + 0.5
    z = jnp.bitwise_and(lane, 15).astype(F32) + 0.5
    along_y = select_by(lax.shift_right_logical(row, 2), [lagrange(y, short, k) for k in range(4)])
    along_z = select_by(jnp.bitwise_and(row, 3), [lagrange(z, tall, k) for k in range(4)])
    plane = along_y * along_z
    return [
        jnp.concatenate([plane * float(lagrange(x + 0.5, short, a)) for a in range(4)], axis=0)
        for x in range(8)
    ]


def node_offset(index):
    short, tall = chebyshev_nodes(8.0), chebyshev_nodes(16.0)
    return [
        select_by(lax.shift_right_logical(index, 4), short),
        select_by(jnp.bitwise_and(lax.shift_right_logical(index, 2), 3), short),
        select_by(jnp.bitwise_and(index, 3), tall),
    ]


def split_two(value):
    high = value.astype(BF16)
    return high, (value - high.astype(F32)).astype(BF16)


def near_tables(table, table_out, sems):
    row = lax.broadcasted_iota(jnp.int32, (128, 128), 0)
    lane = lax.broadcasted_iota(jnp.int32, (128, 128), 1)
    step_y = lax.shift_right_logical(lane, 4) - lax.shift_right_logical(row, 4)
    step_z = jnp.bitwise_and(lane, 15) - jnp.bitwise_and(row, 15)

    def one(o, carry):
        dy = step_y - 8 * (lax.div(o, 3) - 1)
        dz = step_z - 16 * (lax.rem(o, 3) - 1)
        base = (dy * dy + dz * dz).astype(F32)
        for delta in range(16):
            value = 0.05 * lax.rsqrt(base + float(delta * delta + 1))
            table[o, :, delta * 128 : (delta + 1) * 128] = value.astype(BF16)
        pltpu.make_async_copy(table.at[o], table_out.at[o], sems.at[o]).start()
        return carry

    lax.fori_loop(0, 9, one, 0)


def far_tables(coords, i, j, phi, phi_out, sem):
    lane = lax.broadcasted_iota(jnp.int32, (1, TL * NODES), 1)
    slot = lax.shift_right_logical(lane, 6)
    spacing = (8.0, 8.0, 16.0)
    box_at = [select_by(slot, [coords[d, i * TL + t] for t in range(TL)]) for d in range(3)]
    offset = node_offset(jnp.bitwise_and(lane, 63))
    node_at = [box_at[d].astype(F32) * spacing[d] + offset[d] for d in range(3)]
    source = node_offset(lax.broadcasted_iota(jnp.int32, (NODES, TL * NODES), 0))

    def one(s, carry):
        distance = 1.0
        close = None
        for d in range(3):
            box = coords[d, j * SL + s]
            inside = jnp.abs(box_at[d] - box) <= 1
            close = inside if close is None else close & inside
            between = (node_at[d] - box.astype(F32) * spacing[d]) - source[d]
            distance = distance + between * between
        high, low = split_two(jnp.where(close, 0.0, 0.05) * lax.rsqrt(distance))
        phi[0, s] = high
        phi[1, s] = low
        return carry

    lax.fori_loop(0, SL, one, 0)
    pltpu.make_async_copy(phi, phi_out, sem).start()


def pair_lists(coords, i, j):
    lane = lax.broadcasted_iota(jnp.int32, (1, 128), 1)
    t, s = lax.shift_right_logical(lane, 4), jnp.bitwise_and(lane, 15)
    step = [
        select_by(s, [coords[d, j * SL + k] for k in range(SL)])
        - select_by(t, [coords[d, i * TL + k] for k in range(TL)])
        for d in range(3)
    ]
    close = (jnp.abs(step[0]) <= 1) & (jnp.abs(step[1]) <= 1) & (jnp.abs(step[2]) <= 1)
    row = lax.broadcasted_iota(jnp.int32, (8, 128), 0)
    member = jnp.where(jnp.broadcast_to(jnp.where(close, jnp.where(step[0] == 0, 1, 0), 9), (8, 128)) == row, 1.0, 0.0)
    ahead = lax.broadcasted_iota(jnp.int32, (128, 128), 0) < lax.broadcasted_iota(jnp.int32, (128, 128), 1)
    rank = jnp.dot(
        member.astype(BF16), jnp.where(ahead, 1.0, 0.0).astype(BF16), preferred_element_type=F32
    )
    place = jnp.full((1, 128), 511.0, F32)
    for v in range(2):
        place = jnp.where(member[v : v + 1, :] > 0.5, rank[v : v + 1, :] + float(136 * v), place)
    position = lax.broadcasted_iota(jnp.int32, (512, 128), 0)
    spread = jnp.where(jnp.broadcast_to(place.astype(jnp.int32), (512, 128)) == position, 1.0, 0.0)
    parts = [t + 8 * s, (step[1] + 1) * 3 + step[2] + 1, jnp.full((1, 128), 1, jnp.int32), jnp.where(step[0] < 0, 1, 0)]
    left = select_by(row, [jnp.broadcast_to(part, (8, 128)) for part in parts]).astype(F32)
    listed = lax.dot_general(
        left.astype(BF16), spread.astype(BF16), NT_DIMS, preferred_element_type=F32
    ).astype(jnp.int32)
    out = jnp.where(listed[2:3, :] > 0, listed[0:1, :] + 256 * listed[1:2, :] + 4096 * listed[3:4, :], 8 * SL)
    at = lax.broadcasted_iota(jnp.int32, (1, 512), 1)
    for v in range(2):
        length = jnp.sum(member[v : v + 1, :], axis=1, keepdims=True).astype(jnp.int32)
        out = jnp.where(at == 408 + v, length, out)
    return out


def exchange_kernel(
    coords_hbm, order_hbm, w_hbm, block_ref, table_out, phi_out, list_out,
    coords, order_ref, w_ref, mine, table, phi, lists,
    send_a, recv_a, table_sem, phi_sem, in_sem, own_sem, list_sem,
):
    a = lax.axis_index("tgt")
    b = lax.axis_index("src")
    barrier = pltpu.get_barrier_semaphore()
    home = lax.rem(a, 2) * NS + b
    column = lax.div(a, 2)
    loops_back = b == column

    def signal_sender(k, carry):
        at = lax.rem(home + k, NT)
        pl.semaphore_signal(
            barrier, 1, device_id=(2 * b + lax.div(at, NS), lax.rem(at, NS)), device_id_type=MESH
        )
        return carry

    @pl.when(jnp.logical_not(loops_back))
    def _():
        signal_sender(0, 0)

    lax.fori_loop(1, NT, signal_sender, 0)
    fetches = [
        pltpu.make_async_copy(order_hbm, order_ref, in_sem.at[0]),
        pltpu.make_async_copy(w_hbm.at[pl.ds(pl.multiple_of(b * 8, 8), 8)], w_ref, in_sem.at[1]),
        pltpu.make_async_copy(coords_hbm, coords, in_sem.at[2]),
    ]
    for fetch in fetches:
        fetch.start()
    for fetch in fetches:
        fetch.wait()

    rows = lax.broadcasted_iota(jnp.int32, (8, 128), 0)
    lanes = lax.broadcasted_iota(jnp.int32, (8, 128), 1)
    low_rows = lax.broadcasted_iota(jnp.int32, (128, 128), 0)
    square = w_ref[...] * w_ref[...]
    placed = jnp.zeros((40, 128), F32)
    for c in range(8):
        order = order_ref[0:1, c * 128 : (c + 1) * 128]
        hit = lax.shift_right_logical(jnp.broadcast_to(order, (8, 128)), 7) == rows
        value = jnp.broadcast_to(square[c : c + 1, :], (8, 128))
        first = value.astype(BF16).astype(F32)
        rest = value - first
        second = rest.astype(BF16).astype(F32)
        third = rest - second
        parts = [jnp.full((8, 128), float(c), F32), lanes.astype(F32), first, second, third]
        left = jnp.concatenate([jnp.where(hit, part, 0.0) for part in parts], axis=0)
        low = jnp.broadcast_to(jnp.bitwise_and(order, 127), (128, 128)) == low_rows
        right = jnp.where(low, 1.0, 0.0).astype(BF16)
        placed = placed + lax.dot_general(
            left.astype(BF16), right, NT_DIMS, preferred_element_type=F32
        )
    mine[0:8, :] = placed[0:8] * 128.0 + placed[8:16]
    mine[8:16, :] = placed[16:24] + placed[24:32] + placed[32:40]

    pl.semaphore_wait(barrier, jnp.where(loops_back, NT - 1, NT).astype(jnp.int32))

    def block_copy(k):
        return pltpu.make_async_remote_copy(
            src_ref=mine,
            dst_ref=block_ref.at[home],
            send_sem=send_a.at[k],
            recv_sem=recv_a.at[home],
            device_id=(lax.rem(a + k, NT), column),
            device_id_type=MESH,
        )

    def start_block(k, carry):
        block_copy(k).start()
        return carry

    lax.fori_loop(1, NT, start_block, 0)

    @pl.when(jnp.logical_not(loops_back))
    def _():
        block_copy(0).start()

    own_copy = pltpu.make_async_copy(mine, block_ref.at[home], own_sem)

    @pl.when(loops_back)
    def _():
        own_copy.start()

    lists[...] = pair_lists(coords, a, b)
    list_copy = pltpu.make_async_copy(lists, list_out, list_sem)
    list_copy.start()
    far_tables(coords, a, b, phi, phi_out, phi_sem)
    near_tables(table, table_out, table_sem)
    list_copy.wait()
    pltpu.make_async_copy(phi, phi_out, phi_sem).wait()
    for o in range(9):
        pltpu.make_async_copy(table.at[o], table_out.at[o], table_sem.at[o]).wait()

    def block_arrival(slot):
        pltpu.make_async_remote_copy(
            src_ref=mine,
            dst_ref=block_ref.at[slot],
            send_sem=send_a.at[0],
            recv_sem=recv_a.at[slot],
            device_id=(a, b),
            device_id_type=MESH,
        ).wait_recv()

    @pl.when(jnp.logical_not(loops_back))
    def _():
        block_arrival(home)
        block_copy(0).wait_send()

    @pl.when(loops_back)
    def _():
        own_copy.wait()

    def wait_block(k, carry):
        block_arrival(lax.rem(home + k, NT))
        block_copy(k).wait_send()
        return carry

    lax.fori_loop(1, NT, wait_block, 0)


def exchange(coords, order, weights):
    hbm = pl.BlockSpec(memory_space=pltpu.HBM)
    return pl.pallas_call(
        exchange_kernel,
        out_shape=(
            jax.ShapeDtypeStruct((SL, 16, 128), F32),
            jax.ShapeDtypeStruct((9, 128, 2048), BF16),
            jax.ShapeDtypeStruct((2, SL, NODES, TL * NODES), BF16),
            jax.ShapeDtypeStruct((1, 512), jnp.int32),
        ),
        in_specs=[hbm] * 3,
        out_specs=(hbm,) * 4,
        scratch_shapes=[
            pltpu.SMEM((3, LV), jnp.int32),
            pltpu.VMEM((1, LEAF), jnp.int32),
            pltpu.VMEM((8, 128), F32),
            pltpu.VMEM((16, 128), F32),
            pltpu.VMEM((9, 128, 2048), BF16),
            pltpu.VMEM((2, SL, NODES, TL * NODES), BF16),
            pltpu.VMEM((1, 512), jnp.int32),
            pltpu.SemaphoreType.DMA((NT,)),
            pltpu.SemaphoreType.DMA((NT,)),
            pltpu.SemaphoreType.DMA((9,)),
            pltpu.SemaphoreType.DMA,
            pltpu.SemaphoreType.DMA((3,)),
            pltpu.SemaphoreType.DMA,
            pltpu.SemaphoreType.DMA,
        ],
        compiler_params=pltpu.CompilerParams(
            collective_id=0, has_side_effects=True, vmem_limit_bytes=VMEM
        ),
        name="exchange",
    )(coords, order, weights)


def lane_gather(block, lane):
    return jnp.take_along_axis(block, lane, axis=1, mode="promise_in_bounds")


def permute_row(blocks, index):
    block = lax.shift_right_logical(index, 7)
    lane = jnp.bitwise_and(index, 127)
    out = lane_gather(blocks[0], lane)
    for k in range(1, 8):
        out = jnp.where(block == k, lane_gather(blocks[k], lane), out)
    return out


def local_kernel(
    charges_hbm, block_hbm, table_hbm, list_hbm, out, moments_out, sq_out,
    charges, block, table, qf, qb, pairs, sems,
):
    fetches = [
        pltpu.make_async_copy(source, target, sems.at[k])
        for k, (source, target) in enumerate(
            [(charges_hbm, charges), (block_hbm, block), (table_hbm, table), (list_hbm, pairs)]
        )
    ]
    for fetch in fetches:
        fetch.start()
    qb[SL] = jnp.zeros((64, 128), BF16)
    out[...] = jnp.zeros((TL, 8, SCEN, 128), F32)

    fetches[0].wait()
    fetches[1].wait()

    def canonical(leaf, carry):
        base = pl.multiple_of(leaf * LEAF, LEAF)
        raw = charges[:, pl.ds(base, LEAF)].astype(F32)
        blocks = [raw[:, k * 128 : (k + 1) * 128] for k in range(8)]
        order = block[leaf, 0:8, :].astype(jnp.int32)
        pieces = [
            permute_row(blocks, jnp.broadcast_to(order[x : x + 1, :], (8, 128))) for x in range(8)
        ]
        rows = jnp.concatenate(pieces, axis=0)
        qf[leaf] = rows
        qb[leaf] = rows.astype(BF16)
        qb[SL + 1 + leaf] = jnp.concatenate(pieces[::-1], axis=0).astype(BF16)
        return carry

    lax.fori_loop(0, SL, canonical, 0, unroll=4)
    square = block[0, 8:16, :]
    for leaf in range(1, SL):
        square = square + block[leaf, 8:16, :]
    sq_out[...] = square

    moments = jnp.zeros((SL * SCEN, NODES), F32)
    for x, plane in enumerate(basis_by_plane()):
        rows = qf[:, x * 8 : (x + 1) * 8, :].reshape(SL * SCEN, 128).astype(BF16)
        for part in split_two(plane):
            moments = moments + lax.dot_general(rows, part, NT_DIMS, preferred_element_type=F32)
    moments_out[...] = moments
    fetches[2].wait()
    fetches[3].wait()

    def near_pairs(value):
        def contribution(code):
            s = jnp.bitwise_and(lax.shift_right_logical(code, 3), 31)
            which = jnp.bitwise_and(lax.shift_right_logical(code, 8), 15)
            mirrored = lax.shift_right_logical(code, 12)
            left = qb[s + (SL + 1) * mirrored]
            total = [None] * 8
            for chunk in range(4 if value == 1 else 8):
                product = jnp.dot(
                    left,
                    table[which, :, chunk * 256 : (chunk + 1) * 256],
                    preferred_element_type=F32,
                )
                for half in range(2):
                    delta = 2 * chunk + half
                    for sx in range(8):
                        piece = product[sx * 8 : (sx + 1) * 8, half * 128 : (half + 1) * 128]
                        for x in sorted({sx - delta, sx + delta} if value == 1 else {8 + sx - delta}):
                            if 0 <= x < 8:
                                total[x] = piece if total[x] is None else total[x] + piece
            return total

        def four(n, carry):
            codes = [pairs[0, 136 * value + 4 * n + k] for k in range(4)]
            totals = [contribution(code) for code in codes]
            for code, total in zip(codes, totals):
                t = jnp.bitwise_and(code, 7)
                mirrored = lax.shift_right_logical(code, 12)
                for x in range(8):
                    out[t, x if value == 1 else x + mirrored * (7 - 2 * x)] += total[x]
            return carry

        lax.fori_loop(0, lax.shift_right_logical(pairs[0, 408 + value] + 3, 2), four, 0)

    for value in range(2):
        near_pairs(value)


def local_part(charges, block, table, lists):
    hbm = pl.BlockSpec(memory_space=pltpu.HBM)
    vmem = pl.BlockSpec(memory_space=pltpu.VMEM)
    return pl.pallas_call(
        local_kernel,
        out_shape=(
            jax.ShapeDtypeStruct((TL, 8, SCEN, 128), F32),
            jax.ShapeDtypeStruct((SL * SCEN, NODES), F32),
            jax.ShapeDtypeStruct((8, 128), F32),
        ),
        in_specs=[hbm] * 4,
        out_specs=(vmem,) * 3,
        scratch_shapes=[
            pltpu.VMEM((SCEN, SL * LEAF), BF16),
            pltpu.VMEM((SL, 16, 128), F32),
            pltpu.VMEM((9, 128, 2048), BF16),
            pltpu.VMEM((SL, 64, 128), F32),
            pltpu.VMEM((2 * SL + 1, 64, 128), BF16),
            pltpu.SMEM((1, 512), jnp.int32),
            pltpu.SemaphoreType.DMA((4,)),
        ],
        compiler_params=pltpu.CompilerParams(vmem_limit_bytes=VMEM),
        name="local_part",
    )(charges, block, table, lists)


def cholesky(gram, root_ref):
    full = (8, NODES)
    lane = lax.broadcasted_iota(jnp.int32, full, 1)
    row_at = lax.broadcasted_iota(jnp.int32, full, 0)
    left = [gram[8 * k : 8 * k + 8, :] for k in range(8)]
    scale = 1.0 / math.sqrt(CELLS)
    for kb in range(8):
        base = 8 * kb
        rows = [jnp.broadcast_to(left[kb][r : r + 1, :], full) for r in range(8)]
        cols = [
            [jnp.broadcast_to(left[m][:, base + q : base + q + 1], full) for q in range(8)]
            for m in range(kb, 8)
        ]
        splat = [
            [jnp.broadcast_to(cols[0][q][r : r + 1, :], full) if q >= r else None for q in range(8)]
            for r in range(8)
        ]
        out = jnp.zeros(full, F32)
        for r in range(8):
            root = lax.rsqrt(splat[r][r])
            inverse = root * root
            for q in range(r + 1, 8):
                factor = splat[r][q] * inverse
                for p in range(q, 8):
                    splat[q][p] = splat[q][p] - factor * splat[r][p]
                rows[q] = rows[q] - factor * rows[r]
                for m in range(1, len(cols)):
                    cols[m][q] = cols[m][q] - factor * cols[m][r]
            here = (row_at == r) & (lane >= base + r)
            out = jnp.where(here, rows[r] * (root * scale), out)
            for m in range(1, len(cols)):
                left[kb + m] = left[kb + m] - cols[m][r] * (rows[r] * inverse)
        root_ref[base : base + 8, :] = out


def reduce_kernel(
    part_ref, sq_hbm, moments_hbm, phi_hbm, recv, far_recv, root_out,
    buf, root, moments, phi, coeff, send_a, recv_a, send_b, recv_b, send_c, recv_c, own_sem,
):
    a = lax.axis_index("tgt")
    b = lax.axis_index("src")
    barrier = pltpu.get_barrier_semaphore()

    def greet(k, carry):
        pl.semaphore_signal(barrier, 1, device_id=(a, lax.rem(b + k, NS)), device_id_type=MESH)
        return carry

    lax.fori_loop(1, NS, greet, 0)
    sq_copy = pltpu.make_async_copy(sq_hbm, buf.at[b], own_sem.at[0])
    own_copy = pltpu.make_async_copy(part_ref.at[b], recv.at[b], own_sem.at[1])
    sq_copy.start()
    moments_copy = pltpu.make_async_copy(moments_hbm, moments, own_sem.at[3])
    phi_copy = pltpu.make_async_copy(phi_hbm, phi, own_sem.at[4])
    moments_copy.start()
    phi_copy.start()
    own_copy.start()
    sq_copy.wait()
    pl.semaphore_wait(barrier, NS - 1)

    def square_copy(k):
        return pltpu.make_async_remote_copy(
            src_ref=buf.at[b],
            dst_ref=buf.at[b],
            send_sem=send_b.at[k],
            recv_sem=recv_b.at[b],
            device_id=(a, lax.rem(b + k, NS)),
            device_id_type=MESH,
        )

    def part_copy(k):
        at = lax.rem(b + k, NS)
        return pltpu.make_async_remote_copy(
            src_ref=part_ref.at[at],
            dst_ref=recv.at[b],
            send_sem=send_a.at[k],
            recv_sem=recv_a.at[b],
            device_id=(a, at),
            device_id_type=MESH,
        )

    def start(copy):
        def step(k, carry):
            copy(k).start()
            return carry

        lax.fori_loop(1, NS, step, 0)

    start(square_copy)
    start(part_copy)

    moments_copy.wait()
    phi_copy.wait()
    found = jnp.zeros((2 * SCEN, TL * NODES), F32)
    extra = jnp.zeros((SCEN, TL * NODES), F32)
    for s in range(0, SL, 4):
        rows = jnp.concatenate([moments[(s + k) * 8 : (s + k + 1) * 8, :] for k in range(4)], axis=1)
        high = rows.astype(BF16).astype(F32)
        twice = jnp.concatenate([high, rows - high], axis=0).astype(BF16)
        couple = [phi[k, s : s + 4].reshape(4 * NODES, TL * NODES) for k in range(2)]
        found = found + jnp.dot(twice, couple[0], preferred_element_type=F32)
        extra = extra + jnp.dot(high.astype(BF16), couple[1], preferred_element_type=F32)
    total = found[:SCEN] + found[SCEN:] + extra
    for t in range(TL):
        coeff[t, :, 0:NODES] = total[:, t * NODES : (t + 1) * NODES]
        coeff[t, :, NODES:128] = jnp.zeros((SCEN, NODES), F32)

    def far_copy(k):
        at = lax.rem(b + k, NS)
        return pltpu.make_async_remote_copy(
            src_ref=coeff.at[at],
            dst_ref=far_recv.at[b],
            send_sem=send_c.at[k],
            recv_sem=recv_c.at[b],
            device_id=(a, at),
            device_id_type=MESH,
        )

    start(far_copy)
    own_far = pltpu.make_async_copy(coeff.at[b], far_recv.at[b], own_sem.at[5])
    own_far.start()
    planes = basis_by_plane()

    def square_wait(k, carry):
        slot = lax.rem(b + k, NS)
        pltpu.make_async_remote_copy(
            src_ref=buf.at[b],
            dst_ref=buf.at[slot],
            send_sem=send_b.at[0],
            recv_sem=recv_b.at[slot],
            device_id=(a, b),
            device_id_type=MESH,
        ).wait_recv()
        square_copy(k).wait_send()
        return carry

    lax.fori_loop(1, NS, square_wait, 0)
    square = buf[0]
    for k in range(1, NS):
        square = square + buf[k]
    basis = jnp.concatenate(planes, axis=1)
    scaled = jnp.concatenate([planes[k] * square[k : k + 1, :] for k in range(8)], axis=1)
    gram = lax.dot_general(
        scaled, basis, NT_DIMS, precision=lax.Precision.HIGHEST, preferred_element_type=F32
    )
    cholesky(gram, root)
    root_copy = pltpu.make_async_copy(root, root_out, own_sem.at[2])
    root_copy.start()

    def part_wait(k, carry):
        slot = lax.rem(b + k, NS)
        pltpu.make_async_remote_copy(
            src_ref=part_ref.at[0],
            dst_ref=recv.at[slot],
            send_sem=send_a.at[0],
            recv_sem=recv_a.at[slot],
            device_id=(a, b),
            device_id_type=MESH,
        ).wait_recv()
        part_copy(k).wait_send()
        pltpu.make_async_remote_copy(
            src_ref=coeff.at[0],
            dst_ref=far_recv.at[slot],
            send_sem=send_c.at[0],
            recv_sem=recv_c.at[slot],
            device_id=(a, b),
            device_id_type=MESH,
        ).wait_recv()
        far_copy(k).wait_send()
        return carry

    own_copy.wait()
    own_far.wait()
    lax.fori_loop(1, NS, part_wait, 0)
    root_copy.wait()


def reduce_part(part, square, moments, phi):
    hbm = pl.BlockSpec(memory_space=pltpu.HBM)
    return pl.pallas_call(
        reduce_kernel,
        out_shape=(
            jax.ShapeDtypeStruct((NS, 8, SCEN, 128), F32),
            jax.ShapeDtypeStruct((NS, SCEN, 128), F32),
            jax.ShapeDtypeStruct((NODES, NODES), F32),
        ),
        in_specs=[hbm] * 4,
        out_specs=(hbm,) * 3,
        scratch_shapes=[
            pltpu.VMEM((NS, 8, 128), F32),
            pltpu.VMEM((NODES, NODES), F32),
            pltpu.VMEM((SL * SCEN, NODES), F32),
            pltpu.VMEM((2, SL, NODES, TL * NODES), BF16),
            pltpu.VMEM((TL, SCEN, 128), F32),
        ]
        + [pltpu.SemaphoreType.DMA((NS,))] * 6
        + [pltpu.SemaphoreType.DMA((6,))],
        compiler_params=pltpu.CompilerParams(
            collective_id=1, has_side_effects=True, vmem_limit_bytes=VMEM
        ),
        name="reduce_part",
    )(part, square, moments, phi)


def finish_kernel(recv, far_recv, root, order_ref, w_ref, pot_ref, root_ref):
    b = lax.axis_index("src")
    coeff = far_recv[0]
    for k in range(1, NS):
        coeff = coeff + far_recv[k]
    high, low = split_two(coeff[:, 0:NODES])
    left = jnp.concatenate([high, low, high], axis=1)
    basis = [split_two(plane) for plane in basis_by_plane()]
    right = jnp.concatenate(
        [jnp.concatenate([basis[x][k] for x in range(8)], axis=1) for k in (0, 0, 1)], axis=0
    )
    far = jnp.dot(left, right, preferred_element_type=F32)
    blocks = []
    for x in range(8):
        total = recv[0, x]
        for k in range(1, NS):
            total = total + recv[k, x]
        blocks.append(total + far[:, x * 128 : (x + 1) * 128])
    weights = w_ref[pl.ds(pl.multiple_of(b * 8, 8), 8), :]
    for c in range(8):
        index = jnp.broadcast_to(order_ref[0:1, c * 128 : (c + 1) * 128], (8, 128))
        value = permute_row(blocks, index) * weights[c : c + 1, :]
        pot_ref[:, c * 128 : (c + 1) * 128] = value.astype(BF16)
    root_ref[...] = root[...]


def finish(recv, far_recv, root, order, weights):
    vmem = pl.BlockSpec(memory_space=pltpu.VMEM)
    return pl.pallas_call(
        finish_kernel,
        out_shape=(
            jax.ShapeDtypeStruct((SCEN, LEAF), BF16),
            jax.ShapeDtypeStruct((NODES, NODES), F32),
        ),
        in_specs=[vmem] * 5,
        out_specs=(vmem, vmem),
        compiler_params=pltpu.CompilerParams(vmem_limit_bytes=VMEM),
        name="finish",
    )(recv, far_recv, root, order, weights)


def shards(charges, weights, cell_order, leaf_coords, near_src):
    weights = weights.reshape(TL * 8, 128)
    block, table, phi, lists = exchange(leaf_coords, cell_order, weights)
    part, moments, square = local_part(charges, block, table, lists)
    recv, far_recv, root = reduce_part(part, square, moments, phi)
    return tuple(finish(recv, far_recv, root, cell_order, weights))


def solution(mesh):
    placed = (P(None, "src"), P("tgt"), P(("tgt", "src"), None), P(), P("tgt", None))
    return jax.shard_map(
        shards,
        mesh=mesh,
        in_specs=placed,
        out_specs=(P(None, ("tgt", "src")), P()),
        check_vma=False,
    )
```

```python
import math

import jax
import jax.numpy as jnp
import numpy as np
from jax import lax
from jax.experimental import pallas as pl
from jax.experimental.pallas import tpu as pltpu
from jax.sharding import PartitionSpec as P

EDGE = 8
LEAF = 1024
SCEN = 8
LV = 128
NT = 16
NS = 8
TL = LV // NT
SL = LV // NS
NODES = 64
CELLS = LV * LEAF
VMEM = 60 << 20
FAR_FIRST = (4, 3, 5, 2, 6, 1, 7)
MESH = pl.DeviceIdType.MESH
F32 = jnp.float32
BF16 = jnp.bfloat16
NT_DIMS = (((1,), (1,)), ((), ()))


def chebyshev_nodes(extent):
    return [
        extent * 0.5 + extent * 0.5 * math.cos((2.0 * a + 1.0) * (math.pi / 8.0)) for a in range(4)
    ]


def lagrange(points, nodes, a):
    factor = 1.0
    for b in range(4):
        if b != a:
            factor = factor * ((points - nodes[b]) * (1.0 / (nodes[a] - nodes[b])))
    return factor


def select_by(index, values):
    out = values[0]
    for k in range(1, len(values)):
        out = jnp.where(index == k, values[k], out)
    return out


def basis_by_plane():
    row = lax.broadcasted_iota(jnp.int32, (16, 128), 0)
    lane = lax.broadcasted_iota(jnp.int32, (16, 128), 1)
    short, tall = chebyshev_nodes(8.0), chebyshev_nodes(16.0)
    y = lax.shift_right_logical(lane, 4).astype(F32) + 0.5
    z = jnp.bitwise_and(lane, 15).astype(F32) + 0.5
    along_y = select_by(lax.shift_right_logical(row, 2), [lagrange(y, short, k) for k in range(4)])
    along_z = select_by(jnp.bitwise_and(row, 3), [lagrange(z, tall, k) for k in range(4)])
    plane = along_y * along_z
    return [
        jnp.concatenate([plane * float(lagrange(x + 0.5, short, a)) for a in range(4)], axis=0)
        for x in range(8)
    ]


def node_offset(index):
    short, tall = chebyshev_nodes(8.0), chebyshev_nodes(16.0)
    return [
        select_by(lax.shift_right_logical(index, 4), short),
        select_by(jnp.bitwise_and(lax.shift_right_logical(index, 2), 3), short),
        select_by(jnp.bitwise_and(index, 3), tall),
    ]


def split_two(value):
    high = value.astype(BF16)
    return high, (value - high.astype(F32)).astype(BF16)


def near_tables(table, table_out, sems):
    row = lax.broadcasted_iota(jnp.int32, (128, 128), 0)
    lane = lax.broadcasted_iota(jnp.int32, (128, 128), 1)
    step_y = lax.shift_right_logical(lane, 4) - lax.shift_right_logical(row, 4)
    step_z = jnp.bitwise_and(lane, 15) - jnp.bitwise_and(row, 15)

    def one(o, carry):
        dy = step_y - 8 * (lax.div(o, 3) - 1)
        dz = step_z - 16 * (lax.rem(o, 3) - 1)
        base = (dy * dy + dz * dz).astype(F32)
        for delta in range(16):
            value = 0.05 * lax.rsqrt(base + float(delta * delta + 1))
            table[o, :, delta * 128 : (delta + 1) * 128] = value.astype(BF16)
        pltpu.make_async_copy(table.at[o], table_out.at[o], sems.at[o]).start()
        return carry

    lax.fori_loop(0, 9, one, 0)


def far_tables(coords, i, j, phi, phi_out, sem):
    lane = lax.broadcasted_iota(jnp.int32, (1, TL * NODES), 1)
    slot = lax.shift_right_logical(lane, 6)
    spacing = (8.0, 8.0, 16.0)
    box_at = [select_by(slot, [coords[d, i * TL + t] for t in range(TL)]) for d in range(3)]
    offset = node_offset(jnp.bitwise_and(lane, 63))
    node_at = [box_at[d].astype(F32) * spacing[d] + offset[d] for d in range(3)]
    source = node_offset(lax.broadcasted_iota(jnp.int32, (NODES, TL * NODES), 0))

    def one(s, carry):
        distance = 1.0
        close = None
        for d in range(3):
            box = coords[d, j * SL + s]
            inside = jnp.abs(box_at[d] - box) <= 1
            close = inside if close is None else close & inside
            between = (node_at[d] - box.astype(F32) * spacing[d]) - source[d]
            distance = distance + between * between
        high, low = split_two(jnp.where(close, 0.0, 0.05) * lax.rsqrt(distance))
        phi[0, s] = high
        phi[1, s] = low
        return carry

    lax.fori_loop(0, SL, one, 0)
    pltpu.make_async_copy(phi, phi_out, sem).start()


def pair_lists(coords, i, j):
    lane = lax.broadcasted_iota(jnp.int32, (1, 128), 1)
    t, s = lax.shift_right_logical(lane, 4), jnp.bitwise_and(lane, 15)
    step = [
        select_by(s, [coords[d, j * SL + k] for k in range(SL)])
        - select_by(t, [coords[d, i * TL + k] for k in range(TL)])
        for d in range(3)
    ]
    close = (jnp.abs(step[0]) <= 1) & (jnp.abs(step[1]) <= 1) & (jnp.abs(step[2]) <= 1)
    row = lax.broadcasted_iota(jnp.int32, (8, 128), 0)
    member = jnp.where(jnp.broadcast_to(jnp.where(close, jnp.where(step[0] == 0, 1, 0), 9), (8, 128)) == row, 1.0, 0.0)
    ahead = lax.broadcasted_iota(jnp.int32, (128, 128), 0) < lax.broadcasted_iota(jnp.int32, (128, 128), 1)
    rank = jnp.dot(
        member.astype(BF16), jnp.where(ahead, 1.0, 0.0).astype(BF16), preferred_element_type=F32
    )
    place = jnp.full((1, 128), 511.0, F32)
    for v in range(2):
        place = jnp.where(member[v : v + 1, :] > 0.5, rank[v : v + 1, :] + float(136 * v), place)
    position = lax.broadcasted_iota(jnp.int32, (512, 128), 0)
    spread = jnp.where(jnp.broadcast_to(place.astype(jnp.int32), (512, 128)) == position, 1.0, 0.0)
    parts = [t + 8 * s, (step[1] + 1) * 3 + step[2] + 1, jnp.full((1, 128), 1, jnp.int32), jnp.where(step[0] < 0, 1, 0)]
    left = select_by(row, [jnp.broadcast_to(part, (8, 128)) for part in parts]).astype(F32)
    listed = lax.dot_general(
        left.astype(BF16), spread.astype(BF16), NT_DIMS, preferred_element_type=F32
    ).astype(jnp.int32)
    out = jnp.where(listed[2:3, :] > 0, listed[0:1, :] + 256 * listed[1:2, :] + 4096 * listed[3:4, :], 8 * SL)
    at = lax.broadcasted_iota(jnp.int32, (1, 512), 1)
    for v in range(2):
        length = jnp.sum(member[v : v + 1, :], axis=1, keepdims=True).astype(jnp.int32)
        out = jnp.where(at == 408 + v, length, out)
    return out


def exchange_kernel(
    coords_hbm, order_hbm, w_hbm, block_ref, table_out, phi_out, list_out,
    coords, order_ref, w_ref, mine, table, phi, lists,
    send_a, recv_a, table_sem, phi_sem, in_sem, own_sem, list_sem,
):
    a = lax.axis_index("tgt")
    b = lax.axis_index("src")
    barrier = pltpu.get_barrier_semaphore()
    home = lax.rem(a, 2) * NS + b
    column = lax.div(a, 2)
    loops_back = b == column

    def signal_sender(k, carry):
        at = lax.rem(home + k, NT)
        pl.semaphore_signal(
            barrier, 1, device_id=(2 * b + lax.div(at, NS), lax.rem(at, NS)), device_id_type=MESH
        )
        return carry

    @pl.when(jnp.logical_not(loops_back))
    def _():
        signal_sender(0, 0)

    lax.fori_loop(1, NT, signal_sender, 0)
    fetches = [
        pltpu.make_async_copy(order_hbm, order_ref, in_sem.at[0]),
        pltpu.make_async_copy(w_hbm.at[pl.ds(pl.multiple_of(b * 8, 8), 8)], w_ref, in_sem.at[1]),
        pltpu.make_async_copy(coords_hbm, coords, in_sem.at[2]),
    ]
    for fetch in fetches:
        fetch.start()
    for fetch in fetches:
        fetch.wait()

    rows = lax.broadcasted_iota(jnp.int32, (8, 128), 0)
    lanes = lax.broadcasted_iota(jnp.int32, (8, 128), 1)
    low_rows = lax.broadcasted_iota(jnp.int32, (128, 128), 0)
    square = w_ref[...] * w_ref[...]
    placed = jnp.zeros((40, 128), F32)
    for c in range(8):
        order = order_ref[0:1, c * 128 : (c + 1) * 128]
        hit = lax.shift_right_logical(jnp.broadcast_to(order, (8, 128)), 7) == rows
        value = jnp.broadcast_to(square[c : c + 1, :], (8, 128))
        first = value.astype(BF16).astype(F32)
        rest = value - first
        second = rest.astype(BF16).astype(F32)
        third = rest - second
        parts = [jnp.full((8, 128), float(c), F32), lanes.astype(F32), first, second, third]
        left = jnp.concatenate([jnp.where(hit, part, 0.0) for part in parts], axis=0)
        low = jnp.broadcast_to(jnp.bitwise_and(order, 127), (128, 128)) == low_rows
        right = jnp.where(low, 1.0, 0.0).astype(BF16)
        placed = placed + lax.dot_general(
            left.astype(BF16), right, NT_DIMS, preferred_element_type=F32
        )
    mine[0:8, :] = placed[0:8] * 128.0 + placed[8:16]
    mine[8:16, :] = placed[16:24] + placed[24:32] + placed[32:40]

    pl.semaphore_wait(barrier, jnp.where(loops_back, NT - 1, NT).astype(jnp.int32))

    def block_copy(k):
        return pltpu.make_async_remote_copy(
            src_ref=mine,
            dst_ref=block_ref.at[home],
            send_sem=send_a.at[k],
            recv_sem=recv_a.at[home],
            device_id=(lax.rem(a + k, NT), column),
            device_id_type=MESH,
        )

    def start_block(k, carry):
        block_copy(k).start()
        return carry

    lax.fori_loop(1, NT, start_block, 0)

    @pl.when(jnp.logical_not(loops_back))
    def _():
        block_copy(0).start()

    own_copy = pltpu.make_async_copy(mine, block_ref.at[home], own_sem)

    @pl.when(loops_back)
    def _():
        own_copy.start()

    lists[...] = pair_lists(coords, a, b)
    list_copy = pltpu.make_async_copy(lists, list_out, list_sem)
    list_copy.start()
    far_tables(coords, a, b, phi, phi_out, phi_sem)
    near_tables(table, table_out, table_sem)
    list_copy.wait()
    pltpu.make_async_copy(phi, phi_out, phi_sem).wait()
    for o in range(9):
        pltpu.make_async_copy(table.at[o], table_out.at[o], table_sem.at[o]).wait()

    def block_arrival(slot):
        pltpu.make_async_remote_copy(
            src_ref=mine,
            dst_ref=block_ref.at[slot],
            send_sem=send_a.at[0],
            recv_sem=recv_a.at[slot],
            device_id=(a, b),
            device_id_type=MESH,
        ).wait_recv()

    @pl.when(jnp.logical_not(loops_back))
    def _():
        block_arrival(home)
        block_copy(0).wait_send()

    @pl.when(loops_back)
    def _():
        own_copy.wait()

    def wait_block(k, carry):
        block_arrival(lax.rem(home + k, NT))
        block_copy(k).wait_send()
        return carry

    lax.fori_loop(1, NT, wait_block, 0)


def exchange(coords, order, weights):
    hbm = pl.BlockSpec(memory_space=pltpu.HBM)
    return pl.pallas_call(
        exchange_kernel,
        out_shape=(
            jax.ShapeDtypeStruct((SL, 16, 128), F32),
            jax.ShapeDtypeStruct((9, 128, 2048), BF16),
            jax.ShapeDtypeStruct((2, SL, NODES, TL * NODES), BF16),
            jax.ShapeDtypeStruct((1, 512), jnp.int32),
        ),
        in_specs=[hbm] * 3,
        out_specs=(hbm,) * 4,
        scratch_shapes=[
            pltpu.SMEM((3, LV), jnp.int32),
            pltpu.VMEM((1, LEAF), jnp.int32),
            pltpu.VMEM((8, 128), F32),
            pltpu.VMEM((16, 128), F32),
            pltpu.VMEM((9, 128, 2048), BF16),
            pltpu.VMEM((2, SL, NODES, TL * NODES), BF16),
            pltpu.VMEM((1, 512), jnp.int32),
            pltpu.SemaphoreType.DMA((NT,)),
            pltpu.SemaphoreType.DMA((NT,)),
            pltpu.SemaphoreType.DMA((9,)),
            pltpu.SemaphoreType.DMA,
            pltpu.SemaphoreType.DMA((3,)),
            pltpu.SemaphoreType.DMA,
            pltpu.SemaphoreType.DMA,
        ],
        compiler_params=pltpu.CompilerParams(
            collective_id=0, has_side_effects=True, vmem_limit_bytes=VMEM
        ),
        name="exchange",
    )(coords, order, weights)


def lane_gather(block, lane):
    return jnp.take_along_axis(block, lane, axis=1, mode="promise_in_bounds")


def permute_row(blocks, index):
    block = lax.shift_right_logical(index, 7)
    lane = jnp.bitwise_and(index, 127)
    out = lane_gather(blocks[0], lane)
    for k in range(1, 8):
        out = jnp.where(block == k, lane_gather(blocks[k], lane), out)
    return out


def local_kernel(
    charges_hbm, block_hbm, table_hbm, list_hbm, out, moments_out, sq_out,
    charges, block, table, qf, qb, pairs, sems,
):
    fetches = [
        pltpu.make_async_copy(source, target, sems.at[k])
        for k, (source, target) in enumerate(
            [(charges_hbm, charges), (block_hbm, block), (table_hbm, table), (list_hbm, pairs)]
        )
    ]
    for fetch in fetches:
        fetch.start()
    qb[SL] = jnp.zeros((64, 128), BF16)
    out[...] = jnp.zeros((TL, 8, SCEN, 128), F32)

    fetches[0].wait()
    fetches[1].wait()

    low_rows = lax.broadcasted_iota(jnp.int16, (128, 128), 0)
    one = jnp.ones((128, 128), BF16)
    zero = jnp.zeros((128, 128), BF16)

    def by_gather(raw, order):
        blocks = [raw[:, k * 128 : (k + 1) * 128] for k in range(8)]
        return [
            permute_row(blocks, jnp.broadcast_to(order[x : x + 1, :], (8, 128))) for x in range(8)
        ]

    def by_product(raw, order):
        left = jnp.concatenate([raw[:, k * 128 : (k + 1) * 128] for k in range(8)], axis=0).astype(BF16)
        block_at = lax.shift_right_logical(order, 7)
        low = jnp.bitwise_and(order, 127)
        pieces = []
        for x in range(0, 8, 2):
            hots = [
                jnp.where(
                    jnp.broadcast_to(low[y : y + 1, :], (128, 128)).astype(jnp.int16) == low_rows,
                    one,
                    zero,
                )
                for y in (x, x + 1)
            ]
            spread = jnp.dot(left, jnp.concatenate(hots, axis=1), preferred_element_type=F32)
            for half in range(2):
                wanted = jnp.broadcast_to(block_at[x + half : x + half + 1, :], (8, 128))
                lanes = slice(half * 128, (half + 1) * 128)
                pieces.append(select_by(wanted, [spread[k * 8 : (k + 1) * 8, lanes] for k in range(8)]))
        return pieces

    def canonical(group, carry):
        for k in range(4):
            leaf = group * 4 + k
            base = pl.multiple_of(leaf * LEAF, LEAF)
            raw = charges[:, pl.ds(base, LEAF)].astype(F32)
            order = block[leaf, 0:8, :].astype(jnp.int32)
            pieces = by_product(raw, order) if k < 2 else by_gather(raw, order)
            rows = jnp.concatenate(pieces, axis=0)
            qf[leaf] = rows
            qb[leaf] = rows.astype(BF16)
            qb[SL + 1 + leaf] = jnp.concatenate(pieces[::-1], axis=0).astype(BF16)
        return carry

    lax.fori_loop(0, SL // 4, canonical, 0)
    square = block[0, 8:16, :]
    for leaf in range(1, SL):
        square = square + block[leaf, 8:16, :]
    sq_out[...] = square

    moments = jnp.zeros((SL * SCEN, NODES), F32)
    for x, plane in enumerate(basis_by_plane()):
        rows = qf[:, x * 8 : (x + 1) * 8, :].reshape(SL * SCEN, 128).astype(BF16)
        for part in split_two(plane):
            moments = moments + lax.dot_general(rows, part, NT_DIMS, preferred_element_type=F32)
    moments_out[...] = moments
    fetches[2].wait()
    fetches[3].wait()

    def near_pairs(value):
        def contribution(code):
            s = jnp.bitwise_and(lax.shift_right_logical(code, 3), 31)
            which = jnp.bitwise_and(lax.shift_right_logical(code, 8), 15)
            mirrored = lax.shift_right_logical(code, 12)
            left = qb[s + (SL + 1) * mirrored]
            total = [None] * 8
            for chunk in range(4 if value == 1 else 8):
                first, last = (0, 8) if value == 1 else (max(0, 2 * chunk - 8), min(8, 2 * chunk + 2))
                product = jnp.dot(
                    left[first * 8 : last * 8],
                    table[which, :, chunk * 256 : (chunk + 1) * 256],
                    preferred_element_type=F32,
                )
                for half in range(2):
                    delta = 2 * chunk + half
                    for sx in range(first, last):
                        piece = product[(sx - first) * 8 : (sx - first + 1) * 8, half * 128 : (half + 1) * 128]
                        for x in sorted({sx - delta, sx + delta} if value == 1 else {8 + sx - delta}):
                            if 0 <= x < 8:
                                total[x] = piece if total[x] is None else total[x] + piece
            return total

        def step(first, size):
            codes = [pairs[0, first + k] for k in range(size)]
            totals = [contribution(code) for code in codes]
            for code, total in zip(codes, totals):
                t = jnp.bitwise_and(code, 7)
                mirrored = lax.shift_right_logical(code, 12)
                for x in range(8):
                    out[t, x if value == 1 else x + mirrored * (7 - 2 * x)] += total[x]

        def eight(n, carry):
            step(136 * value + 8 * n, 8)
            return carry

        length = pairs[0, 408 + value]
        full = lax.shift_right_logical(length + 3, 3)
        lax.fori_loop(0, full, eight, 0)

        @pl.when(length > 8 * full)
        def _():
            step(136 * value + 8 * full, 4)

    for value in range(2):
        near_pairs(value)


def local_part(charges, block, table, lists):
    hbm = pl.BlockSpec(memory_space=pltpu.HBM)
    vmem = pl.BlockSpec(memory_space=pltpu.VMEM)
    return pl.pallas_call(
        local_kernel,
        out_shape=(
            jax.ShapeDtypeStruct((TL, 8, SCEN, 128), F32),
            jax.ShapeDtypeStruct((SL * SCEN, NODES), F32),
            jax.ShapeDtypeStruct((8, 128), F32),
        ),
        in_specs=[hbm] * 4,
        out_specs=(vmem,) * 3,
        scratch_shapes=[
            pltpu.VMEM((SCEN, SL * LEAF), BF16),
            pltpu.VMEM((SL, 16, 128), F32),
            pltpu.VMEM((9, 128, 2048), BF16),
            pltpu.VMEM((SL, 64, 128), F32),
            pltpu.VMEM((2 * SL + 1, 64, 128), BF16),
            pltpu.SMEM((1, 512), jnp.int32),
            pltpu.SemaphoreType.DMA((4,)),
        ],
        compiler_params=pltpu.CompilerParams(vmem_limit_bytes=VMEM),
        name="local_part",
    )(charges, block, table, lists)


def cholesky(gram, root_ref):
    full = (8, NODES)
    lane = lax.broadcasted_iota(jnp.int32, full, 1)
    row_at = lax.broadcasted_iota(jnp.int32, full, 0)
    left = [gram[8 * k : 8 * k + 8, :] for k in range(8)]
    scale = 1.0 / math.sqrt(CELLS)
    for kb in range(8):
        base = 8 * kb
        rows = [jnp.broadcast_to(left[kb][r : r + 1, :], full) for r in range(8)]
        cols = [
            [jnp.broadcast_to(left[m][:, base + q : base + q + 1], full) for q in range(8)]
            for m in range(kb, 8)
        ]
        splat = [
            [jnp.broadcast_to(cols[0][q][r : r + 1, :], full) if q >= r else None for q in range(8)]
            for r in range(8)
        ]
        out = jnp.zeros(full, F32)
        for r in range(0, 8, 2):
            p, q, w = splat[r][r], splat[r][r + 1], splat[r + 1][r + 1]
            inverse = lax.rsqrt(p * w - q * q)
            inverse = inverse * inverse
            pp, qq, ww = p * inverse, q * inverse, w * inverse
            for k in range(r + 2, 8):
                one = splat[r][k] * ww - splat[r + 1][k] * qq
                two = splat[r + 1][k] * pp - splat[r][k] * qq
                for m in range(k, 8):
                    splat[k][m] = splat[k][m] - (one * splat[r][m] + two * splat[r + 1][m])
                rows[k] = rows[k] - (one * rows[r] + two * rows[r + 1])
                for m in range(1, len(cols)):
                    cols[m][k] = cols[m][k] - (one * cols[m][r] + two * cols[m][r + 1])
            root = lax.rsqrt(p)
            ratio = q * (root * root)
            first = rows[r] * (root * scale)
            second = (rows[r + 1] - ratio * rows[r]) * (lax.rsqrt(w - ratio * q) * scale)
            out = jnp.where((row_at == r) & (lane >= base + r), first, out)
            out = jnp.where((row_at == r + 1) & (lane >= base + r + 1), second, out)
            above = ww * rows[r] - qq * rows[r + 1]
            below = pp * rows[r + 1] - qq * rows[r]
            for m in range(1, len(cols)):
                left[kb + m] = left[kb + m] - (cols[m][r] * above + cols[m][r + 1] * below)
        root_ref[base : base + 8, :] = out


def reduce_kernel(
    part_ref, sq_hbm, moments_hbm, phi_hbm, recv, far_recv, root_out,
    buf, root, moments, phi, coeff, send_a, recv_a, send_b, recv_b, send_c, recv_c, own_sem,
):
    a = lax.axis_index("tgt")
    b = lax.axis_index("src")
    barrier = pltpu.get_barrier_semaphore()

    def greet(k, carry):
        pl.semaphore_signal(barrier, 1, device_id=(a, lax.rem(b + k, NS)), device_id_type=MESH)
        return carry

    lax.fori_loop(1, NS, greet, 0)
    sq_copy = pltpu.make_async_copy(sq_hbm, buf.at[b], own_sem.at[0])
    own_copy = pltpu.make_async_copy(part_ref.at[b], recv.at[b], own_sem.at[1])
    sq_copy.start()
    moments_copy = pltpu.make_async_copy(moments_hbm, moments, own_sem.at[3])
    phi_copy = pltpu.make_async_copy(phi_hbm, phi, own_sem.at[4])
    moments_copy.start()
    phi_copy.start()
    own_copy.start()
    sq_copy.wait()
    pl.semaphore_wait(barrier, NS - 1)

    def square_copy(k):
        return pltpu.make_async_remote_copy(
            src_ref=buf.at[b],
            dst_ref=buf.at[b],
            send_sem=send_b.at[k],
            recv_sem=recv_b.at[b],
            device_id=(a, lax.rem(b + k, NS)),
            device_id_type=MESH,
        )

    def part_copy(k):
        at = lax.rem(b + k, NS)
        return pltpu.make_async_remote_copy(
            src_ref=part_ref.at[at],
            dst_ref=recv.at[b],
            send_sem=send_a.at[k],
            recv_sem=recv_a.at[b],
            device_id=(a, at),
            device_id_type=MESH,
        )

    def start(copy):
        for k in FAR_FIRST:
            copy(k).start()

    start(square_copy)
    start(part_copy)

    moments_copy.wait()
    phi_copy.wait()
    found = jnp.zeros((2 * SCEN, TL * NODES), F32)
    extra = jnp.zeros((SCEN, TL * NODES), F32)
    for s in range(0, SL, 4):
        rows = jnp.concatenate([moments[(s + k) * 8 : (s + k + 1) * 8, :] for k in range(4)], axis=1)
        high = rows.astype(BF16).astype(F32)
        twice = jnp.concatenate([high, rows - high], axis=0).astype(BF16)
        couple = [phi[k, s : s + 4].reshape(4 * NODES, TL * NODES) for k in range(2)]
        found = found + jnp.dot(twice, couple[0], preferred_element_type=F32)
        extra = extra + jnp.dot(high.astype(BF16), couple[1], preferred_element_type=F32)
    total = found[:SCEN] + found[SCEN:] + extra
    for t in range(TL):
        coeff[t, :, 0:NODES] = total[:, t * NODES : (t + 1) * NODES]
        coeff[t, :, NODES:128] = jnp.zeros((SCEN, NODES), F32)

    def far_copy(k):
        at = lax.rem(b + k, NS)
        return pltpu.make_async_remote_copy(
            src_ref=coeff.at[at],
            dst_ref=far_recv.at[b],
            send_sem=send_c.at[k],
            recv_sem=recv_c.at[b],
            device_id=(a, at),
            device_id_type=MESH,
        )

    start(far_copy)
    own_far = pltpu.make_async_copy(coeff.at[b], far_recv.at[b], own_sem.at[5])
    own_far.start()
    planes = basis_by_plane()

    def square_wait(k, carry):
        slot = lax.rem(b + k, NS)
        pltpu.make_async_remote_copy(
            src_ref=buf.at[b],
            dst_ref=buf.at[slot],
            send_sem=send_b.at[0],
            recv_sem=recv_b.at[slot],
            device_id=(a, b),
            device_id_type=MESH,
        ).wait_recv()
        square_copy(k).wait_send()
        return carry

    lax.fori_loop(1, NS, square_wait, 0)
    square = buf[0]
    for k in range(1, NS):
        square = square + buf[k]
    basis = jnp.concatenate(planes, axis=1)
    scaled = jnp.concatenate([planes[k] * square[k : k + 1, :] for k in range(8)], axis=1)
    gram = lax.dot_general(
        scaled, basis, NT_DIMS, precision=lax.Precision.HIGHEST, preferred_element_type=F32
    )
    cholesky(gram, root)
    root_copy = pltpu.make_async_copy(root, root_out, own_sem.at[2])
    root_copy.start()

    def part_wait(k, carry):
        slot = lax.rem(b + k, NS)
        pltpu.make_async_remote_copy(
            src_ref=part_ref.at[0],
            dst_ref=recv.at[slot],
            send_sem=send_a.at[0],
            recv_sem=recv_a.at[slot],
            device_id=(a, b),
            device_id_type=MESH,
        ).wait_recv()
        part_copy(k).wait_send()
        pltpu.make_async_remote_copy(
            src_ref=coeff.at[0],
            dst_ref=far_recv.at[slot],
            send_sem=send_c.at[0],
            recv_sem=recv_c.at[slot],
            device_id=(a, b),
            device_id_type=MESH,
        ).wait_recv()
        far_copy(k).wait_send()
        return carry

    own_copy.wait()
    own_far.wait()
    lax.fori_loop(1, NS, part_wait, 0)
    root_copy.wait()


def reduce_part(part, square, moments, phi):
    hbm = pl.BlockSpec(memory_space=pltpu.HBM)
    return pl.pallas_call(
        reduce_kernel,
        out_shape=(
            jax.ShapeDtypeStruct((NS, 8, SCEN, 128), F32),
            jax.ShapeDtypeStruct((NS, SCEN, 128), F32),
            jax.ShapeDtypeStruct((NODES, NODES), F32),
        ),
        in_specs=[hbm] * 4,
        out_specs=(hbm,) * 3,
        scratch_shapes=[
            pltpu.VMEM((NS, 8, 128), F32),
            pltpu.VMEM((NODES, NODES), F32),
            pltpu.VMEM((SL * SCEN, NODES), F32),
            pltpu.VMEM((2, SL, NODES, TL * NODES), BF16),
            pltpu.VMEM((TL, SCEN, 128), F32),
        ]
        + [pltpu.SemaphoreType.DMA((NS,))] * 6
        + [pltpu.SemaphoreType.DMA((6,))],
        compiler_params=pltpu.CompilerParams(
            collective_id=1, has_side_effects=True, vmem_limit_bytes=VMEM
        ),
        name="reduce_part",
    )(part, square, moments, phi)


def finish_kernel(recv, far_recv, root, order_ref, w_ref, pot_ref, root_ref):
    b = lax.axis_index("src")
    coeff = far_recv[0]
    for k in range(1, NS):
        coeff = coeff + far_recv[k]
    high, low = split_two(coeff[:, 0:NODES])
    left = jnp.concatenate([high, low, high], axis=1)
    basis = [split_two(plane) for plane in basis_by_plane()]
    right = jnp.concatenate(
        [jnp.concatenate([basis[x][k] for x in range(8)], axis=1) for k in (0, 0, 1)], axis=0
    )
    far = jnp.dot(left, right, preferred_element_type=F32)
    blocks = []
    for x in range(8):
        total = recv[0, x]
        for k in range(1, NS):
            total = total + recv[k, x]
        blocks.append(total + far[:, x * 128 : (x + 1) * 128])
    weights = w_ref[pl.ds(pl.multiple_of(b * 8, 8), 8), :]
    for c in range(8):
        index = jnp.broadcast_to(order_ref[0:1, c * 128 : (c + 1) * 128], (8, 128))
        value = permute_row(blocks, index) * weights[c : c + 1, :]
        pot_ref[:, c * 128 : (c + 1) * 128] = value.astype(BF16)
    root_ref[...] = root[...]


def finish(recv, far_recv, root, order, weights):
    vmem = pl.BlockSpec(memory_space=pltpu.VMEM)
    return pl.pallas_call(
        finish_kernel,
        out_shape=(
            jax.ShapeDtypeStruct((SCEN, LEAF), BF16),
            jax.ShapeDtypeStruct((NODES, NODES), F32),
        ),
        in_specs=[vmem] * 5,
        out_specs=(vmem, vmem),
        compiler_params=pltpu.CompilerParams(vmem_limit_bytes=VMEM),
        name="finish",
    )(recv, far_recv, root, order, weights)


def shards(charges, weights, cell_order, leaf_coords, near_src):
    weights = weights.reshape(TL * 8, 128)
    block, table, phi, lists = exchange(leaf_coords, cell_order, weights)
    part, moments, square = local_part(charges, block, table, lists)
    recv, far_recv, root = reduce_part(part, square, moments, phi)
    return tuple(finish(recv, far_recv, root, cell_order, weights))


def solution(mesh):
    placed = (P(None, "src"), P("tgt"), P(("tgt", "src"), None), P(), P("tgt", None))
    return jax.shard_map(
        shards,
        mesh=mesh,
        in_specs=placed,
        out_specs=(P(None, ("tgt", "src")), P()),
        check_vma=False,
    )
```

```python
import math

import jax
import jax.numpy as jnp
import numpy as np
from jax import lax
from jax.experimental import pallas as pl
from jax.experimental.pallas import tpu as pltpu
from jax.sharding import PartitionSpec as P

EDGE = 8
LEAF = 1024
SCEN = 8
LV = 128
NT = 16
NS = 8
TL = LV // NT
SL = LV // NS
NODES = 64
CELLS = LV * LEAF
VMEM = 60 << 20
FAR_FIRST = (4, 3, 5, 2, 6, 1, 7)
MESH = pl.DeviceIdType.MESH
F32 = jnp.float32
BF16 = jnp.bfloat16
NT_DIMS = (((1,), (1,)), ((), ()))


def chebyshev_nodes(extent):
    return [
        extent * 0.5 + extent * 0.5 * math.cos((2.0 * a + 1.0) * (math.pi / 8.0)) for a in range(4)
    ]


def lagrange(points, nodes, a):
    factor = 1.0
    for b in range(4):
        if b != a:
            factor = factor * ((points - nodes[b]) * (1.0 / (nodes[a] - nodes[b])))
    return factor


def select_by(index, values):
    out = values[0]
    for k in range(1, len(values)):
        out = jnp.where(index == k, values[k], out)
    return out


def basis_by_plane():
    row = lax.broadcasted_iota(jnp.int32, (16, 128), 0)
    lane = lax.broadcasted_iota(jnp.int32, (16, 128), 1)
    short, tall = chebyshev_nodes(8.0), chebyshev_nodes(16.0)
    y = lax.shift_right_logical(lane, 4).astype(F32) + 0.5
    z = jnp.bitwise_and(lane, 15).astype(F32) + 0.5
    along_y = select_by(lax.shift_right_logical(row, 2), [lagrange(y, short, k) for k in range(4)])
    along_z = select_by(jnp.bitwise_and(row, 3), [lagrange(z, tall, k) for k in range(4)])
    plane = along_y * along_z
    return [
        jnp.concatenate([plane * float(lagrange(x + 0.5, short, a)) for a in range(4)], axis=0)
        for x in range(8)
    ]


def node_offset(index):
    short, tall = chebyshev_nodes(8.0), chebyshev_nodes(16.0)
    return [
        select_by(lax.shift_right_logical(index, 4), short),
        select_by(jnp.bitwise_and(lax.shift_right_logical(index, 2), 3), short),
        select_by(jnp.bitwise_and(index, 3), tall),
    ]


def split_two(value):
    high = value.astype(BF16)
    return high, (value - high.astype(F32)).astype(BF16)


def near_tables(table, table_out, sems):
    row = lax.broadcasted_iota(jnp.int32, (128, 128), 0)
    lane = lax.broadcasted_iota(jnp.int32, (128, 128), 1)
    step_y = lax.shift_right_logical(lane, 4) - lax.shift_right_logical(row, 4)
    step_z = jnp.bitwise_and(lane, 15) - jnp.bitwise_and(row, 15)

    def one(o, carry):
        dy = step_y - 8 * (lax.div(o, 3) - 1)
        dz = step_z - 16 * (lax.rem(o, 3) - 1)
        base = (dy * dy + dz * dz).astype(F32)
        for delta in range(16):
            value = 0.05 * lax.rsqrt(base + float(delta * delta + 1))
            table[o, :, delta * 128 : (delta + 1) * 128] = value.astype(BF16)
        pltpu.make_async_copy(table.at[o], table_out.at[o], sems.at[o]).start()
        return carry

    lax.fori_loop(0, 9, one, 0)


def far_tables(coords, i, j, phi, phi_out, sem):
    lane = lax.broadcasted_iota(jnp.int32, (1, TL * NODES), 1)
    slot = lax.shift_right_logical(lane, 6)
    spacing = (8.0, 8.0, 16.0)
    box_at = [select_by(slot, [coords[d, i * TL + t] for t in range(TL)]) for d in range(3)]
    offset = node_offset(jnp.bitwise_and(lane, 63))
    node_at = [box_at[d].astype(F32) * spacing[d] + offset[d] for d in range(3)]
    source = node_offset(lax.broadcasted_iota(jnp.int32, (NODES, TL * NODES), 0))

    def one(s, carry):
        distance = 1.0
        close = None
        for d in range(3):
            box = coords[d, j * SL + s]
            inside = jnp.abs(box_at[d] - box) <= 1
            close = inside if close is None else close & inside
            between = (node_at[d] - box.astype(F32) * spacing[d]) - source[d]
            distance = distance + between * between
        high, low = split_two(jnp.where(close, 0.0, 0.05) * lax.rsqrt(distance))
        phi[0, s] = high
        phi[1, s] = low
        return carry

    lax.fori_loop(0, SL, one, 0)
    pltpu.make_async_copy(phi, phi_out, sem).start()


def pair_lists(coords, i, j):
    lane = lax.broadcasted_iota(jnp.int32, (1, 128), 1)
    t, s = lax.shift_right_logical(lane, 4), jnp.bitwise_and(lane, 15)
    step = [
        select_by(s, [coords[d, j * SL + k] for k in range(SL)])
        - select_by(t, [coords[d, i * TL + k] for k in range(TL)])
        for d in range(3)
    ]
    close = (jnp.abs(step[0]) <= 1) & (jnp.abs(step[1]) <= 1) & (jnp.abs(step[2]) <= 1)
    row = lax.broadcasted_iota(jnp.int32, (8, 128), 0)
    member = jnp.where(jnp.broadcast_to(jnp.where(close, jnp.where(step[0] == 0, 1, 0), 9), (8, 128)) == row, 1.0, 0.0)
    ahead = lax.broadcasted_iota(jnp.int32, (128, 128), 0) < lax.broadcasted_iota(jnp.int32, (128, 128), 1)
    rank = jnp.dot(
        member.astype(BF16), jnp.where(ahead, 1.0, 0.0).astype(BF16), preferred_element_type=F32
    )
    place = jnp.full((1, 128), 511.0, F32)
    for v in range(2):
        place = jnp.where(member[v : v + 1, :] > 0.5, rank[v : v + 1, :] + float(136 * v), place)
    position = lax.broadcasted_iota(jnp.int32, (512, 128), 0)
    spread = jnp.where(jnp.broadcast_to(place.astype(jnp.int32), (512, 128)) == position, 1.0, 0.0)
    parts = [t + 8 * s, (step[1] + 1) * 3 + step[2] + 1, jnp.full((1, 128), 1, jnp.int32), jnp.where(step[0] < 0, 1, 0)]
    left = select_by(row, [jnp.broadcast_to(part, (8, 128)) for part in parts]).astype(F32)
    listed = lax.dot_general(
        left.astype(BF16), spread.astype(BF16), NT_DIMS, preferred_element_type=F32
    ).astype(jnp.int32)
    out = jnp.where(listed[2:3, :] > 0, listed[0:1, :] + 256 * listed[1:2, :] + 4096 * listed[3:4, :], 8 * SL)
    at = lax.broadcasted_iota(jnp.int32, (1, 512), 1)
    for v in range(2):
        length = jnp.sum(member[v : v + 1, :], axis=1, keepdims=True).astype(jnp.int32)
        out = jnp.where(at == 408 + v, length, out)
    return out


def exchange_kernel(
    coords_hbm, order_hbm, w_hbm, block_ref, table_out, phi_out, list_out,
    coords, order_ref, w_ref, mine, table, phi, lists,
    send_a, recv_a, table_sem, phi_sem, in_sem, own_sem, list_sem,
):
    a = lax.axis_index("tgt")
    b = lax.axis_index("src")
    barrier = pltpu.get_barrier_semaphore()
    home = lax.rem(a, 2) * NS + b
    column = lax.div(a, 2)
    loops_back = b == column

    def signal_sender(k, carry):
        at = lax.rem(home + k, NT)
        pl.semaphore_signal(
            barrier, 1, device_id=(2 * b + lax.div(at, NS), lax.rem(at, NS)), device_id_type=MESH
        )
        return carry

    @pl.when(jnp.logical_not(loops_back))
    def _():
        signal_sender(0, 0)

    lax.fori_loop(1, NT, signal_sender, 0)
    fetches = [
        pltpu.make_async_copy(order_hbm, order_ref, in_sem.at[0]),
        pltpu.make_async_copy(w_hbm.at[pl.ds(pl.multiple_of(b * 8, 8), 8)], w_ref, in_sem.at[1]),
        pltpu.make_async_copy(coords_hbm, coords, in_sem.at[2]),
    ]
    for fetch in fetches:
        fetch.start()
    for fetch in fetches:
        fetch.wait()

    rows = lax.broadcasted_iota(jnp.int32, (8, 128), 0)
    lanes = lax.broadcasted_iota(jnp.int32, (8, 128), 1)
    low_rows = lax.broadcasted_iota(jnp.int32, (128, 128), 0)
    square = w_ref[...] * w_ref[...]
    placed = jnp.zeros((40, 128), F32)
    for c in range(8):
        order = order_ref[0:1, c * 128 : (c + 1) * 128]
        hit = lax.shift_right_logical(jnp.broadcast_to(order, (8, 128)), 7) == rows
        value = jnp.broadcast_to(square[c : c + 1, :], (8, 128))
        first = value.astype(BF16).astype(F32)
        rest = value - first
        second = rest.astype(BF16).astype(F32)
        third = rest - second
        parts = [jnp.full((8, 128), float(c), F32), lanes.astype(F32), first, second, third]
        left = jnp.concatenate([jnp.where(hit, part, 0.0) for part in parts], axis=0)
        low = jnp.broadcast_to(jnp.bitwise_and(order, 127), (128, 128)) == low_rows
        right = jnp.where(low, 1.0, 0.0).astype(BF16)
        placed = placed + lax.dot_general(
            left.astype(BF16), right, NT_DIMS, preferred_element_type=F32
        )
    mine[0:8, :] = placed[0:8] * 128.0 + placed[8:16]
    mine[8:16, :] = placed[16:24] + placed[24:32] + placed[32:40]

    pl.semaphore_wait(barrier, jnp.where(loops_back, NT - 1, NT).astype(jnp.int32))

    def block_copy(k):
        return pltpu.make_async_remote_copy(
            src_ref=mine,
            dst_ref=block_ref.at[home],
            send_sem=send_a.at[k],
            recv_sem=recv_a.at[home],
            device_id=(lax.rem(a + k, NT), column),
            device_id_type=MESH,
        )

    def start_block(k, carry):
        block_copy(k).start()
        return carry

    lax.fori_loop(1, NT, start_block, 0)

    @pl.when(jnp.logical_not(loops_back))
    def _():
        block_copy(0).start()

    own_copy = pltpu.make_async_copy(mine, block_ref.at[home], own_sem)

    @pl.when(loops_back)
    def _():
        own_copy.start()

    lists[...] = pair_lists(coords, a, b)
    list_copy = pltpu.make_async_copy(lists, list_out, list_sem)
    list_copy.start()
    far_tables(coords, a, b, phi, phi_out, phi_sem)
    near_tables(table, table_out, table_sem)
    list_copy.wait()
    pltpu.make_async_copy(phi, phi_out, phi_sem).wait()
    for o in range(9):
        pltpu.make_async_copy(table.at[o], table_out.at[o], table_sem.at[o]).wait()

    def block_arrival(slot):
        pltpu.make_async_remote_copy(
            src_ref=mine,
            dst_ref=block_ref.at[slot],
            send_sem=send_a.at[0],
            recv_sem=recv_a.at[slot],
            device_id=(a, b),
            device_id_type=MESH,
        ).wait_recv()

    @pl.when(jnp.logical_not(loops_back))
    def _():
        block_arrival(home)
        block_copy(0).wait_send()

    @pl.when(loops_back)
    def _():
        own_copy.wait()

    def wait_block(k, carry):
        block_arrival(lax.rem(home + k, NT))
        block_copy(k).wait_send()
        return carry

    lax.fori_loop(1, NT, wait_block, 0)


def exchange(coords, order, weights):
    hbm = pl.BlockSpec(memory_space=pltpu.HBM)
    return pl.pallas_call(
        exchange_kernel,
        out_shape=(
            jax.ShapeDtypeStruct((SL, 16, 128), F32),
            jax.ShapeDtypeStruct((9, 128, 2048), BF16),
            jax.ShapeDtypeStruct((2, SL, NODES, TL * NODES), BF16),
            jax.ShapeDtypeStruct((1, 512), jnp.int32),
        ),
        in_specs=[hbm] * 3,
        out_specs=(hbm,) * 4,
        scratch_shapes=[
            pltpu.SMEM((3, LV), jnp.int32),
            pltpu.VMEM((1, LEAF), jnp.int32),
            pltpu.VMEM((8, 128), F32),
            pltpu.VMEM((16, 128), F32),
            pltpu.VMEM((9, 128, 2048), BF16),
            pltpu.VMEM((2, SL, NODES, TL * NODES), BF16),
            pltpu.VMEM((1, 512), jnp.int32),
            pltpu.SemaphoreType.DMA((NT,)),
            pltpu.SemaphoreType.DMA((NT,)),
            pltpu.SemaphoreType.DMA((9,)),
            pltpu.SemaphoreType.DMA,
            pltpu.SemaphoreType.DMA((3,)),
            pltpu.SemaphoreType.DMA,
            pltpu.SemaphoreType.DMA,
        ],
        compiler_params=pltpu.CompilerParams(
            collective_id=0, has_side_effects=True, vmem_limit_bytes=VMEM
        ),
        name="exchange",
    )(coords, order, weights)


def lane_gather(block, lane):
    return jnp.take_along_axis(block, lane, axis=1, mode="promise_in_bounds")


def permute_row(blocks, index):
    block = lax.shift_right_logical(index, 7)
    lane = jnp.bitwise_and(index, 127)
    out = lane_gather(blocks[0], lane)
    for k in range(1, 8):
        out = jnp.where(block == k, lane_gather(blocks[k], lane), out)
    return out


def local_kernel(
    charges_hbm, block_hbm, table_hbm, list_hbm, out, moments_out, sq_out,
    charges, block, table, qf, qb, pairs, sems,
):
    fetches = [
        pltpu.make_async_copy(source, target, sems.at[k])
        for k, (source, target) in enumerate(
            [(charges_hbm, charges), (block_hbm, block), (table_hbm, table), (list_hbm, pairs)]
        )
    ]
    for fetch in fetches:
        fetch.start()
    qb[SL] = jnp.zeros((64, 128), BF16)
    out[...] = jnp.zeros((TL, 8, SCEN, 128), F32)

    fetches[0].wait()
    fetches[1].wait()

    low_rows = lax.broadcasted_iota(jnp.int16, (128, 128), 0)
    one = jnp.ones((128, 128), BF16)
    zero = jnp.zeros((128, 128), BF16)

    def by_gather(raw, order):
        blocks = [raw[:, k * 128 : (k + 1) * 128] for k in range(8)]
        return [
            permute_row(blocks, jnp.broadcast_to(order[x : x + 1, :], (8, 128))) for x in range(8)
        ]

    def by_product(raw, order):
        left = jnp.concatenate([raw[:, k * 128 : (k + 1) * 128] for k in range(8)], axis=0).astype(BF16)
        block_at = lax.shift_right_logical(order, 7)
        low = jnp.bitwise_and(order, 127)
        pieces = []
        for x in range(0, 8, 2):
            hots = [
                jnp.where(
                    jnp.broadcast_to(low[y : y + 1, :], (128, 128)).astype(jnp.int16) == low_rows,
                    one,
                    zero,
                )
                for y in (x, x + 1)
            ]
            spread = jnp.dot(left, jnp.concatenate(hots, axis=1), preferred_element_type=F32)
            for half in range(2):
                wanted = jnp.broadcast_to(block_at[x + half : x + half + 1, :], (8, 128))
                lanes = slice(half * 128, (half + 1) * 128)
                pieces.append(select_by(wanted, [spread[k * 8 : (k + 1) * 8, lanes] for k in range(8)]))
        return pieces

    def canonical(group, carry):
        for k in range(8):
            leaf = group * 8 + k
            base = pl.multiple_of(leaf * LEAF, LEAF)
            raw = charges[:, pl.ds(base, LEAF)].astype(F32)
            order = block[leaf, 0:8, :].astype(jnp.int32)
            pieces = by_product(raw, order) if k % 2 == 0 else by_gather(raw, order)
            rows = jnp.concatenate(pieces, axis=0)
            qf[leaf] = rows
            qb[leaf] = rows.astype(BF16)
            qb[SL + 1 + leaf] = jnp.concatenate(pieces[::-1], axis=0).astype(BF16)
        return carry

    lax.fori_loop(0, SL // 8, canonical, 0)
    square = block[0, 8:16, :]
    for leaf in range(1, SL):
        square = square + block[leaf, 8:16, :]
    sq_out[...] = square

    moments = jnp.zeros((SL * SCEN, NODES), F32)
    for x, plane in enumerate(basis_by_plane()):
        rows = qf[:, x * 8 : (x + 1) * 8, :].reshape(SL * SCEN, 128).astype(BF16)
        for part in split_two(plane):
            moments = moments + lax.dot_general(rows, part, NT_DIMS, preferred_element_type=F32)
    moments_out[...] = moments
    fetches[2].wait()
    fetches[3].wait()

    def near_pairs(value):
        def contribution(code):
            s = jnp.bitwise_and(lax.shift_right_logical(code, 3), 31)
            which = jnp.bitwise_and(lax.shift_right_logical(code, 8), 15)
            mirrored = lax.shift_right_logical(code, 12)
            left = qb[s + (SL + 1) * mirrored]
            total = [None] * 8
            for chunk in range(4 if value == 1 else 8):
                first, last = (0, 8) if value == 1 else (max(0, 2 * chunk - 8), min(8, 2 * chunk + 2))
                product = jnp.dot(
                    left[first * 8 : last * 8],
                    table[which, :, chunk * 256 : (chunk + 1) * 256],
                    preferred_element_type=F32,
                )
                for half in range(2):
                    delta = 2 * chunk + half
                    for sx in range(first, last):
                        piece = product[(sx - first) * 8 : (sx - first + 1) * 8, half * 128 : (half + 1) * 128]
                        for x in sorted({sx - delta, sx + delta} if value == 1 else {8 + sx - delta}):
                            if 0 <= x < 8:
                                total[x] = piece if total[x] is None else total[x] + piece
            return total

        def step(first, size):
            codes = [pairs[0, first + k] for k in range(size)]
            totals = [contribution(code) for code in codes]
            for code, total in zip(codes, totals):
                t = jnp.bitwise_and(code, 7)
                mirrored = lax.shift_right_logical(code, 12)
                for x in range(8):
                    out[t, x if value == 1 else x + mirrored * (7 - 2 * x)] += total[x]

        def eight(n, carry):
            step(136 * value + 8 * n, 8)
            return carry

        length = pairs[0, 408 + value]
        full = lax.shift_right_logical(length + 3, 3)
        lax.fori_loop(0, full, eight, 0)

        @pl.when(length > 8 * full)
        def _():
            step(136 * value + 8 * full, 4)

    for value in range(2):
        near_pairs(value)


def local_part(charges, block, table, lists):
    hbm = pl.BlockSpec(memory_space=pltpu.HBM)
    vmem = pl.BlockSpec(memory_space=pltpu.VMEM)
    return pl.pallas_call(
        local_kernel,
        out_shape=(
            jax.ShapeDtypeStruct((TL, 8, SCEN, 128), F32),
            jax.ShapeDtypeStruct((SL * SCEN, NODES), F32),
            jax.ShapeDtypeStruct((8, 128), F32),
        ),
        in_specs=[hbm] * 4,
        out_specs=(vmem,) * 3,
        scratch_shapes=[
            pltpu.VMEM((SCEN, SL * LEAF), BF16),
            pltpu.VMEM((SL, 16, 128), F32),
            pltpu.VMEM((9, 128, 2048), BF16),
            pltpu.VMEM((SL, 64, 128), F32),
            pltpu.VMEM((2 * SL + 1, 64, 128), BF16),
            pltpu.SMEM((1, 512), jnp.int32),
            pltpu.SemaphoreType.DMA((4,)),
        ],
        compiler_params=pltpu.CompilerParams(vmem_limit_bytes=VMEM),
        name="local_part",
    )(charges, block, table, lists)


def cholesky(gram, root_ref):
    full = (8, NODES)
    lane = lax.broadcasted_iota(jnp.int32, full, 1)
    row_at = lax.broadcasted_iota(jnp.int32, full, 0)
    left = [gram[8 * k : 8 * k + 8, :] for k in range(8)]
    scale = 1.0 / math.sqrt(CELLS)
    for kb in range(8):
        base = 8 * kb
        rows = [jnp.broadcast_to(left[kb][r : r + 1, :], full) for r in range(8)]
        cols = [
            [jnp.broadcast_to(left[m][:, base + q : base + q + 1], full) for q in range(8)]
            for m in range(kb, 8)
        ]
        splat = [
            [jnp.broadcast_to(cols[0][q][r : r + 1, :], full) if q >= r else None for q in range(8)]
            for r in range(8)
        ]
        out = jnp.zeros(full, F32)
        for r in range(0, 8, 2):
            p, q, w = splat[r][r], splat[r][r + 1], splat[r + 1][r + 1]
            inverse = lax.rsqrt(p * w - q * q)
            inverse = inverse * inverse
            pp, qq, ww = p * inverse, q * inverse, w * inverse
            for k in range(r + 2, 8):
                one = splat[r][k] * ww - splat[r + 1][k] * qq
                two = splat[r + 1][k] * pp - splat[r][k] * qq
                for m in range(k, 8):
                    splat[k][m] = splat[k][m] - (one * splat[r][m] + two * splat[r + 1][m])
                rows[k] = rows[k] - (one * rows[r] + two * rows[r + 1])
                for m in range(1, len(cols)):
                    cols[m][k] = cols[m][k] - (one * cols[m][r] + two * cols[m][r + 1])
            root = lax.rsqrt(p)
            ratio = q * (root * root)
            first = rows[r] * (root * scale)
            second = (rows[r + 1] - ratio * rows[r]) * (lax.rsqrt(w - ratio * q) * scale)
            out = jnp.where((row_at == r) & (lane >= base + r), first, out)
            out = jnp.where((row_at == r + 1) & (lane >= base + r + 1), second, out)
            above = ww * rows[r] - qq * rows[r + 1]
            below = pp * rows[r + 1] - qq * rows[r]
            for m in range(1, len(cols)):
                left[kb + m] = left[kb + m] - (cols[m][r] * above + cols[m][r + 1] * below)
        root_ref[base : base + 8, :] = out


def reduce_kernel(
    part_ref, sq_hbm, moments_hbm, phi_hbm, recv, far_recv, root_out,
    buf, root, moments, phi, coeff, send_a, recv_a, send_b, recv_b, send_c, recv_c, own_sem,
):
    a = lax.axis_index("tgt")
    b = lax.axis_index("src")
    barrier = pltpu.get_barrier_semaphore()

    def greet(k, carry):
        pl.semaphore_signal(barrier, 1, device_id=(a, lax.rem(b + k, NS)), device_id_type=MESH)
        return carry

    lax.fori_loop(1, NS, greet, 0)
    sq_copy = pltpu.make_async_copy(sq_hbm, buf.at[b], own_sem.at[0])
    own_copy = pltpu.make_async_copy(part_ref.at[b], recv.at[b], own_sem.at[1])
    sq_copy.start()
    moments_copy = pltpu.make_async_copy(moments_hbm, moments, own_sem.at[3])
    phi_copy = pltpu.make_async_copy(phi_hbm, phi, own_sem.at[4])
    moments_copy.start()
    phi_copy.start()
    own_copy.start()
    sq_copy.wait()
    pl.semaphore_wait(barrier, NS - 1)

    def square_copy(k):
        return pltpu.make_async_remote_copy(
            src_ref=buf.at[b],
            dst_ref=buf.at[b],
            send_sem=send_b.at[k],
            recv_sem=recv_b.at[b],
            device_id=(a, lax.rem(b + k, NS)),
            device_id_type=MESH,
        )

    def part_copy(k):
        at = lax.rem(b + k, NS)
        return pltpu.make_async_remote_copy(
            src_ref=part_ref.at[at],
            dst_ref=recv.at[b],
            send_sem=send_a.at[k],
            recv_sem=recv_a.at[b],
            device_id=(a, at),
            device_id_type=MESH,
        )

    def start(copy):
        for k in FAR_FIRST:
            copy(k).start()

    start(square_copy)
    start(part_copy)

    moments_copy.wait()
    phi_copy.wait()
    found = jnp.zeros((2 * SCEN, TL * NODES), F32)
    extra = jnp.zeros((SCEN, TL * NODES), F32)
    for s in range(0, SL, 4):
        rows = jnp.concatenate([moments[(s + k) * 8 : (s + k + 1) * 8, :] for k in range(4)], axis=1)
        high = rows.astype(BF16).astype(F32)
        twice = jnp.concatenate([high, rows - high], axis=0).astype(BF16)
        couple = [phi[k, s : s + 4].reshape(4 * NODES, TL * NODES) for k in range(2)]
        found = found + jnp.dot(twice, couple[0], preferred_element_type=F32)
        extra = extra + jnp.dot(high.astype(BF16), couple[1], preferred_element_type=F32)
    total = found[:SCEN] + found[SCEN:] + extra
    for t in range(TL):
        coeff[t, :, 0:NODES] = total[:, t * NODES : (t + 1) * NODES]
        coeff[t, :, NODES:128] = jnp.zeros((SCEN, NODES), F32)

    def far_copy(k):
        at = lax.rem(b + k, NS)
        return pltpu.make_async_remote_copy(
            src_ref=coeff.at[at],
            dst_ref=far_recv.at[b],
            send_sem=send_c.at[k],
            recv_sem=recv_c.at[b],
            device_id=(a, at),
            device_id_type=MESH,
        )

    start(far_copy)
    own_far = pltpu.make_async_copy(coeff.at[b], far_recv.at[b], own_sem.at[5])
    own_far.start()
    planes = basis_by_plane()

    def square_wait(k, carry):
        slot = lax.rem(b + k, NS)
        pltpu.make_async_remote_copy(
            src_ref=buf.at[b],
            dst_ref=buf.at[slot],
            send_sem=send_b.at[0],
            recv_sem=recv_b.at[slot],
            device_id=(a, b),
            device_id_type=MESH,
        ).wait_recv()
        square_copy(k).wait_send()
        return carry

    lax.fori_loop(1, NS, square_wait, 0)
    square = buf[0]
    for k in range(1, NS):
        square = square + buf[k]
    basis = jnp.concatenate(planes, axis=1)
    scaled = jnp.concatenate([planes[k] * square[k : k + 1, :] for k in range(8)], axis=1)
    gram = lax.dot_general(
        scaled, basis, NT_DIMS, precision=lax.Precision.HIGHEST, preferred_element_type=F32
    )
    cholesky(gram, root)
    root_copy = pltpu.make_async_copy(root, root_out, own_sem.at[2])
    root_copy.start()

    def part_wait(k, carry):
        slot = lax.rem(b + k, NS)
        pltpu.make_async_remote_copy(
            src_ref=part_ref.at[0],
            dst_ref=recv.at[slot],
            send_sem=send_a.at[0],
            recv_sem=recv_a.at[slot],
            device_id=(a, b),
            device_id_type=MESH,
        ).wait_recv()
        part_copy(k).wait_send()
        pltpu.make_async_remote_copy(
            src_ref=coeff.at[0],
            dst_ref=far_recv.at[slot],
            send_sem=send_c.at[0],
            recv_sem=recv_c.at[slot],
            device_id=(a, b),
            device_id_type=MESH,
        ).wait_recv()
        far_copy(k).wait_send()
        return carry

    own_copy.wait()
    own_far.wait()
    lax.fori_loop(1, NS, part_wait, 0)
    root_copy.wait()


def reduce_part(part, square, moments, phi):
    hbm = pl.BlockSpec(memory_space=pltpu.HBM)
    return pl.pallas_call(
        reduce_kernel,
        out_shape=(
            jax.ShapeDtypeStruct((NS, 8, SCEN, 128), F32),
            jax.ShapeDtypeStruct((NS, SCEN, 128), F32),
            jax.ShapeDtypeStruct((NODES, NODES), F32),
        ),
        in_specs=[hbm] * 4,
        out_specs=(hbm,) * 3,
        scratch_shapes=[
            pltpu.VMEM((NS, 8, 128), F32),
            pltpu.VMEM((NODES, NODES), F32),
            pltpu.VMEM((SL * SCEN, NODES), F32),
            pltpu.VMEM((2, SL, NODES, TL * NODES), BF16),
            pltpu.VMEM((TL, SCEN, 128), F32),
        ]
        + [pltpu.SemaphoreType.DMA((NS,))] * 6
        + [pltpu.SemaphoreType.DMA((6,))],
        compiler_params=pltpu.CompilerParams(
            collective_id=1, has_side_effects=True, vmem_limit_bytes=VMEM
        ),
        name="reduce_part",
    )(part, square, moments, phi)


def finish_kernel(recv, far_recv, root, order_ref, w_ref, pot_ref, root_ref):
    b = lax.axis_index("src")
    coeff = far_recv[0]
    for k in range(1, NS):
        coeff = coeff + far_recv[k]
    high, low = split_two(coeff[:, 0:NODES])
    left = jnp.concatenate([high, low, high], axis=1)
    basis = [split_two(plane) for plane in basis_by_plane()]
    right = jnp.concatenate(
        [jnp.concatenate([basis[x][k] for x in range(8)], axis=1) for k in (0, 0, 1)], axis=0
    )
    far = jnp.dot(left, right, preferred_element_type=F32)
    blocks = []
    for x in range(8):
        total = recv[0, x]
        for k in range(1, NS):
            total = total + recv[k, x]
        blocks.append(total + far[:, x * 128 : (x + 1) * 128])
    weights = w_ref[pl.ds(pl.multiple_of(b * 8, 8), 8), :]
    for c in range(8):
        index = jnp.broadcast_to(order_ref[0:1, c * 128 : (c + 1) * 128], (8, 128))
        value = permute_row(blocks, index) * weights[c : c + 1, :]
        pot_ref[:, c * 128 : (c + 1) * 128] = value.astype(BF16)
    root_ref[...] = root[...]


def finish(recv, far_recv, root, order, weights):
    vmem = pl.BlockSpec(memory_space=pltpu.VMEM)
    return pl.pallas_call(
        finish_kernel,
        out_shape=(
            jax.ShapeDtypeStruct((SCEN, LEAF), BF16),
            jax.ShapeDtypeStruct((NODES, NODES), F32),
        ),
        in_specs=[vmem] * 5,
        out_specs=(vmem, vmem),
        compiler_params=pltpu.CompilerParams(vmem_limit_bytes=VMEM),
        name="finish",
    )(recv, far_recv, root, order, weights)


def shards(charges, weights, cell_order, leaf_coords, near_src):
    weights = weights.reshape(TL * 8, 128)
    block, table, phi, lists = exchange(leaf_coords, cell_order, weights)
    part, moments, square = local_part(charges, block, table, lists)
    recv, far_recv, root = reduce_part(part, square, moments, phi)
    return tuple(finish(recv, far_recv, root, cell_order, weights))


def solution(mesh):
    placed = (P(None, "src"), P("tgt"), P(("tgt", "src"), None), P(), P("tgt", None))
    return jax.shard_map(
        shards,
        mesh=mesh,
        in_specs=placed,
        out_specs=(P(None, ("tgt", "src")), P()),
        check_vma=False,
    )
```

```python
import math

import jax
import jax.numpy as jnp
import numpy as np
from jax import lax
from jax.experimental import pallas as pl
from jax.experimental.pallas import tpu as pltpu
from jax.sharding import PartitionSpec as P

EDGE = 8
LEAF = 1024
SCEN = 8
LV = 128
NT = 16
NS = 8
TL = LV // NT
SL = LV // NS
NODES = 64
CELLS = LV * LEAF
VMEM = 60 << 20
MESH = pl.DeviceIdType.MESH
F32 = jnp.float32
BF16 = jnp.bfloat16
NT_DIMS = (((1,), (1,)), ((), ()))


def chebyshev_nodes(extent):
    return [
        extent * 0.5 + extent * 0.5 * math.cos((2.0 * a + 1.0) * (math.pi / 8.0)) for a in range(4)
    ]


def lagrange(points, nodes, a):
    factor = 1.0
    for b in range(4):
        if b != a:
            factor = factor * ((points - nodes[b]) * (1.0 / (nodes[a] - nodes[b])))
    return factor


def select_by(index, values):
    out = values[0]
    for k in range(1, len(values)):
        out = jnp.where(index == k, values[k], out)
    return out


def basis_by_plane():
    row = lax.broadcasted_iota(jnp.int32, (16, 128), 0)
    lane = lax.broadcasted_iota(jnp.int32, (16, 128), 1)
    short, tall = chebyshev_nodes(8.0), chebyshev_nodes(16.0)
    y = lax.shift_right_logical(lane, 4).astype(F32) + 0.5
    z = jnp.bitwise_and(lane, 15).astype(F32) + 0.5
    along_y = select_by(lax.shift_right_logical(row, 2), [lagrange(y, short, k) for k in range(4)])
    along_z = select_by(jnp.bitwise_and(row, 3), [lagrange(z, tall, k) for k in range(4)])
    plane = along_y * along_z
    return [
        jnp.concatenate([plane * float(lagrange(x + 0.5, short, a)) for a in range(4)], axis=0)
        for x in range(8)
    ]


def node_offset(index):
    short, tall = chebyshev_nodes(8.0), chebyshev_nodes(16.0)
    return [
        select_by(lax.shift_right_logical(index, 4), short),
        select_by(jnp.bitwise_and(lax.shift_right_logical(index, 2), 3), short),
        select_by(jnp.bitwise_and(index, 3), tall),
    ]


def split_two(value):
    high = value.astype(BF16)
    return high, (value - high.astype(F32)).astype(BF16)


def near_tables(table, table_out, sems):
    row = lax.broadcasted_iota(jnp.int32, (128, 128), 0)
    lane = lax.broadcasted_iota(jnp.int32, (128, 128), 1)
    step_y = lax.shift_right_logical(lane, 4) - lax.shift_right_logical(row, 4)
    step_z = jnp.bitwise_and(lane, 15) - jnp.bitwise_and(row, 15)

    def one(o, carry):
        dy = step_y - 8 * (lax.div(o, 3) - 1)
        dz = step_z - 16 * (lax.rem(o, 3) - 1)
        base = (dy * dy + dz * dz).astype(F32)
        for delta in range(16):
            value = 0.05 * lax.rsqrt(base + float(delta * delta + 1))
            table[o, :, delta * 128 : (delta + 1) * 128] = value.astype(BF16)
        pltpu.make_async_copy(table.at[o], table_out.at[o], sems.at[o]).start()
        return carry

    lax.fori_loop(0, 9, one, 0)


def far_tables(coords, i, j, phi, phi_out, sem):
    lane = lax.broadcasted_iota(jnp.int32, (1, TL * NODES), 1)
    slot = lax.shift_right_logical(lane, 6)
    spacing = (8.0, 8.0, 16.0)
    box_at = [select_by(slot, [coords[d, i * TL + t] for t in range(TL)]) for d in range(3)]
    offset = node_offset(jnp.bitwise_and(lane, 63))
    node_at = [box_at[d].astype(F32) * spacing[d] + offset[d] for d in range(3)]
    source = node_offset(lax.broadcasted_iota(jnp.int32, (NODES, TL * NODES), 0))

    def one(s, carry):
        distance = 1.0
        close = None
        for d in range(3):
            box = coords[d, j * SL + s]
            inside = jnp.abs(box_at[d] - box) <= 1
            close = inside if close is None else close & inside
            between = (node_at[d] - box.astype(F32) * spacing[d]) - source[d]
            distance = distance + between * between
        high, low = split_two(jnp.where(close, 0.0, 0.05) * lax.rsqrt(distance))
        phi[0, s] = high
        phi[1, s] = low
        return carry

    lax.fori_loop(0, SL, one, 0)
    pltpu.make_async_copy(phi, phi_out, sem).start()


def pair_lists(coords, i, j):
    lane = lax.broadcasted_iota(jnp.int32, (1, 128), 1)
    t, s = lax.shift_right_logical(lane, 4), jnp.bitwise_and(lane, 15)
    step = [
        select_by(s, [coords[d, j * SL + k] for k in range(SL)])
        - select_by(t, [coords[d, i * TL + k] for k in range(TL)])
        for d in range(3)
    ]
    close = (jnp.abs(step[0]) <= 1) & (jnp.abs(step[1]) <= 1) & (jnp.abs(step[2]) <= 1)
    row = lax.broadcasted_iota(jnp.int32, (8, 128), 0)
    member = jnp.where(jnp.broadcast_to(jnp.where(close, jnp.where(step[0] == 0, 1, 0), 9), (8, 128)) == row, 1.0, 0.0)
    ahead = lax.broadcasted_iota(jnp.int32, (128, 128), 0) < lax.broadcasted_iota(jnp.int32, (128, 128), 1)
    rank = jnp.dot(
        member.astype(BF16), jnp.where(ahead, 1.0, 0.0).astype(BF16), preferred_element_type=F32
    )
    place = jnp.full((1, 128), 511.0, F32)
    for v in range(2):
        place = jnp.where(member[v : v + 1, :] > 0.5, rank[v : v + 1, :] + float(136 * v), place)
    position = lax.broadcasted_iota(jnp.int32, (512, 128), 0)
    spread = jnp.where(jnp.broadcast_to(place.astype(jnp.int32), (512, 128)) == position, 1.0, 0.0)
    parts = [t + 8 * s, (step[1] + 1) * 3 + step[2] + 1, jnp.full((1, 128), 1, jnp.int32), jnp.where(step[0] < 0, 1, 0)]
    left = select_by(row, [jnp.broadcast_to(part, (8, 128)) for part in parts]).astype(F32)
    listed = lax.dot_general(
        left.astype(BF16), spread.astype(BF16), NT_DIMS, preferred_element_type=F32
    ).astype(jnp.int32)
    out = jnp.where(listed[2:3, :] > 0, listed[0:1, :] + 256 * listed[1:2, :] + 4096 * listed[3:4, :], 8 * SL)
    at = lax.broadcasted_iota(jnp.int32, (1, 512), 1)
    for v in range(2):
        length = jnp.sum(member[v : v + 1, :], axis=1, keepdims=True).astype(jnp.int32)
        out = jnp.where(at == 408 + v, length, out)
    return out


def exchange_kernel(
    coords_hbm, order_hbm, w_hbm, block_ref, table_out, phi_out, list_out,
    coords, order_ref, w_ref, mine, table, phi, lists,
    send_a, recv_a, table_sem, phi_sem, in_sem, own_sem, list_sem,
):
    a = lax.axis_index("tgt")
    b = lax.axis_index("src")
    barrier = pltpu.get_barrier_semaphore()
    home = lax.rem(a, 2) * NS + b
    column = lax.div(a, 2)
    loops_back = b == column

    def signal_sender(k, carry):
        at = lax.rem(home + k, NT)
        pl.semaphore_signal(
            barrier, 1, device_id=(2 * b + lax.div(at, NS), lax.rem(at, NS)), device_id_type=MESH
        )
        return carry

    @pl.when(jnp.logical_not(loops_back))
    def _():
        signal_sender(0, 0)

    lax.fori_loop(1, NT, signal_sender, 0)
    fetches = [
        pltpu.make_async_copy(order_hbm, order_ref, in_sem.at[0]),
        pltpu.make_async_copy(w_hbm.at[pl.ds(pl.multiple_of(b * 8, 8), 8)], w_ref, in_sem.at[1]),
        pltpu.make_async_copy(coords_hbm, coords, in_sem.at[2]),
    ]
    for fetch in fetches:
        fetch.start()
    for fetch in fetches:
        fetch.wait()

    rows = lax.broadcasted_iota(jnp.int32, (8, 128), 0)
    lanes = lax.broadcasted_iota(jnp.int32, (8, 128), 1)
    low_rows = lax.broadcasted_iota(jnp.int32, (128, 128), 0)
    square = w_ref[...] * w_ref[...]
    placed = jnp.zeros((40, 128), F32)
    for c in range(8):
        order = order_ref[0:1, c * 128 : (c + 1) * 128]
        hit = lax.shift_right_logical(jnp.broadcast_to(order, (8, 128)), 7) == rows
        value = jnp.broadcast_to(square[c : c + 1, :], (8, 128))
        first = value.astype(BF16).astype(F32)
        rest = value - first
        second = rest.astype(BF16).astype(F32)
        third = rest - second
        parts = [jnp.full((8, 128), float(c), F32), lanes.astype(F32), first, second, third]
        left = jnp.concatenate([jnp.where(hit, part, 0.0) for part in parts], axis=0)
        low = jnp.broadcast_to(jnp.bitwise_and(order, 127), (128, 128)) == low_rows
        right = jnp.where(low, 1.0, 0.0).astype(BF16)
        placed = placed + lax.dot_general(
            left.astype(BF16), right, NT_DIMS, preferred_element_type=F32
        )
    mine[0:8, :] = placed[0:8] * 128.0 + placed[8:16]
    mine[8:16, :] = placed[16:24] + placed[24:32] + placed[32:40]

    pl.semaphore_wait(barrier, jnp.where(loops_back, NT - 1, NT).astype(jnp.int32))

    def block_copy(k):
        return pltpu.make_async_remote_copy(
            src_ref=mine,
            dst_ref=block_ref.at[home],
            send_sem=send_a.at[k],
            recv_sem=recv_a.at[home],
            device_id=(lax.rem(a + k, NT), column),
            device_id_type=MESH,
        )

    def start_block(k, carry):
        block_copy(k).start()
        return carry

    lax.fori_loop(1, NT, start_block, 0)

    @pl.when(jnp.logical_not(loops_back))
    def _():
        block_copy(0).start()

    own_copy = pltpu.make_async_copy(mine, block_ref.at[home], own_sem)

    @pl.when(loops_back)
    def _():
        own_copy.start()

    lists[...] = pair_lists(coords, a, b)
    list_copy = pltpu.make_async_copy(lists, list_out, list_sem)
    list_copy.start()
    far_tables(coords, a, b, phi, phi_out, phi_sem)
    near_tables(table, table_out, table_sem)
    list_copy.wait()
    pltpu.make_async_copy(phi, phi_out, phi_sem).wait()
    for o in range(9):
        pltpu.make_async_copy(table.at[o], table_out.at[o], table_sem.at[o]).wait()

    def block_arrival(slot):
        pltpu.make_async_remote_copy(
            src_ref=mine,
            dst_ref=block_ref.at[slot],
            send_sem=send_a.at[0],
            recv_sem=recv_a.at[slot],
            device_id=(a, b),
            device_id_type=MESH,
        ).wait_recv()

    @pl.when(jnp.logical_not(loops_back))
    def _():
        block_arrival(home)
        block_copy(0).wait_send()

    @pl.when(loops_back)
    def _():
        own_copy.wait()

    def wait_block(k, carry):
        block_arrival(lax.rem(home + k, NT))
        block_copy(k).wait_send()
        return carry

    lax.fori_loop(1, NT, wait_block, 0)


def exchange(coords, order, weights):
    hbm = pl.BlockSpec(memory_space=pltpu.HBM)
    return pl.pallas_call(
        exchange_kernel,
        out_shape=(
            jax.ShapeDtypeStruct((SL, 16, 128), F32),
            jax.ShapeDtypeStruct((9, 128, 2048), BF16),
            jax.ShapeDtypeStruct((2, SL, NODES, TL * NODES), BF16),
            jax.ShapeDtypeStruct((1, 512), jnp.int32),
        ),
        in_specs=[hbm] * 3,
        out_specs=(hbm,) * 4,
        scratch_shapes=[
            pltpu.SMEM((3, LV), jnp.int32),
            pltpu.VMEM((1, LEAF), jnp.int32),
            pltpu.VMEM((8, 128), F32),
            pltpu.VMEM((16, 128), F32),
            pltpu.VMEM((9, 128, 2048), BF16),
            pltpu.VMEM((2, SL, NODES, TL * NODES), BF16),
            pltpu.VMEM((1, 512), jnp.int32),
            pltpu.SemaphoreType.DMA((NT,)),
            pltpu.SemaphoreType.DMA((NT,)),
            pltpu.SemaphoreType.DMA((9,)),
            pltpu.SemaphoreType.DMA,
            pltpu.SemaphoreType.DMA((3,)),
            pltpu.SemaphoreType.DMA,
            pltpu.SemaphoreType.DMA,
        ],
        compiler_params=pltpu.CompilerParams(
            collective_id=0, has_side_effects=True, vmem_limit_bytes=VMEM
        ),
        name="exchange",
    )(coords, order, weights)


def lane_gather(block, lane):
    return jnp.take_along_axis(block, lane, axis=1, mode="promise_in_bounds")


def permute_row(blocks, index):
    block = lax.shift_right_logical(index, 7)
    lane = jnp.bitwise_and(index, 127)
    out = lane_gather(blocks[0], lane)
    for k in range(1, 8):
        out = jnp.where(block == k, lane_gather(blocks[k], lane), out)
    return out


def local_kernel(
    charges_hbm, block_hbm, table_hbm, list_hbm, out, moments_out, sq_out,
    charges, block, table, qf, qb, pairs, sems,
):
    fetches = [
        pltpu.make_async_copy(source, target, sems.at[k])
        for k, (source, target) in enumerate(
            [(charges_hbm, charges), (block_hbm, block), (table_hbm, table), (list_hbm, pairs)]
        )
    ]
    for fetch in fetches:
        fetch.start()
    qb[SL] = jnp.zeros((64, 128), BF16)
    out[...] = jnp.zeros((TL, 8, SCEN, 128), F32)

    fetches[0].wait()
    fetches[1].wait()

    low_rows = lax.broadcasted_iota(jnp.int16, (128, 128), 0)
    one = jnp.ones((128, 128), BF16)
    zero = jnp.zeros((128, 128), BF16)

    def by_gather(raw, order):
        blocks = [raw[:, k * 128 : (k + 1) * 128] for k in range(8)]
        return [
            permute_row(blocks, jnp.broadcast_to(order[x : x + 1, :], (8, 128))) for x in range(8)
        ]

    def by_product(raw, order):
        left = jnp.concatenate([raw[:, k * 128 : (k + 1) * 128] for k in range(8)], axis=0).astype(BF16)
        block_at = lax.shift_right_logical(order, 7)
        low = jnp.bitwise_and(order, 127)
        pieces = []
        for x in range(0, 8, 2):
            hots = [
                jnp.where(
                    jnp.broadcast_to(low[y : y + 1, :], (128, 128)).astype(jnp.int16) == low_rows,
                    one,
                    zero,
                )
                for y in (x, x + 1)
            ]
            spread = jnp.dot(left, jnp.concatenate(hots, axis=1), preferred_element_type=F32)
            for half in range(2):
                wanted = jnp.broadcast_to(block_at[x + half : x + half + 1, :], (8, 128))
                lanes = slice(half * 128, (half + 1) * 128)
                pieces.append(select_by(wanted, [spread[k * 8 : (k + 1) * 8, lanes] for k in range(8)]))
        return pieces

    def canonical(group, carry):
        for k in range(4):
            leaf = group * 4 + k
            base = pl.multiple_of(leaf * LEAF, LEAF)
            raw = charges[:, pl.ds(base, LEAF)].astype(F32)
            order = block[leaf, 0:8, :].astype(jnp.int32)
            pieces = by_product(raw, order) if k < 2 else by_gather(raw, order)
            rows = jnp.concatenate(pieces, axis=0)
            qf[leaf] = rows
            qb[leaf] = rows.astype(BF16)
            qb[SL + 1 + leaf] = jnp.concatenate(pieces[::-1], axis=0).astype(BF16)
        return carry

    lax.fori_loop(0, SL // 4, canonical, 0)
    square = block[0, 8:16, :]
    for leaf in range(1, SL):
        square = square + block[leaf, 8:16, :]
    sq_out[...] = square

    moments = jnp.zeros((SL * SCEN, NODES), F32)
    for x, plane in enumerate(basis_by_plane()):
        rows = qf[:, x * 8 : (x + 1) * 8, :].reshape(SL * SCEN, 128).astype(BF16)
        for part in split_two(plane):
            moments = moments + lax.dot_general(rows, part, NT_DIMS, preferred_element_type=F32)
    moments_out[...] = moments
    fetches[2].wait()
    fetches[3].wait()

    def near_pairs(value):
        def contribution(code):
            s = jnp.bitwise_and(lax.shift_right_logical(code, 3), 31)
            which = jnp.bitwise_and(lax.shift_right_logical(code, 8), 15)
            mirrored = lax.shift_right_logical(code, 12)
            left = qb[s + (SL + 1) * mirrored]
            total = [None] * 8
            for chunk in range(4 if value == 1 else 8):
                first, last = (0, 8) if value == 1 else (max(0, 2 * chunk - 8), min(8, 2 * chunk + 2))
                product = jnp.dot(
                    left[first * 8 : last * 8],
                    table[which, :, chunk * 256 : (chunk + 1) * 256],
                    preferred_element_type=F32,
                )
                for half in range(2):
                    delta = 2 * chunk + half
                    for sx in range(first, last):
                        piece = product[(sx - first) * 8 : (sx - first + 1) * 8, half * 128 : (half + 1) * 128]
                        for x in sorted({sx - delta, sx + delta} if value == 1 else {8 + sx - delta}):
                            if 0 <= x < 8:
                                total[x] = piece if total[x] is None else total[x] + piece
            return total

        def step(first, size):
            codes = [pairs[0, first + k] for k in range(size)]
            totals = [contribution(code) for code in codes]
            for code, total in zip(codes, totals):
                t = jnp.bitwise_and(code, 7)
                mirrored = lax.shift_right_logical(code, 12)
                for x in range(8):
                    out[t, x if value == 1 else x + mirrored * (7 - 2 * x)] += total[x]

        def eight(n, carry):
            step(136 * value + 8 * n, 8)
            return carry

        length = pairs[0, 408 + value]
        full = lax.shift_right_logical(length + 3, 3)
        lax.fori_loop(0, full, eight, 0)

        @pl.when(length > 8 * full)
        def _():
            step(136 * value + 8 * full, 4)

    for value in range(2):
        near_pairs(value)


def local_part(charges, block, table, lists):
    hbm = pl.BlockSpec(memory_space=pltpu.HBM)
    vmem = pl.BlockSpec(memory_space=pltpu.VMEM)
    return pl.pallas_call(
        local_kernel,
        out_shape=(
            jax.ShapeDtypeStruct((TL, 8, SCEN, 128), F32),
            jax.ShapeDtypeStruct((SL * SCEN, NODES), F32),
            jax.ShapeDtypeStruct((8, 128), F32),
        ),
        in_specs=[hbm] * 4,
        out_specs=(vmem,) * 3,
        scratch_shapes=[
            pltpu.VMEM((SCEN, SL * LEAF), BF16),
            pltpu.VMEM((SL, 16, 128), F32),
            pltpu.VMEM((9, 128, 2048), BF16),
            pltpu.VMEM((SL, 64, 128), F32),
            pltpu.VMEM((2 * SL + 1, 64, 128), BF16),
            pltpu.SMEM((1, 512), jnp.int32),
            pltpu.SemaphoreType.DMA((4,)),
        ],
        compiler_params=pltpu.CompilerParams(vmem_limit_bytes=VMEM),
        name="local_part",
    )(charges, block, table, lists)


def cholesky(gram, root_ref):
    full = (8, NODES)
    lane = lax.broadcasted_iota(jnp.int32, full, 1)
    row_at = lax.broadcasted_iota(jnp.int32, full, 0)
    left = [gram[8 * k : 8 * k + 8, :] for k in range(8)]
    scale = 1.0 / math.sqrt(CELLS)
    for kb in range(8):
        base = 8 * kb
        rows = [jnp.broadcast_to(left[kb][r : r + 1, :], full) for r in range(8)]
        cols = [
            [jnp.broadcast_to(left[m][:, base + q : base + q + 1], full) for q in range(8)]
            for m in range(kb, 8)
        ]
        splat = [
            [jnp.broadcast_to(cols[0][q][r : r + 1, :], full) if q >= r else None for q in range(8)]
            for r in range(8)
        ]
        out = jnp.zeros(full, F32)
        for r in range(0, 8, 2):
            p, q, w = splat[r][r], splat[r][r + 1], splat[r + 1][r + 1]
            inverse = lax.rsqrt(p * w - q * q)
            inverse = inverse * inverse
            pp, qq, ww = p * inverse, q * inverse, w * inverse
            for k in range(r + 2, 8):
                one = splat[r][k] * ww - splat[r + 1][k] * qq
                two = splat[r + 1][k] * pp - splat[r][k] * qq
                for m in range(k, 8):
                    splat[k][m] = splat[k][m] - (one * splat[r][m] + two * splat[r + 1][m])
                rows[k] = rows[k] - (one * rows[r] + two * rows[r + 1])
                for m in range(1, len(cols)):
                    cols[m][k] = cols[m][k] - (one * cols[m][r] + two * cols[m][r + 1])
            root = lax.rsqrt(p)
            ratio = q * (root * root)
            first = rows[r] * (root * scale)
            second = (rows[r + 1] - ratio * rows[r]) * (lax.rsqrt(w - ratio * q) * scale)
            out = jnp.where((row_at == r) & (lane >= base + r), first, out)
            out = jnp.where((row_at == r + 1) & (lane >= base + r + 1), second, out)
            above = ww * rows[r] - qq * rows[r + 1]
            below = pp * rows[r + 1] - qq * rows[r]
            for m in range(1, len(cols)):
                left[kb + m] = left[kb + m] - (cols[m][r] * above + cols[m][r + 1] * below)
        root_ref[base : base + 8, :] = out


def reduce_kernel(
    part_ref, sq_hbm, moments_hbm, phi_hbm, recv, far_recv, root_out,
    buf, root, moments, phi, coeff, send_a, recv_a, send_b, recv_b, send_c, recv_c, own_sem,
):
    a = lax.axis_index("tgt")
    b = lax.axis_index("src")
    barrier = pltpu.get_barrier_semaphore()

    def greet(k, carry):
        pl.semaphore_signal(barrier, 1, device_id=(a, lax.rem(b + k, NS)), device_id_type=MESH)
        return carry

    lax.fori_loop(1, NS, greet, 0)
    sq_copy = pltpu.make_async_copy(sq_hbm, buf.at[b], own_sem.at[0])
    own_copy = pltpu.make_async_copy(part_ref.at[b], recv.at[b], own_sem.at[1])
    sq_copy.start()
    moments_copy = pltpu.make_async_copy(moments_hbm, moments, own_sem.at[3])
    phi_copy = pltpu.make_async_copy(phi_hbm, phi, own_sem.at[4])
    moments_copy.start()
    phi_copy.start()
    own_copy.start()
    sq_copy.wait()
    pl.semaphore_wait(barrier, NS - 1)

    def square_copy(k):
        return pltpu.make_async_remote_copy(
            src_ref=buf.at[b],
            dst_ref=buf.at[b],
            send_sem=send_b.at[k],
            recv_sem=recv_b.at[b],
            device_id=(a, lax.rem(b + k, NS)),
            device_id_type=MESH,
        )

    def part_copy(k):
        at = lax.rem(b + k, NS)
        return pltpu.make_async_remote_copy(
            src_ref=part_ref.at[at],
            dst_ref=recv.at[b],
            send_sem=send_a.at[k],
            recv_sem=recv_a.at[b],
            device_id=(a, at),
            device_id_type=MESH,
        )

    def start(copy):
        def step(n, carry):
            half = lax.div(n + 1, 2)
            copy(4 + half * (1 - 2 * lax.rem(n, 2))).start()
            return carry

        lax.fori_loop(0, NS - 1, step, 0)

    start(square_copy)
    start(part_copy)

    moments_copy.wait()
    phi_copy.wait()
    found = jnp.zeros((2 * SCEN, TL * NODES), F32)
    extra = jnp.zeros((SCEN, TL * NODES), F32)
    for s in range(0, SL, 4):
        rows = jnp.concatenate([moments[(s + k) * 8 : (s + k + 1) * 8, :] for k in range(4)], axis=1)
        high = rows.astype(BF16).astype(F32)
        twice = jnp.concatenate([high, rows - high], axis=0).astype(BF16)
        couple = [phi[k, s : s + 4].reshape(4 * NODES, TL * NODES) for k in range(2)]
        found = found + jnp.dot(twice, couple[0], preferred_element_type=F32)
        extra = extra + jnp.dot(high.astype(BF16), couple[1], preferred_element_type=F32)
    total = found[:SCEN] + found[SCEN:] + extra
    for t in range(TL):
        coeff[t, :, 0:NODES] = total[:, t * NODES : (t + 1) * NODES]
        coeff[t, :, NODES:128] = jnp.zeros((SCEN, NODES), F32)

    def far_copy(k):
        at = lax.rem(b + k, NS)
        return pltpu.make_async_remote_copy(
            src_ref=coeff.at[at],
            dst_ref=far_recv.at[b],
            send_sem=send_c.at[k],
            recv_sem=recv_c.at[b],
            device_id=(a, at),
            device_id_type=MESH,
        )

    start(far_copy)
    own_far = pltpu.make_async_copy(coeff.at[b], far_recv.at[b], own_sem.at[5])
    own_far.start()
    planes = basis_by_plane()

    def square_wait(k, carry):
        slot = lax.rem(b + k, NS)
        pltpu.make_async_remote_copy(
            src_ref=buf.at[b],
            dst_ref=buf.at[slot],
            send_sem=send_b.at[0],
            recv_sem=recv_b.at[slot],
            device_id=(a, b),
            device_id_type=MESH,
        ).wait_recv()
        square_copy(k).wait_send()
        return carry

    lax.fori_loop(1, NS, square_wait, 0)
    square = buf[0]
    for k in range(1, NS):
        square = square + buf[k]
    basis = jnp.concatenate(planes, axis=1)
    scaled = jnp.concatenate([planes[k] * square[k : k + 1, :] for k in range(8)], axis=1)
    gram = lax.dot_general(
        scaled, basis, NT_DIMS, precision=lax.Precision.HIGHEST, preferred_element_type=F32
    )
    cholesky(gram, root)
    root_copy = pltpu.make_async_copy(root, root_out, own_sem.at[2])
    root_copy.start()

    def part_wait(k, carry):
        slot = lax.rem(b + k, NS)
        pltpu.make_async_remote_copy(
            src_ref=part_ref.at[0],
            dst_ref=recv.at[slot],
            send_sem=send_a.at[0],
            recv_sem=recv_a.at[slot],
            device_id=(a, b),
            device_id_type=MESH,
        ).wait_recv()
        part_copy(k).wait_send()
        pltpu.make_async_remote_copy(
            src_ref=coeff.at[0],
            dst_ref=far_recv.at[slot],
            send_sem=send_c.at[0],
            recv_sem=recv_c.at[slot],
            device_id=(a, b),
            device_id_type=MESH,
        ).wait_recv()
        far_copy(k).wait_send()
        return carry

    own_copy.wait()
    own_far.wait()
    lax.fori_loop(1, NS, part_wait, 0)
    root_copy.wait()


def reduce_part(part, square, moments, phi):
    hbm = pl.BlockSpec(memory_space=pltpu.HBM)
    return pl.pallas_call(
        reduce_kernel,
        out_shape=(
            jax.ShapeDtypeStruct((NS, 8, SCEN, 128), F32),
            jax.ShapeDtypeStruct((NS, SCEN, 128), F32),
            jax.ShapeDtypeStruct((NODES, NODES), F32),
        ),
        in_specs=[hbm] * 4,
        out_specs=(hbm,) * 3,
        scratch_shapes=[
            pltpu.VMEM((NS, 8, 128), F32),
            pltpu.VMEM((NODES, NODES), F32),
            pltpu.VMEM((SL * SCEN, NODES), F32),
            pltpu.VMEM((2, SL, NODES, TL * NODES), BF16),
            pltpu.VMEM((TL, SCEN, 128), F32),
        ]
        + [pltpu.SemaphoreType.DMA((NS,))] * 6
        + [pltpu.SemaphoreType.DMA((6,))],
        compiler_params=pltpu.CompilerParams(
            collective_id=1, has_side_effects=True, vmem_limit_bytes=VMEM
        ),
        name="reduce_part",
    )(part, square, moments, phi)


def finish_kernel(recv, far_recv, root, order_ref, w_ref, pot_ref, root_ref):
    b = lax.axis_index("src")
    coeff = far_recv[0]
    for k in range(1, NS):
        coeff = coeff + far_recv[k]
    high, low = split_two(coeff[:, 0:NODES])
    left = jnp.concatenate([high, low, high], axis=1)
    basis = [split_two(plane) for plane in basis_by_plane()]
    right = jnp.concatenate(
        [jnp.concatenate([basis[x][k] for x in range(8)], axis=1) for k in (0, 0, 1)], axis=0
    )
    far = jnp.dot(left, right, preferred_element_type=F32)
    blocks = []
    for x in range(8):
        total = recv[0, x]
        for k in range(1, NS):
            total = total + recv[k, x]
        blocks.append(total + far[:, x * 128 : (x + 1) * 128])
    weights = w_ref[pl.ds(pl.multiple_of(b * 8, 8), 8), :]
    for c in range(8):
        index = jnp.broadcast_to(order_ref[0:1, c * 128 : (c + 1) * 128], (8, 128))
        value = permute_row(blocks, index) * weights[c : c + 1, :]
        pot_ref[:, c * 128 : (c + 1) * 128] = value.astype(BF16)
    root_ref[...] = root[...]


def finish(recv, far_recv, root, order, weights):
    vmem = pl.BlockSpec(memory_space=pltpu.VMEM)
    return pl.pallas_call(
        finish_kernel,
        out_shape=(
            jax.ShapeDtypeStruct((SCEN, LEAF), BF16),
            jax.ShapeDtypeStruct((NODES, NODES), F32),
        ),
        in_specs=[vmem] * 5,
        out_specs=(vmem, vmem),
        compiler_params=pltpu.CompilerParams(vmem_limit_bytes=VMEM),
        name="finish",
    )(recv, far_recv, root, order, weights)


def shards(charges, weights, cell_order, leaf_coords, near_src):
    weights = weights.reshape(TL * 8, 128)
    block, table, phi, lists = exchange(leaf_coords, cell_order, weights)
    part, moments, square = local_part(charges, block, table, lists)
    recv, far_recv, root = reduce_part(part, square, moments, phi)
    return tuple(finish(recv, far_recv, root, cell_order, weights))


def solution(mesh):
    placed = (P(None, "src"), P("tgt"), P(("tgt", "src"), None), P(), P("tgt", None))
    return jax.shard_map(
        shards,
        mesh=mesh,
        in_specs=placed,
        out_specs=(P(None, ("tgt", "src")), P()),
        check_vma=False,
    )
```
